128 devices in a mesh: ctx: 64 (over x, z, y_hi, core), kvh: 2 (over y_lo).
Axes of the slice: x: 4, y: 4 (y_hi: 2, y_lo: 2; y = y_hi * 2 + y_lo), z: 4, core: 2. Of those that a mesh axis runs over, the one named last changes fastest.
Arguments:
- queries: bfloat16 [32768, 3584], P('ctx', 'kvh'), may hold values from -7.5 to 7.5
- keys: bfloat16 [32768, 512], P('ctx', 'kvh'), may hold values from -6 to 6
- values: bfloat16 [32768, 512], P('ctx', 'kvh'), may hold values from -6 to 6
- columns: int32 [28, 16], P('kvh'), may hold values from 0 to 255, as said below
- offsets: int32 [28, 128], P('kvh'), may hold values from 0 to 511, as said below
- out_weight: bfloat16 [3584, 3584], P('kvh'), may hold values from -0.09375 to 0.09375
Outputs:
- mixed: bfloat16 [32768, 3584], P('ctx', 'kvh')
The draws below stay inside these ranges and needn't reach their ends.
Inputs may be any that keep to these rules, and one draw needn't show every extreme that they name: `columns`: each row lists 16 different blocks of 128 tokens. Rows h with equal h // 7 share a KV head; the union of their lists holds at most 2 blocks among the tokens of any one aligned run of 512 tokens, and exactly 2 among tokens 0 to 511. `offsets`: each row holds 128 different diagonal distances, 0 and 1 among them.
All inputs are finite; a program needn't handle non-finite values.
Results may differ from the reference program's by a relative error of at most 0.012.
Values may be sent and summed in bfloat16 or wider, within the bound.
No kernel may reach another device: no remote copies, remote signals or barrier semaphores. Data moves between devices by JAX's collectives and lax.ppermute only.
A program may use at most 320 MiB of HBM per device.

```python
import math
import jax
import jax.numpy as jnp
from jax import lax

D = 3584
QH = 28
KVH = 4
HD = 128
TOK_DEV = 512
BLK = 128
NV = 16
NS = 128
CAP = 2
TOKENS = 32768
WIN = 512


def draw_columns(key, part):
    device_count = TOKENS // TOK_DEV
    per_device = TOK_DEV // BLK
    group_size = QH // KVH
    pool_size = device_count * CAP

    def one_group(group_key):
        cand_key, head_key, sink_key = jax.random.split(group_key, 3)
        picks = jax.vmap(lambda split_key: jax.random.permutation(split_key, per_device)[:CAP])(jax.random.split(cand_key, device_count))
        candidates = (jnp.arange(device_count, dtype=jnp.int32)[:, None] * per_device + picks.astype(jnp.int32)).reshape(-1)
        sink_head = jax.random.randint(sink_key, (), 0, group_size)

        def one_head(split_key, index):
            drawn_key, rest_key, order_key = jax.random.split(split_key, 3)
            drawn = jax.random.permutation(drawn_key, pool_size)[:NV].astype(jnp.int32)
            forced = jnp.concatenate([jnp.arange(CAP, dtype=jnp.int32), jax.random.permutation(rest_key, pool_size - CAP)[:NV - CAP].astype(jnp.int32) + CAP])
            chosen = jnp.where(index == sink_head, forced, drawn)
            chosen = chosen[jax.random.permutation(order_key, NV)]
            return candidates[chosen]
        return jax.vmap(one_head)(jax.random.split(head_key, group_size), jnp.arange(group_size, dtype=jnp.int32))
    lists = jax.vmap(one_group)(jax.random.split(jax.random.fold_in(key, 11), KVH))
    return lists.reshape(QH, NV).astype(jnp.int32)


def draw_offsets(key, part):

    def one_row(split_key):
        first_key, order_key = jax.random.split(split_key)
        others = jax.random.permutation(first_key, WIN - 2)[:NS - 2].astype(jnp.int32) + 2
        row_values = jnp.concatenate([jnp.array([0, 1], jnp.int32), others])
        return row_values[jax.random.permutation(order_key, NS)]
    return jax.vmap(one_row)(jax.random.split(jax.random.fold_in(key, 23), QH)).astype(jnp.int32)


def make_pair(key):
    base_key = jax.random.fold_in(key, 5)
    query_key, key_key = jax.random.split(base_key, 2)
    query_part = jnp.clip(jax.random.normal(query_key, (TOKENS, QH * HD), jnp.float32), -6.0, 6.0)
    key_part = jnp.clip(jax.random.normal(key_key, (TOKENS, KVH * HD), jnp.float32), -6.0, 6.0)
    return (query_part, key_part)


def draw_queries(key, part):
    return make_pair(key)[0].astype(jnp.bfloat16)


def draw_keys(key, part):
    return make_pair(key)[1].astype(jnp.bfloat16)


def levels(key, extent, shards, least, high):
    level, own = 1.0, jax.random.fold_in(key, 6)
    for position, parts in shards:
        draws = jnp.exp(jax.random.uniform(jax.random.fold_in(own, position), (parts,), jnp.float32, least / len(shards), high / len(shards)))
        level = level * jnp.repeat(draws, extent[position] // parts).reshape([-1 if axis == position else 1 for axis in range(len(extent))])
    return level


def normal_values(stream_key, dims, scale, reach, pieces=(), kind=jnp.bfloat16):
    entries = jax.random.normal(stream_key, dims, jnp.float32) * scale
    if len(pieces) > 0:
        entries = levels(stream_key, dims, pieces, -0.22, 0.18) * entries
    return jnp.clip(entries, min=-reach, max=reach).astype(kind)


def setup_inputs(seed: int = 0) -> dict:
    arg_keys = jax.random.split(jax.random.key(seed), 7)
    queries = draw_queries(jax.random.fold_in(arg_keys[6], 71), 0)
    keys = draw_keys(jax.random.fold_in(arg_keys[6], 71), 0)
    values = normal_values(arg_keys[2], (TOKENS, KVH * HD), 1.0, 6.0, ((0, 64), (1, 2)))
    columns = draw_columns(jax.random.fold_in(arg_keys[6], 71), 0)
    offsets = draw_offsets(jax.random.fold_in(arg_keys[6], 71), 0)
    out_weight = normal_values(arg_keys[5], (QH * HD, D), (QH * HD) ** -0.5, 0.09375, ((0, 2),))
    return {"queries": queries, "keys": keys, "values": values, "columns": columns, "offsets": offsets, "out_weight": out_weight}


masked_score = -1e+30

def reference(queries, keys, values, columns, offsets, out_weight):
    total_rows = queries.shape[0]
    block_count = total_rows // TOK_DEV
    group_size = QH // KVH
    score_scale = 1.0 / math.sqrt(HD)
    query_heads = queries.reshape(total_rows, QH, HD).transpose(1, 0, 2)
    key_heads = keys.reshape(total_rows, KVH, HD).transpose(1, 0, 2)
    value_heads = values.reshape(total_rows, KVH, HD).transpose(1, 0, 2)
    block_lane = jnp.arange(BLK, dtype=jnp.int32)
    query_lane = jnp.arange(TOK_DEV, dtype=jnp.int32)
    window_lane = jnp.arange(2 * TOK_DEV, dtype=jnp.int32)
    distances = jnp.arange(WIN, dtype=jnp.int32)
    padding = jnp.zeros((TOK_DEV, HD), keys.dtype)

    def one_head(head):
        kv_index = head // group_size
        key_rows = key_heads[kv_index]
        value_rows = value_heads[kv_index]
        column_pos = (columns[head][:, None] * BLK + block_lane[None, :]).reshape(-1).astype(jnp.int32)
        far_keys = jnp.take(key_rows, column_pos, axis=0)
        far_values = jnp.take(value_rows, column_pos, axis=0)
        listed = jnp.any(offsets[head][:, None] == distances[None, :], axis=0)
        padded_keys = jnp.concatenate([padding, key_rows], axis=0)
        padded_values = jnp.concatenate([padding, value_rows], axis=0)
        query_all = query_heads[head]

        def one_block(block):
            start = (block * TOK_DEV).astype(jnp.int32)
            query_rows = lax.dynamic_slice_in_dim(query_all, start, TOK_DEV, 0)
            near_keys = lax.dynamic_slice_in_dim(padded_keys, start, 2 * TOK_DEV, 0)
            near_values = lax.dynamic_slice_in_dim(padded_values, start, 2 * TOK_DEV, 0)
            query_pos = start + query_lane
            key_pos = start - TOK_DEV + window_lane
            far_scores = jnp.dot(query_rows, far_keys.T, preferred_element_type=jnp.float32) * score_scale
            near_scores = jnp.dot(query_rows, near_keys.T, preferred_element_type=jnp.float32) * score_scale
            far_ok = query_pos[:, None] - column_pos[None, :] >= WIN
            distance = query_pos[:, None] - key_pos[None, :]
            near_ok = (distance >= 0) & (distance < WIN) & (key_pos[None, :] >= 0)
            near_ok = near_ok & jnp.take(listed, jnp.clip(distance, 0, WIN - 1))
            far_scores = jnp.where(far_ok, far_scores, masked_score)
            near_scores = jnp.where(near_ok, near_scores, masked_score)
            row_top = jnp.maximum(lax.optimization_barrier(jnp.max(far_scores, axis=1)), lax.optimization_barrier(jnp.max(near_scores, axis=1)))
            far_exp = jnp.exp(far_scores - row_top[:, None])
            near_exp = jnp.exp(near_scores - row_top[:, None])
            row_total = lax.optimization_barrier(jnp.sum(far_exp, axis=1)) + lax.optimization_barrier(jnp.sum(near_exp, axis=1))
            far_weight = (far_exp / row_total[:, None]).astype(jnp.bfloat16)
            near_weight = (near_exp / row_total[:, None]).astype(jnp.bfloat16)
            result = jnp.dot(far_weight, far_values, preferred_element_type=jnp.float32)
            result = result + jnp.dot(near_weight, near_values, preferred_element_type=jnp.float32)
            return result.astype(jnp.bfloat16)
        return lax.map(one_block, jnp.arange(block_count, dtype=jnp.int32))
    head_outputs = lax.map(one_head, jnp.arange(QH, dtype=jnp.int32))
    attended = head_outputs.reshape(QH, total_rows, HD).transpose(1, 0, 2).reshape(total_rows, QH * HD)
    return jnp.dot(attended, out_weight, preferred_element_type=jnp.float32).astype(jnp.bfloat16)
```

```python
import functools
import math

import jax
import jax.numpy as jnp
from jax import lax
from jax.experimental import pallas as pl
from jax.experimental.pallas import tpu as pltpu
from jax.sharding import PartitionSpec as P

HD = 128
BLK = 128
NV = 16
CAP = 2
WIN = 512
TOK = 512
GRP = 7
GW = GRP * HD
CHUNKS = 4
WINB = WIN // BLK
BAND = WIN + BLK
NEG = -1e30
LOG2 = math.log2(math.e) / math.sqrt(HD)


def coords(i):
    return i // 16, i // 4 % 4, i // 2 % 2, i % 2


def index(x, z, y, c):
    return (x % 4) * 16 + (z % 4) * 4 + (y % 2) * 2 + c % 2


def send_x(by):
    def to(i):
        x, z, y, c = coords(i)
        return index(x + by, z, y, c)

    return to


def send_z(by):
    def to(i):
        x, z, y, c = coords(i)
        return index(x, z + by, y, c)

    return to


def send_y(i):
    x, z, y, c = coords(i)
    return index(x, z, y + 1, c)


def send_core(i):
    return i ^ 1


def permute(value, to, axis="ctx"):
    return lax.ppermute(value, axis, [(i, to(i)) for i in range(lax.axis_size(axis))])


def ring(piece, send):
    return [
        piece,
        permute(piece, send(1)),
        permute(piece, send(-1)),
        permute(piece, send(2)),
    ]


def dot_t(a, b):
    return lax.dot_general(a, b, (((1,), (1,)), ((), ())), preferred_element_type=jnp.float32)


def near_kernel(sc, q_own, q_oth, kv, pattern, o_ref, l_ref, vext, acc_s, m_s):
    h = pl.program_id(0)

    @pl.when(h == 0)
    def _():
        vext[:, :HD] = kv[:, HD:]
        vext[:, HD:] = jnp.ones((vext.shape[0], HD), jnp.bfloat16)

    bias = pltpu.roll(
        jnp.broadcast_to(pattern[0, 0:1, :], (BLK, BAND)), 0, 1, stride=1, stride_axis=0
    )
    rows = lax.broadcasted_iota(jnp.int32, (BLK, BLK), 0)
    lanes = lax.broadcasted_iota(jnp.int32, (BLK, BLK), 1)
    far_side = lanes <= rows
    band_lane = lax.broadcasted_iota(jnp.int32, (1, BAND), 1)
    core = sc[0]

    def tile_of(i):
        return (i // 4, i % 4, 4 * jnp.where(i // 4 == 0, core, 1 - core) + i % 4)

    def q_of(part, k):
        return (q_own if part == 0 else q_oth)[k * BLK : (k + 1) * BLK, :]

    for i in range(8):
        part, k, t = tile_of(i)
        base = pl.multiple_of(t * BLK, BLK)
        s = dot_t(q_of(part, k), kv[pl.ds(base, BAND), :HD])
        listed = jnp.where(sc[2 + h * 8 + t] > 0, 0.0, NEG).astype(jnp.float32)
        first = jnp.where(far_side, listed, bias[:, :BLK])
        absent = jnp.where(sc[1] > 0, BLK * (WINB - t), 0)
        edge = jnp.where(band_lane < absent, NEG, 0.0).astype(jnp.float32)
        s = s + jnp.concatenate([first, bias[:, BLK:]], axis=1) + edge
        m = jnp.max(s, axis=1, keepdims=True)
        p = jnp.exp2((s - m) * LOG2).astype(jnp.bfloat16)
        acc_s[i] = jnp.dot(p, vext[pl.ds(base, BAND), :], preferred_element_type=jnp.float32)
        m_s[i] = jnp.broadcast_to(m, (BLK, BLK))

    ex = 2 + 8 * GRP + 4 * h
    lowest = jnp.minimum(jnp.minimum(sc[ex], sc[ex + 1]), jnp.minimum(sc[ex + 2], sc[ex + 3]))

    @pl.when(lowest < 8)
    def _():
        for i in range(8):
            part, k, t = tile_of(i)
            for g in range(2):
                wa, wb = sc[ex + 2 * g], sc[ex + 2 * g + 1]

                @pl.when((wa < t) | (wb < t))
                def _():
                    ra = pl.multiple_of(jnp.minimum(wa, 11) * BLK, BLK)
                    rb = pl.multiple_of(jnp.minimum(wb, 11) * BLK, BLK)
                    ks = jnp.concatenate([kv[pl.ds(ra, BLK), :HD], kv[pl.ds(rb, BLK), :HD]], 0)
                    vs = jnp.concatenate([vext[pl.ds(ra, BLK), :], vext[pl.ds(rb, BLK), :]], 0)
                    s = dot_t(q_of(part, k), ks)
                    lane = lax.broadcasted_iota(jnp.int32, (1, 2 * BLK), 1)
                    ba = jnp.where(wa < t, 0.0, NEG).astype(jnp.float32)
                    bb = jnp.where(wb < t, 0.0, NEG).astype(jnp.float32)
                    s = s + jnp.where(lane < BLK, ba, bb)
                    m_old = m_s[i]
                    m_new = jnp.maximum(m_old, jnp.max(s, axis=1, keepdims=True))
                    scale = jnp.exp2((m_old - m_new) * LOG2)
                    p = jnp.exp2((s - jnp.concatenate([m_new, m_new], 1)) * LOG2)
                    acc_s[i] = acc_s[i] * jnp.concatenate([scale, scale], 1) + jnp.dot(
                        p.astype(jnp.bfloat16), vs, preferred_element_type=jnp.float32
                    )
                    m_s[i] = m_new

    for i in range(8):
        total = acc_s[i, :, HD:]
        o_ref[0, i * BLK : (i + 1) * BLK, :] = acc_s[i, :, :HD] / total
        l_ref[0, i * BLK : (i + 1) * BLK, :] = m_s[i] * LOG2 + jnp.log2(total)


def near_attention(scalars, queries, q_oth, window, pattern):
    rows = 8 * BLK
    state = jax.ShapeDtypeStruct((GRP, rows, HD), jnp.float32)
    return pl.pallas_call(
        near_kernel,
        grid_spec=pltpu.PrefetchScalarGridSpec(
            num_scalar_prefetch=1,
            grid=(GRP,),
            in_specs=[
                pl.BlockSpec((TOK, HD), lambda h, sc: (0, sc[0] * GRP + h)),
                pl.BlockSpec((TOK, HD), lambda h, sc: (0, h)),
                pl.BlockSpec((3 * TOK, 2 * HD), lambda h, sc: (0, 0)),
                pl.BlockSpec((1, 8, BAND), lambda h, sc: (h, 0, 0)),
            ],
            out_specs=[
                pl.BlockSpec((1, rows, HD), lambda h, sc: (h, 0, 0)),
                pl.BlockSpec((1, rows, HD), lambda h, sc: (h, 0, 0)),
            ],
            scratch_shapes=[
                pltpu.VMEM((3 * TOK, 2 * HD), jnp.bfloat16),
                pltpu.VMEM((8, BLK, 2 * HD), jnp.float32),
                pltpu.VMEM((8, BLK, BLK), jnp.float32),
            ],
        ),
        out_shape=[state, state],
        compiler_params=pltpu.CompilerParams(vmem_limit_bytes=40 << 20),
        name="near_attention",
    )(scalars, queries, q_oth, window, pattern)


PIECE = 16 * BLK
POOL = 8 * PIECE


def far_kernel(sc, q_own, q_oth, oa, la, ob, lb, *rest):
    pieces, (out_own, out_oth, pool, sem) = rest[:8], rest[8:]
    h = pl.program_id(0)

    @pl.when(h == 0)
    def _():
        copies = [
            pltpu.make_async_copy(
                pieces[k], pool.at[pl.ds(k * PIECE, PIECE), pl.ds(0, 2 * HD)], sem.at[k]
            )
            for k in range(8)
        ]
        for copy in copies:
            copy.start()
        pool[:POOL, 2 * HD :] = jnp.ones((POOL, HD), jnp.bfloat16)
        pool[POOL:, :] = jnp.zeros((BLK, 3 * HD), jnp.bfloat16)
        for copy in copies:
            copy.wait()

    n = sc[1 + h]

    @pl.when(n > 0)
    def _():
        q = jnp.concatenate([q_own[...], q_oth[...]], axis=0)

        def row(at, j):
            return pl.ds(pl.multiple_of(sc[at + h * NV + j] * BLK, BLK), BLK)

        ks = jnp.concatenate([pool[row(8, j), :HD] for j in range(NV)], axis=0)
        s = dot_t(q, ks)
        m = jnp.max(s, axis=1, keepdims=True)
        p = jnp.exp2((s - m) * LOG2).astype(jnp.bfloat16)
        vs = jnp.concatenate([pool[row(8 + GRP * NV, j), HD:] for j in range(NV)], axis=0)
        acc = jnp.dot(p, vs, preferred_element_type=jnp.float32)
        top = jnp.broadcast_to(m * LOG2, (2 * BLK, HD))
        for part, (o, l, out) in enumerate(((oa, la, out_own), (ob, lb, out_oth))):
            rows = slice(part * BLK, (part + 1) * BLK)
            both = jnp.maximum(l[0], top[rows])
            wn = jnp.exp2(l[0] - both)
            wf = jnp.exp2(top[rows] - both)
            out[...] = (
                (o[0] * wn + acc[rows, :HD] * wf) / (wn + acc[rows, HD:] * wf)
            ).astype(jnp.bfloat16)

    @pl.when(n == 0)
    def _():
        out_own[...] = oa[0].astype(jnp.bfloat16)
        out_oth[...] = ob[0].astype(jnp.bfloat16)


def far_attention(chunk, scalars, queries, q_oth, o, l, pieces):
    out = jax.ShapeDtypeStruct((BLK, GW), jnp.bfloat16)
    state = [
        pl.BlockSpec((1, BLK, HD), lambda h, sc: (h, chunk, 0)),
        pl.BlockSpec((1, BLK, HD), lambda h, sc: (h, chunk, 0)),
        pl.BlockSpec((1, BLK, HD), lambda h, sc: (h, 4 + chunk, 0)),
        pl.BlockSpec((1, BLK, HD), lambda h, sc: (h, 4 + chunk, 0)),
    ]
    return pl.pallas_call(
        far_kernel,
        grid_spec=pltpu.PrefetchScalarGridSpec(
            num_scalar_prefetch=1,
            grid=(GRP,),
            in_specs=[
                pl.BlockSpec((BLK, HD), lambda h, sc: (chunk, sc[0] * GRP + h)),
                pl.BlockSpec((BLK, HD), lambda h, sc: (chunk, h)),
                *state,
                *[pl.BlockSpec(memory_space=pl.ANY)] * 8,
            ],
            out_specs=[
                pl.BlockSpec((BLK, HD), lambda h, sc: (0, h)),
                pl.BlockSpec((BLK, HD), lambda h, sc: (0, h)),
            ],
            scratch_shapes=[
                pltpu.VMEM((POOL + BLK, 3 * HD), jnp.bfloat16),
                pltpu.SemaphoreType.DMA((8,)),
            ],
        ),
        out_shape=[out, out],
        compiler_params=pltpu.CompilerParams(vmem_limit_bytes=48 << 20),
        name="far_attention",
    )(scalars, queries, q_oth, o, l, o, l, *pieces)


def place_code(offset):
    step = offset % 4
    return jnp.where(step == 0, 0, jnp.where(step == 3, 1, step + 1))


def shards(queries, keys, values, columns, offsets, out_weight):
    me = lax.axis_index("ctx")
    core = me % 2
    chip = me // 2
    half = lax.axis_index("kvh")
    x, z, y, _ = coords(me)
    i32 = jnp.int32

    def cut(value, which, width, axis=1):
        return lax.dynamic_slice_in_dim(value, which * width, width, axis)

    kv_own = jnp.concatenate([cut(keys, core, HD), cut(values, core, HD)], axis=1)
    kv_sent = jnp.concatenate([cut(keys, 1 - core, HD), cut(values, 1 - core, HD)], axis=1)
    kv_oth = permute(kv_sent, send_core)
    lists = cut(columns, core, GRP, 0)
    group_offsets = cut(offsets, core, GRP, 0)

    blocks = jnp.arange(256, dtype=i32)
    listed = jnp.any(lists.reshape(-1)[:, None] == blocks[None, :], axis=0)
    runs = listed.reshape(64, 4).astype(i32)
    rank = jnp.stack(
        [jnp.zeros((64,), i32), runs[:, 0], runs[:, 0] + runs[:, 1], runs[:, :3].sum(1)], axis=1
    )
    slot_lane = jnp.arange(CAP, dtype=i32)
    chosen = (runs[:, :, None] > 0) & (rank[:, :, None] == slot_lane[None, None, :])
    picks = jnp.sum(jnp.where(chosen, jnp.arange(4, dtype=i32)[None, :, None], 0), axis=1)

    def pack(kv, run):
        pick = lax.dynamic_slice(picks, (run, 0), (1, CAP))[0]
        return jnp.concatenate(
            [lax.dynamic_slice_in_dim(kv, pick[k] * BLK, BLK, 0) for k in range(CAP)], axis=0
        )

    pool_a = pack(kv_own, me)
    pool_b = pack(kv_oth, me ^ 1)
    pool_a = jnp.concatenate([pool_a, permute(pool_a, send_y)], axis=0)
    pool_b = jnp.concatenate([pool_b, permute(pool_b, send_y)], axis=0)
    pool_a = jnp.concatenate(ring(pool_a, send_z), axis=0)
    pool_b = jnp.concatenate(ring(pool_b, send_x), axis=0)
    pieces = ring(pool_a, send_x) + ring(pool_b, send_z)

    q_oth = permute(cut(queries, 1 - core, GW), send_core)
    first = jnp.where(core == 0, kv_own, kv_oth)
    second = jnp.where(core == 0, kv_oth, kv_own)
    before = lax.ppermute(second, "ctx", [(i, i + 2) for i in range(62)])
    window = jnp.concatenate([before, first, second], axis=0)

    run = lists // 4
    src_x, src_z, src_y, src_c = coords(run)
    slot = jnp.sum(
        jnp.where(
            lists[:, :, None] == blocks[None, None, :], rank.reshape(-1)[None, None, :], 0
        ),
        axis=2,
    )
    code_x, code_z = place_code(src_x - x), place_code(src_z - z)
    rel_y = src_y ^ y
    code = jnp.where(
        src_c == core,
        code_x * 16 + (code_z * 2 + rel_y) * 2 + slot,
        64 + code_z * 16 + (code_x * 2 + rel_y) * 2 + slot,
    )
    start = chip * 8
    far = lists <= start - 5
    count = jnp.sum(far.astype(i32), axis=1)
    earlier = jnp.arange(NV)[:, None] < jnp.arange(NV)[None, :]
    far_rank = jnp.sum(jnp.where(far[:, :, None] & earlier[None], 1, 0), axis=1)
    lane = jnp.arange(NV, dtype=i32)
    packed = jnp.sum(
        jnp.where(
            far[:, :, None] & (far_rank[:, :, None] == lane[None, None, :]), code[:, :, None], 0
        ),
        axis=1,
    )
    filled = lane[None, :] < count[:, None]
    key_codes = jnp.where(filled, packed, packed[:, :1])
    value_codes = jnp.where(filled, packed, POOL // BLK)
    far_scalars = jnp.concatenate(
        [core[None].astype(i32), count, key_codes.reshape(-1), value_codes.reshape(-1)]
    )

    window_block = lists - (start - WINB)
    tiles = jnp.arange(8, dtype=i32)
    flags = jnp.any(window_block[:, :, None] == tiles[None, None, :], axis=1).astype(i32)
    extra = []
    for run_index in range(2):
        held = (window_block >= 4 * run_index) & (window_block < 4 * run_index + 4)
        low = jnp.min(jnp.where(held, window_block, 99), axis=1)
        high = jnp.min(jnp.where(held & (window_block > low[:, None]), window_block, 99), axis=1)
        extra += [low, high]
    near_scalars = jnp.concatenate(
        [
            core[None].astype(i32),
            (chip == 0).astype(i32)[None],
            flags.reshape(-1),
            jnp.stack(extra, axis=1).reshape(-1),
        ]
    )
    distance = WIN - jnp.arange(BAND, dtype=i32)
    in_band = jnp.any(group_offsets[:, :, None] == distance[None, None, :], axis=1)
    pattern = jnp.broadcast_to(
        jnp.where(in_band, 0.0, NEG).astype(jnp.float32)[:, None, :], (GRP, 8, BAND)
    )

    o, l = near_attention(near_scalars, queries, q_oth, window, pattern)

    columns_out = out_weight.shape[1] // 2
    weight_kept = cut(out_weight, half, columns_out)
    weight_sent = cut(out_weight, 1 - half, columns_out)
    results = []
    for chunk in range(CHUNKS):
        own, oth = far_attention(chunk, far_scalars, queries, q_oth, o, l, pieces)
        got = permute(oth, send_core)
        attended = jnp.where(
            core == 0, jnp.concatenate([own, got], 1), jnp.concatenate([got, own], 1)
        )
        sent = jnp.dot(attended, weight_sent, preferred_element_type=jnp.float32)
        taken = permute(sent.astype(jnp.bfloat16), lambda i: 1 - i, "kvh")
        kept = jnp.dot(attended, weight_kept, preferred_element_type=jnp.float32)
        results.append((kept + taken.astype(jnp.float32)).astype(jnp.bfloat16))
    return jnp.concatenate(results, axis=0)


def solution(mesh):
    placed = (
        P("ctx", "kvh"),
        P("ctx", "kvh"),
        P("ctx", "kvh"),
        P("kvh", None),
        P("kvh", None),
        P("kvh", None),
    )
    return jax.shard_map(
        shards, mesh=mesh, in_specs=placed, out_specs=P("ctx", "kvh"), check_vma=False
    )
```

```python
import functools
import math

import jax
import jax.numpy as jnp
from jax import lax
from jax.experimental import pallas as pl
from jax.experimental.pallas import tpu as pltpu
from jax.sharding import PartitionSpec as P

HD = 128
BLK = 128
NV = 16
CAP = 2
WIN = 512
TOK = 512
GRP = 7
GW = GRP * HD
CHUNKS = 4
WINB = WIN // BLK
BAND = WIN + BLK
NEG = -1e30
LOG2 = math.log2(math.e) / math.sqrt(HD)


def coords(i):
    return i // 16, i // 4 % 4, i // 2 % 2, i % 2


def index(x, z, y, c):
    return (x % 4) * 16 + (z % 4) * 4 + (y % 2) * 2 + c % 2


def send_x(by):
    def to(i):
        x, z, y, c = coords(i)
        return index(x + by, z, y, c)

    return to


def send_z(by):
    def to(i):
        x, z, y, c = coords(i)
        return index(x, z + by, y, c)

    return to


def send_y(i):
    x, z, y, c = coords(i)
    return index(x, z, y + 1, c)


def send_core(i):
    return i ^ 1


def permute(value, to, axis="ctx"):
    return lax.ppermute(value, axis, [(i, to(i)) for i in range(lax.axis_size(axis))])


def ring(piece, send):
    middle = piece.shape[0] // 2
    low = permute(piece, send(1))
    high = permute(piece, send(-1))
    return [
        piece,
        low,
        high,
        permute(low[:middle], send(1)),
        permute(high[middle:], send(-1)),
    ]


def dot_t(a, b):
    return lax.dot_general(a, b, (((1,), (1,)), ((), ())), preferred_element_type=jnp.float32)


def near_kernel(sc, q_own, q_oth, kv, pattern, o_ref, l_ref, vext, acc_s, m_s):
    h = pl.program_id(0)

    @pl.when(h == 0)
    def _():
        vext[:, :HD] = kv[:, HD:]
        vext[:, HD:] = jnp.ones((vext.shape[0], HD), jnp.bfloat16)

    bias = pltpu.roll(
        jnp.broadcast_to(pattern[0, 0:1, :], (BLK, BAND)), 0, 1, stride=1, stride_axis=0
    )
    rows = lax.broadcasted_iota(jnp.int32, (BLK, BLK), 0)
    lanes = lax.broadcasted_iota(jnp.int32, (BLK, BLK), 1)
    far_side = lanes <= rows
    band_lane = lax.broadcasted_iota(jnp.int32, (1, BAND), 1)
    core = sc[0]

    def tile_of(i):
        return (i // 4, i % 4, 4 * jnp.where(i // 4 == 0, core, 1 - core) + i % 4)

    def q_of(part, k):
        return (q_own if part == 0 else q_oth)[k * BLK : (k + 1) * BLK, :]

    for i in range(8):
        part, k, t = tile_of(i)
        base = pl.multiple_of(t * BLK, BLK)
        s = dot_t(q_of(part, k), kv[pl.ds(base, BAND), :HD])
        listed = jnp.where(sc[2 + h * 8 + t] > 0, 0.0, NEG).astype(jnp.float32)
        first = jnp.where(far_side, listed, bias[:, :BLK])
        absent = jnp.where(sc[1] > 0, BLK * (WINB - t), 0)
        edge = jnp.where(band_lane < absent, NEG, 0.0).astype(jnp.float32)
        s = s + jnp.concatenate([first, bias[:, BLK:]], axis=1) + edge
        m = jnp.max(s, axis=1, keepdims=True)
        p = jnp.exp2((s - m) * LOG2).astype(jnp.bfloat16)
        acc_s[i] = jnp.dot(p, vext[pl.ds(base, BAND), :], preferred_element_type=jnp.float32)
        m_s[i] = jnp.broadcast_to(m, (BLK, BLK))

    ex = 2 + 8 * GRP + 4 * h
    lowest = jnp.minimum(jnp.minimum(sc[ex], sc[ex + 1]), jnp.minimum(sc[ex + 2], sc[ex + 3]))

    @pl.when(lowest < 8)
    def _():
        for i in range(8):
            part, k, t = tile_of(i)
            for g in range(2):
                wa, wb = sc[ex + 2 * g], sc[ex + 2 * g + 1]

                @pl.when((wa < t) | (wb < t))
                def _():
                    ra = pl.multiple_of(jnp.minimum(wa, 11) * BLK, BLK)
                    rb = pl.multiple_of(jnp.minimum(wb, 11) * BLK, BLK)
                    ks = jnp.concatenate([kv[pl.ds(ra, BLK), :HD], kv[pl.ds(rb, BLK), :HD]], 0)
                    vs = jnp.concatenate([vext[pl.ds(ra, BLK), :], vext[pl.ds(rb, BLK), :]], 0)
                    s = dot_t(q_of(part, k), ks)
                    lane = lax.broadcasted_iota(jnp.int32, (1, 2 * BLK), 1)
                    ba = jnp.where(wa < t, 0.0, NEG).astype(jnp.float32)
                    bb = jnp.where(wb < t, 0.0, NEG).astype(jnp.float32)
                    s = s + jnp.where(lane < BLK, ba, bb)
                    m_old = m_s[i]
                    m_new = jnp.maximum(m_old, jnp.max(s, axis=1, keepdims=True))
                    scale = jnp.exp2((m_old - m_new) * LOG2)
                    p = jnp.exp2((s - jnp.concatenate([m_new, m_new], 1)) * LOG2)
                    acc_s[i] = acc_s[i] * jnp.concatenate([scale, scale], 1) + jnp.dot(
                        p.astype(jnp.bfloat16), vs, preferred_element_type=jnp.float32
                    )
                    m_s[i] = m_new

    for i in range(8):
        total = acc_s[i, :, HD:]
        o_ref[0, i * BLK : (i + 1) * BLK, :] = acc_s[i, :, :HD] / total
        l_ref[0, i * BLK : (i + 1) * BLK, :] = m_s[i] * LOG2 + jnp.log2(total)


def near_attention(scalars, queries, q_oth, window, pattern):
    rows = 8 * BLK
    state = jax.ShapeDtypeStruct((GRP, rows, HD), jnp.float32)
    return pl.pallas_call(
        near_kernel,
        grid_spec=pltpu.PrefetchScalarGridSpec(
            num_scalar_prefetch=1,
            grid=(GRP,),
            in_specs=[
                pl.BlockSpec((TOK, HD), lambda h, sc: (0, sc[0] * GRP + h)),
                pl.BlockSpec((TOK, HD), lambda h, sc: (0, h)),
                pl.BlockSpec((3 * TOK, 2 * HD), lambda h, sc: (0, 0)),
                pl.BlockSpec((1, 8, BAND), lambda h, sc: (h, 0, 0)),
            ],
            out_specs=[
                pl.BlockSpec((1, rows, HD), lambda h, sc: (h, 0, 0)),
                pl.BlockSpec((1, rows, HD), lambda h, sc: (h, 0, 0)),
            ],
            scratch_shapes=[
                pltpu.VMEM((3 * TOK, 2 * HD), jnp.bfloat16),
                pltpu.VMEM((8, BLK, 2 * HD), jnp.float32),
                pltpu.VMEM((8, BLK, BLK), jnp.float32),
            ],
        ),
        out_shape=[state, state],
        compiler_params=pltpu.CompilerParams(vmem_limit_bytes=40 << 20),
        name="near_attention",
    )(scalars, queries, q_oth, window, pattern)


def pack_kernel(sc, lists, keys, values, own_slots, oth_slots, kv_own, kv_sent, sem):
    core, me = sc[0], sc[1]
    group = lax.broadcasted_iota(jnp.int32, lists.shape, 0) // GRP
    table = lists[...]
    copies = []

    def copy(source, head, row, rows, target, at, side):
        cols = pl.ds(pl.multiple_of(head * HD, HD), HD)
        copies.append(
            pltpu.make_async_copy(
                source.at[pl.ds(row, rows), cols],
                target.at[pl.ds(at, rows), pl.ds(side * HD, HD)],
                sem.at[len(copies)],
            )
        )
        copies[-1].start()

    for head, slots in ((core, own_slots), (1 - core, oth_slots)):
        pick = [jnp.int32(0)] * CAP
        seen = jnp.int32(0)
        for b in range(TOK // BLK):
            hit = jnp.max(jnp.where((group == head) & (table == me * (TOK // BLK) + b), 1, 0))
            for k in range(CAP):
                pick[k] = jnp.where((hit > 0) & (seen == k), b, pick[k])
            seen = seen + hit
        for k in range(CAP):
            row = pl.multiple_of(pick[k] * BLK, BLK)
            copy(keys, head, row, BLK, slots, k * BLK, 0)
            copy(values, head, row, BLK, slots, k * BLK, 1)
    for head, target in ((core, kv_own), (1 - core, kv_sent)):
        copy(keys, head, 0, TOK, target, 0, 0)
        copy(values, head, 0, TOK, target, 0, 1)
    for done in copies:
        done.wait()


def pack(scalars, columns, keys, values):
    slots = jax.ShapeDtypeStruct((CAP * BLK, 2 * HD), jnp.bfloat16)
    whole = jax.ShapeDtypeStruct((TOK, 2 * HD), jnp.bfloat16)
    anywhere = pl.BlockSpec(memory_space=pl.ANY)
    return pl.pallas_call(
        pack_kernel,
        grid_spec=pltpu.PrefetchScalarGridSpec(
            num_scalar_prefetch=1,
            grid=(1,),
            in_specs=[pl.BlockSpec(columns.shape, lambda i, sc: (0, 0)), anywhere, anywhere],
            out_specs=[anywhere] * 4,
            scratch_shapes=[pltpu.SemaphoreType.DMA((12,))],
        ),
        out_shape=[slots, slots, whole, whole],
        name="pack_blocks",
    )(scalars, columns, keys, values)


ROWS = 2 * TOK
SUB = 2 * BLK


def far_kernel(heights, sizes, last, sc, q_own, q_oth, o_in, l_in, *rest):
    pieces, rest = rest[: len(heights)], rest[len(heights) :]
    outs, (pool, sem) = rest[:-2], rest[-2:]
    total = sum(heights)
    h = pl.program_id(0)

    @pl.when(h == 0)
    def _():
        copies = []
        at = 0
        for k, height in enumerate(heights):
            copies.append(
                pltpu.make_async_copy(
                    pieces[k], pool.at[pl.ds(at, height), pl.ds(0, 2 * HD)], sem.at[k]
                )
            )
            copies[-1].start()
            at += height
        pool[:total, 2 * HD :] = jnp.ones((total, HD), jnp.bfloat16)
        pool[total:, :] = jnp.zeros((BLK, 3 * HD), jnp.bfloat16)
        for copy in copies:
            copy.wait()

    def put(rows, o, l):
        part = rows.start // TOK
        if last:
            local = slice(rows.start - part * TOK, rows.stop - part * TOK)
            outs[part][local, :] = o.astype(jnp.bfloat16)
        else:
            outs[0][0, rows, :] = o
            outs[1][0, rows, :] = l

    n = sc[1 + h]
    below = 0
    for size in sizes:

        @pl.when((n > below) & (n <= size))
        def _(size=size):
            def row(at, j):
                return pl.ds(pl.multiple_of(sc[at + h * NV + j] * BLK, BLK), BLK)

            for r in range(ROWS // SUB):
                rows = slice(r * SUB, (r + 1) * SUB)
                part = rows.start // TOK
                local = slice(rows.start - part * TOK, rows.stop - part * TOK)
                q = (q_own if part == 0 else q_oth)[local, :]
                ks = jnp.concatenate([pool[row(8, j), :HD] for j in range(size)], axis=0)
                s = dot_t(q, ks)
                m = jnp.max(s, axis=1, keepdims=True)
                p = jnp.exp2((s - m) * LOG2).astype(jnp.bfloat16)
                vs = jnp.concatenate(
                    [pool[row(8 + GRP * NV, j), HD:] for j in range(size)], axis=0
                )
                acc = jnp.dot(p, vs, preferred_element_type=jnp.float32)
                top = jnp.broadcast_to(m * LOG2, (SUB, HD))
                o, l = o_in[0, rows, :], l_in[0, rows, :]
                both = jnp.maximum(l, top)
                wn = jnp.exp2(l - both)
                wf = jnp.exp2(top - both)
                weight = wn + acc[:, HD:] * wf
                o = (o * wn + acc[:, :HD] * wf) / weight
                put(rows, o, None if last else both + jnp.log2(weight))

        below = size

    @pl.when(n == 0)
    def _():
        for r in range(ROWS // SUB):
            rows = slice(r * SUB, (r + 1) * SUB)
            put(rows, o_in[0, rows, :], l_in[0, rows, :])


def far_attention(last, sizes, scalars, queries, q_oth, o, l, pieces):
    heights = [piece.shape[0] for piece in pieces]
    state = pl.BlockSpec((1, ROWS, HD), lambda h, sc: (h, 0, 0))
    flat = pl.BlockSpec((TOK, HD), lambda h, sc: (0, h))
    if last:
        out_specs = [flat, flat]
        out_shape = [jax.ShapeDtypeStruct((TOK, GW), jnp.bfloat16)] * 2
    else:
        out_specs = [state, state]
        out_shape = [jax.ShapeDtypeStruct((GRP, ROWS, HD), jnp.float32)] * 2
    return pl.pallas_call(
        functools.partial(far_kernel, heights, sizes, last),
        grid_spec=pltpu.PrefetchScalarGridSpec(
            num_scalar_prefetch=1,
            grid=(GRP,),
            in_specs=[
                pl.BlockSpec((TOK, HD), lambda h, sc: (0, sc[0] * GRP + h)),
                flat,
                state,
                state,
                *[pl.BlockSpec(memory_space=pl.ANY)] * len(pieces),
            ],
            out_specs=out_specs,
            scratch_shapes=[
                pltpu.VMEM((sum(heights) + BLK, 3 * HD), jnp.bfloat16),
                pltpu.SemaphoreType.DMA((len(pieces),)),
            ],
        ),
        out_shape=out_shape,
        compiler_params=pltpu.CompilerParams(vmem_limit_bytes=48 << 20),
        name="far_last" if last else "far_first",
    )(scalars, queries, q_oth, o, l, *pieces)


def place_code(offset):
    step = offset % 4
    return jnp.where(step == 0, 0, jnp.where(step == 3, 1, step + 1))


def shards(queries, keys, values, columns, offsets, out_weight):
    me = lax.axis_index("ctx")
    core = me % 2
    chip = me // 2
    half = lax.axis_index("kvh")
    x, z, y, _ = coords(me)
    i32 = jnp.int32

    def cut(value, which, width, axis=1):
        return lax.dynamic_slice_in_dim(value, which * width, width, axis)

    own_slots, oth_slots, kv_own, kv_sent = pack(
        jnp.stack([core, me]).astype(i32), columns, keys, values
    )
    pool_a = own_slots
    pool_b = permute(oth_slots, send_core)
    pool_a = jnp.concatenate([pool_a, permute(pool_a, send_y)], axis=0)
    pool_b = jnp.concatenate([pool_b, permute(pool_b, send_y)], axis=0)
    pool_a, columns, offsets = lax.optimization_barrier((pool_a, columns, offsets))
    ring_a = ring(jnp.concatenate(ring(pool_a, send_z), axis=0), send_x)
    ring_b = ring(jnp.concatenate(ring(pool_b, send_x), axis=0), send_z)

    kv_oth = permute(kv_sent, send_core)
    q_oth = permute(cut(queries, 1 - core, GW), send_core)
    first = jnp.where(core == 0, kv_own, kv_oth)
    second = jnp.where(core == 0, kv_oth, kv_own)
    before = lax.ppermute(second, "ctx", [(i, i + 2) for i in range(62)])
    window = jnp.concatenate([before, first, second], axis=0)

    lists = cut(columns, core, GRP, 0)
    group_offsets = cut(offsets, core, GRP, 0)
    run = lists // 4
    src_x, src_z, src_y, src_c = coords(run)
    names = lists.reshape(-1)
    lower = (names[:, None] // 4 == names[None, :] // 4) & (names[None, :] < names[:, None])
    slot = jnp.any(lower, axis=1).astype(i32).reshape(GRP, NV)
    code_x, code_z = place_code(src_x - x), place_code(src_z - z)
    low = (src_y ^ y) * 2 + slot
    same = src_c == core
    piece = jnp.where(same, code_x, code_z)
    within = jnp.where(same, code_z, code_x) * 4 + low
    start = chip * 8
    far = lists <= start - 5
    lane = jnp.arange(NV, dtype=i32)

    def tables(taken, code, blocks):
        count = jnp.sum(taken.astype(i32), axis=1)
        place = jnp.sum(jnp.where(taken[:, :, None] & (lane[:, None] < lane[None, :]), 1, 0), axis=1)
        hit = taken[:, :, None] & (place[:, :, None] == lane[None, None, :])
        packed = jnp.sum(jnp.where(hit, code[:, :, None], 0), axis=1)
        filled = lane[None, :] < count[:, None]
        key_codes = jnp.where(filled, packed, packed[:, :1])
        value_codes = jnp.where(filled, packed, blocks)
        return jnp.concatenate(
            [core[None].astype(i32), count, key_codes.reshape(-1), value_codes.reshape(-1)]
        )

    first_scalars = tables(far & (piece < 3), jnp.where(same, 0, 48) + piece * 16 + within, 96)
    last_scalars = tables(far & (piece == 3), jnp.where(same, 0, 16) + within, 32)

    window_block = lists - (start - WINB)
    tiles = jnp.arange(8, dtype=i32)
    flags = jnp.any(window_block[:, :, None] == tiles[None, None, :], axis=1).astype(i32)
    extra = []
    for run_index in range(2):
        held = (window_block >= 4 * run_index) & (window_block < 4 * run_index + 4)
        low = jnp.min(jnp.where(held, window_block, 99), axis=1)
        high = jnp.min(jnp.where(held & (window_block > low[:, None]), window_block, 99), axis=1)
        extra += [low, high]
    near_scalars = jnp.concatenate(
        [
            core[None].astype(i32),
            (chip == 0).astype(i32)[None],
            flags.reshape(-1),
            jnp.stack(extra, axis=1).reshape(-1),
        ]
    )
    distance = WIN - jnp.arange(BAND, dtype=i32)
    in_band = jnp.any(group_offsets[:, :, None] == distance[None, None, :], axis=1)
    pattern = jnp.broadcast_to(
        jnp.where(in_band, 0.0, NEG).astype(jnp.float32)[:, None, :], (GRP, 8, BAND)
    )

    o, l = near_attention(near_scalars, queries, q_oth, window, pattern)

    o, l = far_attention(
        False, (8, 12, 16), first_scalars, queries, q_oth, o, l, ring_a[:3] + ring_b[:3]
    )
    own, oth = far_attention(
        True, (4, 8, 16), last_scalars, queries, q_oth, o, l, ring_a[3:] + ring_b[3:]
    )

    columns_out = out_weight.shape[1] // 2
    weight_kept = cut(out_weight, half, columns_out)
    weight_sent = cut(out_weight, 1 - half, columns_out)
    results = []
    for chunk in range(CHUNKS):
        rows = slice(chunk * BLK, (chunk + 1) * BLK)
        got = permute(oth[rows], send_core)
        attended = jnp.where(
            core == 0,
            jnp.concatenate([own[rows], got], 1),
            jnp.concatenate([got, own[rows]], 1),
        )
        sent = jnp.dot(attended, weight_sent, preferred_element_type=jnp.float32)
        taken = permute(sent.astype(jnp.bfloat16), lambda i: 1 - i, "kvh")
        kept = jnp.dot(attended, weight_kept, preferred_element_type=jnp.float32)
        results.append((kept + taken.astype(jnp.float32)).astype(jnp.bfloat16))
    return jnp.concatenate(results, axis=0)


def solution(mesh):
    placed = (
        P("ctx", "kvh"),
        P("ctx", "kvh"),
        P("ctx", "kvh"),
        P("kvh", None),
        P("kvh", None),
        P("kvh", None),
    )
    return jax.shard_map(
        shards, mesh=mesh, in_specs=placed, out_specs=P("ctx", "kvh"), check_vma=False
    )
```

```python
import functools
import math

import jax
import jax.numpy as jnp
from jax import lax
from jax.experimental import pallas as pl
from jax.experimental.pallas import tpu as pltpu
from jax.sharding import PartitionSpec as P

HD = 128
BLK = 128
NV = 16
CAP = 2
WIN = 512
TOK = 512
GRP = 7
GW = GRP * HD
WINB = WIN // BLK
NEG = -1e30
LOG2 = math.log2(math.e) / math.sqrt(HD)


def coords(i):
    return i // 16, i // 4 % 4, i // 2 % 2, i % 2


def index(x, z, y, c):
    return (x % 4) * 16 + (z % 4) * 4 + (y % 2) * 2 + c % 2


def send_x(by):
    def to(i):
        x, z, y, c = coords(i)
        return index(x + by, z, y, c)

    return to


def send_z(by):
    def to(i):
        x, z, y, c = coords(i)
        return index(x, z + by, y, c)

    return to


def send_y(i):
    x, z, y, c = coords(i)
    return index(x, z, y + 1, c)


def send_core(i):
    return i ^ 1


def permute(value, to, axis="ctx"):
    return lax.ppermute(value, axis, [(i, to(i)) for i in range(lax.axis_size(axis))])


def ring(piece, send):
    return [piece] + [permute(piece, send(by)) for by in (1, -1, 2)]


def dot_t(a, b):
    return lax.dot_general(a, b, (((1,), (1,)), ((), ())), preferred_element_type=jnp.float32)


TILE = 2 * BLK
SPAN = WIN + TILE
NEAR_FLAGS = 2
NEAR_EXTRA = NEAR_FLAGS + 8 * GRP
NEAR_SIZE = NEAR_EXTRA + 4 * GRP
PIECES = 8
FAR_OFF = 1 + GRP
FAR_CODE = FAR_OFF + GRP * (PIECES + 1)
FAR_SIZE = FAR_CODE + GRP * NV


def table_kernel(sc, lists, near, far, marks, codes, heads):
    me = sc[0]
    core, chip = me % 2, me // 2
    x, z, y = chip // 8, chip // 2 % 4, chip % 2
    start = chip * 8
    near[0] = core
    near[1] = (chip == 0).astype(jnp.int32)
    far[0] = core

    def clear(i, _):
        for k in range(4):
            marks[4 * i + k] = 0
        return 0

    lax.fori_loop(0, 64, clear, 0)

    def clear_near(i, _):
        near[NEAR_FLAGS + i] = 0
        near[NEAR_EXTRA + i // 2] = 99
        return 0

    lax.fori_loop(0, 8 * GRP, clear_near, 0)

    def mark(h, _):
        for j in range(NV):
            marks[lists[core * GRP + h, j]] = 1
        return 0

    lax.fori_loop(0, GRP, mark, 0)

    def place(step):
        return jnp.where(step == 0, 0, jnp.where(step == 3, 1, step + 1))

    def one_head(h, _):
        for k in range(PIECES):
            heads[k] = 0

        def classify(j, _):
            b = lists[core * GRP + h, j]
            run = b // 4
            at = b % 4
            base = b - at
            slot = jnp.where(at > 0, marks[base], 0)
            slot = slot + jnp.where(at > 1, marks[base + 1], 0)
            slot = slot + jnp.where(at > 2, marks[base + 2], 0)
            cx = place((run // 16 - x + 4) % 4)
            cz = place((run // 4 % 4 - z + 4) % 4)
            same = run % 2 == core
            piece = jnp.where(same, cx, 4 + cz)
            low = jnp.where(run // 2 % 2 == y, 0, 2) + jnp.minimum(slot, 1)
            within = jnp.where(same, cz, cx) * 4 + low
            far_block = b <= start - 5
            codes[j] = jnp.where(far_block, piece * 16 + within, -1)
            heads[piece] = heads[piece] + far_block.astype(jnp.int32)
            w = b - (start - WINB)

            @pl.when((w >= 0) & (w < 8))
            def _():
                near[NEAR_FLAGS + h * 8 + w] = 1
                pair = NEAR_EXTRA + h * 4 + (w // 4) * 2
                second = (near[pair] < 99).astype(jnp.int32)
                near[pair + second] = w

            return 0

        lax.fori_loop(0, NV, classify, 0)
        total = jnp.int32(0)
        for k in range(PIECES):
            far[FAR_OFF + h * (PIECES + 1) + k] = total
            held = heads[k]
            heads[k] = total
            total = total + held
        far[FAR_OFF + h * (PIECES + 1) + PIECES] = total
        far[1 + h] = total

        def store(j, _):
            code = codes[j]

            @pl.when(code >= 0)
            def _():
                k = code // 16
                far[FAR_CODE + h * NV + heads[k]] = code % 16
                heads[k] = heads[k] + 1

            return 0

        lax.fori_loop(0, NV, store, 0)
        return 0

    lax.fori_loop(0, GRP, one_head, 0)


def tables(me, columns):
    smem = pltpu.MemorySpace.SMEM
    return pl.pallas_call(
        table_kernel,
        in_specs=[pl.BlockSpec(memory_space=smem)] * 2,
        out_specs=[pl.BlockSpec(memory_space=smem)] * 2,
        out_shape=[
            jax.ShapeDtypeStruct((NEAR_SIZE,), jnp.int32),
            jax.ShapeDtypeStruct((FAR_SIZE,), jnp.int32),
        ],
        scratch_shapes=[
            pltpu.SMEM((256,), jnp.int32),
            pltpu.SMEM((NV,), jnp.int32),
            pltpu.SMEM((PIECES,), jnp.int32),
        ],
        name="index_tables",
    )(me, columns)


def near_kernel(
    sc, q_own, q_oth, kv_own, kv_oth, kv_low, kv_high, offs, o_ref, l_ref, kext, vext, acc_s, m_s
):
    h = pl.program_id(0)
    core = sc[0]

    @pl.when(h == 0)
    def _():
        own_at = pl.ds(pl.multiple_of(TOK + core * TOK, TOK), TOK)
        oth_at = pl.ds(pl.multiple_of(2 * TOK - core * TOK, TOK), TOK)
        for at, part in ((own_at, kv_own), (oth_at, kv_oth)):
            kext[at, :] = part[:, :HD]
            vext[at, :HD] = part[:, HD:]

        @pl.when(core == 0)
        def _():
            kext[:TOK, :] = kv_low[:, :HD]
            vext[:TOK, :HD] = kv_low[:, HD:]

        @pl.when(core == 1)
        def _():
            kext[:TOK, :] = kv_high[:, :HD]
            vext[:TOK, :HD] = kv_high[:, HD:]

        vext[:, HD:] = jnp.ones((vext.shape[0], HD), jnp.bfloat16)

    line = offs[pl.ds(core * GRP + h, 1), :]
    spread = jnp.broadcast_to(line.astype(jnp.float32), (BLK, BLK)).T
    lane = lax.broadcasted_iota(jnp.int32, (BLK, BLK), 1)
    marks = []
    for k in range(SPAN // BLK):
        hit = spread == (WIN - k * BLK - lane).astype(jnp.float32)
        marks.append(jnp.max(jnp.where(hit, 0.0, NEG), axis=0, keepdims=True))
    pattern = jnp.concatenate(marks, axis=1)
    bias = pltpu.roll(
        jnp.broadcast_to(pattern, (TILE, SPAN)), 0, 1, stride=1, stride_axis=0
    )
    rows = lax.broadcasted_iota(jnp.int32, (TILE, TILE), 0)
    lanes = lax.broadcasted_iota(jnp.int32, (TILE, TILE), 1)
    far_side = lanes <= rows
    tile_lane = lax.broadcasted_iota(jnp.int32, (1, TILE), 1)
    span_lane = lax.broadcasted_iota(jnp.int32, (1, SPAN), 1)

    def tile_of(i):
        return 4 * (core if i < 2 else 1 - core) + 2 * (i % 2)

    def q_of(i):
        return (q_own if i < 2 else q_oth)[(i % 2) * TILE : (i % 2 + 1) * TILE, :]

    for i in range(4):
        t = tile_of(i)
        base = pl.multiple_of(t * BLK, BLK)
        s = dot_t(q_of(i), kext[pl.ds(base, SPAN), :])
        flag = NEAR_FLAGS + h * 8 + t
        la = jnp.where(sc[flag] > 0, 0.0, NEG).astype(jnp.float32)
        lb = jnp.where(sc[flag + 1] > 0, 0.0, NEG).astype(jnp.float32)
        first = jnp.where(far_side, jnp.where(tile_lane < BLK, la, lb), bias[:, :TILE])
        absent = jnp.where(sc[1] > 0, BLK * (WINB - t), 0)
        edge = jnp.where(span_lane < absent, NEG, 0.0).astype(jnp.float32)
        s = s + jnp.concatenate([first, bias[:, TILE:]], axis=1) + edge
        m = jnp.max(s, axis=1, keepdims=True)
        p = jnp.exp2((s - m) * LOG2).astype(jnp.bfloat16)
        acc_s[i] = jnp.dot(p, vext[pl.ds(base, SPAN), :], preferred_element_type=jnp.float32)
        m_s[i] = jnp.broadcast_to(m, (TILE, HD))

    ex = NEAR_EXTRA + 4 * h
    lowest = jnp.minimum(jnp.minimum(sc[ex], sc[ex + 1]), jnp.minimum(sc[ex + 2], sc[ex + 3]))

    @pl.when(lowest < 6)
    def _():
        for i in range(4):
            t = tile_of(i)
            for g in range(2):
                wa, wb = sc[ex + 2 * g], sc[ex + 2 * g + 1]

                @pl.when((wa < t) | (wb < t))
                def _():
                    ra = pl.multiple_of(jnp.minimum(wa, 11) * BLK, BLK)
                    rb = pl.multiple_of(jnp.minimum(wb, 11) * BLK, BLK)
                    ks = jnp.concatenate([kext[pl.ds(ra, BLK), :], kext[pl.ds(rb, BLK), :]], 0)
                    vs = jnp.concatenate([vext[pl.ds(ra, BLK), :], vext[pl.ds(rb, BLK), :]], 0)
                    s = dot_t(q_of(i), ks)
                    ba = jnp.where(wa < t, 0.0, NEG).astype(jnp.float32)
                    bb = jnp.where(wb < t, 0.0, NEG).astype(jnp.float32)
                    s = s + jnp.where(tile_lane < BLK, ba, bb)
                    m_old = m_s[i]
                    m_new = jnp.maximum(m_old, jnp.max(s, axis=1, keepdims=True))
                    scale = jnp.exp2((m_old - m_new) * LOG2)
                    p = jnp.exp2((s - jnp.concatenate([m_new, m_new], 1)) * LOG2)
                    acc_s[i] = acc_s[i] * jnp.concatenate([scale, scale], 1) + jnp.dot(
                        p.astype(jnp.bfloat16), vs, preferred_element_type=jnp.float32
                    )
                    m_s[i] = m_new

    for i in range(4):
        total = acc_s[i, :, HD:]
        o_ref[0, i * TILE : (i + 1) * TILE, :] = acc_s[i, :, :HD] / total
        l_ref[0, i * TILE : (i + 1) * TILE, :] = m_s[i] * LOG2 + jnp.log2(total)


def near_attention(scalars, queries, q_oth, parts, offsets):
    rows = 2 * TOK
    state = jax.ShapeDtypeStruct((GRP, rows, HD), jnp.float32)
    q_spec = pl.BlockSpec((TOK, HD), lambda h, sc: (0, sc[0] * GRP + h))
    return pl.pallas_call(
        near_kernel,
        grid_spec=pltpu.PrefetchScalarGridSpec(
            num_scalar_prefetch=1,
            grid=(GRP,),
            in_specs=[
                q_spec,
                q_spec,
                *[pl.BlockSpec((TOK, 2 * HD), lambda h, sc: (0, 0))] * 4,
                pl.BlockSpec(offsets.shape, lambda h, sc: (0, 0)),
            ],
            out_specs=[
                pl.BlockSpec((1, rows, HD), lambda h, sc: (h, 0, 0)),
                pl.BlockSpec((1, rows, HD), lambda h, sc: (h, 0, 0)),
            ],
            scratch_shapes=[
                pltpu.VMEM((3 * TOK, HD), jnp.bfloat16),
                pltpu.VMEM((3 * TOK, 2 * HD), jnp.bfloat16),
                pltpu.VMEM((4, TILE, 2 * HD), jnp.float32),
                pltpu.VMEM((4, TILE, HD), jnp.float32),
            ],
        ),
        out_shape=[state, state],
        compiler_params=pltpu.CompilerParams(vmem_limit_bytes=40 << 20),
        name="near_attention",
    )(scalars, queries, q_oth, *parts, offsets)


def pack_kernel(sc, lists, keys, values, own_slots, oth_slots, kv_own, kv_sent):
    core, me = sc[0], sc[1]
    group = lax.broadcasted_iota(jnp.int32, lists.shape, 0) // GRP
    table = lists[...]

    def head_of(source, head, rows):
        low, high = source[rows, :HD], source[rows, HD:]
        return jnp.where(head == 0, low, high)

    for head, slots in ((core, own_slots), (1 - core, oth_slots)):
        pick = [jnp.int32(0)] * CAP
        seen = jnp.int32(0)
        for b in range(TOK // BLK):
            hit = jnp.max(jnp.where((group == head) & (table == me * (TOK // BLK) + b), 1, 0))
            for k in range(CAP):
                pick[k] = jnp.where((hit > 0) & (seen == k), b, pick[k])
            seen = seen + hit
        for k in range(CAP):
            rows = pl.ds(pl.multiple_of(pick[k] * BLK, BLK), BLK)
            slots[k * BLK : (k + 1) * BLK, :HD] = head_of(keys, head, rows)
            slots[k * BLK : (k + 1) * BLK, HD:] = head_of(values, head, rows)
    whole = slice(0, TOK)
    for head, target in ((core, kv_own), (1 - core, kv_sent)):
        target[:, :HD] = head_of(keys, head, whole)
        target[:, HD:] = head_of(values, head, whole)


def pack(scalars, columns, keys, values):
    slots = jax.ShapeDtypeStruct((CAP * BLK, 2 * HD), jnp.bfloat16)
    whole = jax.ShapeDtypeStruct((TOK, 2 * HD), jnp.bfloat16)

    def full(shape):
        return pl.BlockSpec(shape, lambda i, sc: (0, 0))

    return pl.pallas_call(
        pack_kernel,
        grid_spec=pltpu.PrefetchScalarGridSpec(
            num_scalar_prefetch=1,
            grid=(1,),
            in_specs=[full(columns.shape), full(keys.shape), full(values.shape)],
            out_specs=[full(a.shape) for a in (slots, slots, whole, whole)],
        ),
        out_shape=[slots, slots, whole, whole],
        name="pack_blocks",
    )(scalars, columns, keys, values)


FAR_ROWS = TOK // 2
SIZES = (8, 16)


def far_kernel(sc, q_own, q_oth, oa, la, ob, lb, *rest):
    pieces, (out_own, out_oth, buf, sem) = rest[:PIECES], rest[PIECES:]
    h = pl.program_id(0)

    def fetch(head, slot):
        for k in range(PIECES):
            at = FAR_OFF + head * (PIECES + 1) + k

            def start(i, _, k=k):
                code = sc[FAR_CODE + head * NV + i]
                pltpu.make_async_copy(
                    pieces[k].at[pl.ds(pl.multiple_of(code * BLK, BLK), BLK), :],
                    buf.at[slot, pl.ds(pl.multiple_of(i * BLK, BLK), BLK), pl.ds(0, 2 * HD)],
                    sem.at[slot],
                ).start()
                return 0

            lax.fori_loop(sc[at], sc[at + 1], start, 0)

    slot = h % 2

    @pl.when(h == 0)
    def _():
        fetch(0, 0)

    @pl.when(h + 1 < GRP)
    def _():
        fetch(h + 1, 1 - slot)

    n = sc[1 + h]

    def arrived(i, _):
        pltpu.make_async_copy(
            pieces[0].at[pl.ds(0, BLK), :],
            buf.at[slot, pl.ds(0, BLK), pl.ds(0, 2 * HD)],
            sem.at[slot],
        ).wait()
        return 0

    lax.fori_loop(0, n, arrived, 0)
    buf[slot, :, 2 * HD :] = jnp.ones((NV * BLK, HD), jnp.bfloat16)

    def fill(i, _):
        rows = pl.ds(pl.multiple_of(i * BLK, BLK), BLK)
        buf[slot, rows, :HD] = buf[slot, :BLK, :HD]
        buf[slot, rows, HD:] = jnp.zeros((BLK, 2 * HD), jnp.bfloat16)
        return 0

    lax.fori_loop(jnp.where(n > 0, n, NV), NV, fill, 0)
    below = 0
    for size in SIZES:

        @pl.when((n > below) & (n <= size))
        def _(size=size):
            keys = size * BLK
            for q_ref, o_ref, l_ref, out in ((q_own, oa, la, out_own), (q_oth, ob, lb, out_oth)):
                s = dot_t(q_ref[...], buf[slot, :keys, :HD])
                m = jnp.max(s, axis=1, keepdims=True)
                p = jnp.exp2((s - m) * LOG2).astype(jnp.bfloat16)
                acc = jnp.dot(p, buf[slot, :keys, HD:], preferred_element_type=jnp.float32)
                top = jnp.broadcast_to(m * LOG2, (FAR_ROWS, HD))
                o, l = o_ref[0], l_ref[0]
                both = jnp.maximum(l, top)
                wn = jnp.exp2(l - both)
                wf = jnp.exp2(top - both)
                out[...] = (
                    (o * wn + acc[:, :HD] * wf) / (wn + acc[:, HD:] * wf)
                ).astype(jnp.bfloat16)

        below = size

    @pl.when(n == 0)
    def _():
        out_own[...] = oa[0].astype(jnp.bfloat16)
        out_oth[...] = ob[0].astype(jnp.bfloat16)


def far_attention(part, scalars, queries, q_oth, o, l, pieces):
    q_spec = pl.BlockSpec((FAR_ROWS, HD), lambda h, sc: (part, sc[0] * GRP + h))
    own = pl.BlockSpec((1, FAR_ROWS, HD), lambda h, sc: (h, part, 0))
    oth = pl.BlockSpec((1, FAR_ROWS, HD), lambda h, sc: (h, 2 + part, 0))
    flat = pl.BlockSpec((FAR_ROWS, HD), lambda h, sc: (0, h))
    return pl.pallas_call(
        far_kernel,
        grid_spec=pltpu.PrefetchScalarGridSpec(
            num_scalar_prefetch=1,
            grid=(GRP,),
            in_specs=[
                q_spec,
                q_spec,
                own,
                own,
                oth,
                oth,
                *[pl.BlockSpec(memory_space=pl.ANY)] * PIECES,
            ],
            out_specs=[flat, flat],
            scratch_shapes=[
                pltpu.VMEM((2, NV * BLK, 3 * HD), jnp.bfloat16),
                pltpu.SemaphoreType.DMA((2,)),
            ],
        ),
        out_shape=[jax.ShapeDtypeStruct((FAR_ROWS, GW), jnp.bfloat16)] * 2,
        compiler_params=pltpu.CompilerParams(vmem_limit_bytes=48 << 20),
        name="far_attention",
    )(scalars, queries, q_oth, o, l, o, l, *pieces)


def shards(queries, keys, values, columns, offsets, out_weight):
    me = lax.axis_index("ctx")
    core = me % 2
    half = lax.axis_index("kvh")
    i32 = jnp.int32

    def cut(value, which, width, axis=1):
        return lax.dynamic_slice_in_dim(value, which * width, width, axis)

    own_slots, oth_slots, kv_own, kv_sent = pack(
        jnp.stack([core, me]).astype(i32), columns, keys, values
    )
    pool_a = own_slots
    pool_b = permute(oth_slots, send_core)
    pool_a = jnp.concatenate([pool_a, permute(pool_a, send_y)], axis=0)
    pool_b = jnp.concatenate([pool_b, permute(pool_b, send_y)], axis=0)
    ring_a = ring(jnp.concatenate(ring(pool_a, send_z), axis=0), send_x)
    ring_b = ring(jnp.concatenate(ring(pool_b, send_x), axis=0), send_z)

    near_scalars, far_scalars = tables(me[None].astype(i32), columns)
    kv_oth = permute(kv_sent, send_core)
    q_oth = permute(queries, send_core)
    chips = range(31)
    kv_low = lax.ppermute(kv_sent, "ctx", [(2 * i + 1, 2 * i + 2) for i in chips])
    kv_high = lax.ppermute(kv_own, "ctx", [(2 * i + 1, 2 * i + 3) for i in chips])
    o, l = near_attention(
        near_scalars, queries, q_oth, (kv_own, kv_oth, kv_low, kv_high), offsets
    )

    columns_out = out_weight.shape[1] // 2
    weight_kept = cut(out_weight, half, columns_out)
    weight_sent = cut(out_weight, 1 - half, columns_out)
    results = []
    previous = None
    for part in range(2):
        scalars = far_scalars
        if previous is not None:
            scalars, previous = lax.optimization_barrier((scalars, previous))
        own, oth = far_attention(part, scalars, queries, q_oth, o, l, ring_a + ring_b)
        got_all = permute(oth, send_core)
        for chunk in range(2):
            rows = slice(chunk * BLK, (chunk + 1) * BLK)
            got = got_all[rows]
            attended = jnp.where(
                core == 0,
                jnp.concatenate([own[rows], got], 1),
                jnp.concatenate([got, own[rows]], 1),
            )
            sent = jnp.dot(attended, weight_sent, preferred_element_type=jnp.float32)
            sent = sent.astype(jnp.bfloat16)
            previous = sent
            taken = permute(sent, lambda i: 1 - i, "kvh")
            kept = jnp.dot(attended, weight_kept, preferred_element_type=jnp.float32)
            results.append((kept + taken.astype(jnp.float32)).astype(jnp.bfloat16))
    return jnp.concatenate(results, axis=0)


def solution(mesh):
    placed = (
        P("ctx", "kvh"),
        P("ctx", "kvh"),
        P("ctx", "kvh"),
        P("kvh", None),
        P("kvh", None),
        P("kvh", None),
    )
    return jax.shard_map(
        shards, mesh=mesh, in_specs=placed, out_specs=P("ctx", "kvh"), check_vma=False
    )
```

```python
import functools
import math

import jax
import jax.numpy as jnp
from jax import lax
from jax.experimental import pallas as pl
from jax.experimental.pallas import tpu as pltpu
from jax.sharding import PartitionSpec as P

HD = 128
BLK = 128
NV = 16
CAP = 2
WIN = 512
TOK = 512
GRP = 7
GW = GRP * HD
WINB = WIN // BLK
NEG = -1e30
LOG2 = math.log2(math.e) / math.sqrt(HD)


def coords(i):
    return i // 16, i // 4 % 4, i // 2 % 2, i % 2


def index(x, z, y, c):
    return (x % 4) * 16 + (z % 4) * 4 + (y % 2) * 2 + c % 2


def send_x(by):
    def to(i):
        x, z, y, c = coords(i)
        return index(x + by, z, y, c)

    return to


def send_z(by):
    def to(i):
        x, z, y, c = coords(i)
        return index(x, z + by, y, c)

    return to


def send_y(i):
    x, z, y, c = coords(i)
    return index(x, z, y + 1, c)


def send_core(i):
    return i ^ 1


def permute(value, to, axis="ctx"):
    return lax.ppermute(value, axis, [(i, to(i)) for i in range(lax.axis_size(axis))])


def ring(piece, send):
    return [piece] + [permute(piece, send(by)) for by in (1, -1, 2)]


def ring_halves(piece, send):
    middle = piece.shape[0] // 2
    low = permute(piece, send(1))
    high = permute(piece, send(-1))
    return [
        piece,
        low,
        high,
        permute(low[:middle], send(1)),
        permute(high[middle:], send(-1)),
    ]


def dot_t(a, b):
    return lax.dot_general(a, b, (((1,), (1,)), ((), ())), preferred_element_type=jnp.float32)


TILE = 2 * BLK
SPAN = WIN + TILE
NEAR_FLAGS = 2
NEAR_EXTRA = NEAR_FLAGS + 8 * GRP
NEAR_SIZE = NEAR_EXTRA + 4 * GRP
PIECES = 10
FAR_OFF = 1 + GRP
FAR_CODE = FAR_OFF + GRP * (PIECES + 1)
FAR_SIZE = FAR_CODE + GRP * NV


def table_kernel(sc, lists, near, far, marks, codes, heads):
    me = sc[0]
    core, chip = me & 1, me >> 1
    x, z, y = chip >> 3, (chip >> 1) & 3, chip & 1
    start = chip * 8
    near[0] = core
    near[1] = (chip == 0).astype(jnp.int32)
    far[0] = core

    def clear(i, _):
        for k in range(4):
            marks[4 * i + k] = 0
        return 0

    lax.fori_loop(0, 64, clear, 0)

    def clear_near(i, _):
        for k in range(8):
            near[NEAR_FLAGS + 8 * i + k] = 0
        for k in range(4):
            near[NEAR_EXTRA + 4 * i + k] = 99
        return 0

    lax.fori_loop(0, GRP, clear_near, 0)

    def mark(h, _):
        for j in range(NV):
            marks[lists[core * GRP + h, j]] = 1
        return 0

    lax.fori_loop(0, GRP, mark, 0)

    def place(step):
        return jnp.where(step == 0, 0, jnp.where(step == 3, 1, step + 1))

    def one_head(h, _):
        for k in range(PIECES):
            heads[k] = 0

        def classify(j, _):
            b = lists[core * GRP + h, j]
            run = b >> 2
            at = b & 3
            base = b - at
            slot = jnp.where(at > 0, marks[base], 0)
            slot = slot + jnp.where(at > 1, marks[base + 1], 0)
            slot = slot + jnp.where(at > 2, marks[base + 2], 0)
            cx = place(((run >> 4) - x) & 3)
            cz = place(((run >> 2) - z) & 3)
            same = (run & 1) == core
            ring = jnp.where(same, cx, cz)
            low = jnp.where(((run >> 1) & 1) == y, 0, 2) + jnp.minimum(slot, 1)
            within = jnp.where(same, cz, cx) * 4 + low
            upper = (ring == 3) & (within > 7)
            piece = jnp.where(same, 0, 5) + ring + upper.astype(jnp.int32)
            within = within - jnp.where(upper, 8, 0)
            far_block = b <= start - 5
            codes[j] = jnp.where(far_block, piece * 16 + within, -1)
            heads[piece] = heads[piece] + far_block.astype(jnp.int32)
            w = b - (start - WINB)

            @pl.when((w >= 0) & (w < 8))
            def _():
                near[NEAR_FLAGS + h * 8 + w] = 1
                pair = NEAR_EXTRA + h * 4 + (w >> 2) * 2
                second = (near[pair] < 99).astype(jnp.int32)
                near[pair + second] = w

            return 0

        lax.fori_loop(0, NV, classify, 0)
        total = jnp.int32(0)
        for k in range(PIECES):
            far[FAR_OFF + h * (PIECES + 1) + k] = total
            held = heads[k]
            heads[k] = total
            total = total + held
        far[FAR_OFF + h * (PIECES + 1) + PIECES] = total
        far[1 + h] = total

        def store(j, _):
            code = codes[j]

            @pl.when(code >= 0)
            def _():
                k = code >> 4
                far[FAR_CODE + h * NV + heads[k]] = code & 15
                heads[k] = heads[k] + 1

            return 0

        lax.fori_loop(0, NV, store, 0)
        return 0

    lax.fori_loop(0, GRP, one_head, 0)


def tables(me, columns):
    smem = pltpu.MemorySpace.SMEM
    return pl.pallas_call(
        table_kernel,
        in_specs=[pl.BlockSpec(memory_space=smem)] * 2,
        out_specs=[pl.BlockSpec(memory_space=smem)] * 2,
        out_shape=[
            jax.ShapeDtypeStruct((NEAR_SIZE,), jnp.int32),
            jax.ShapeDtypeStruct((FAR_SIZE,), jnp.int32),
        ],
        scratch_shapes=[
            pltpu.SMEM((256,), jnp.int32),
            pltpu.SMEM((NV,), jnp.int32),
            pltpu.SMEM((PIECES,), jnp.int32),
        ],
        name="index_tables",
    )(me, columns)


def near_kernel(
    sc, q_own, q_oth, kv_own, kv_oth, kv_before, offs, o_ref, l_ref, kext, vext, acc_s, m_s
):
    h = pl.program_id(0)
    core = sc[0]

    @pl.when(h == 0)
    def _():
        own_at = pl.ds(pl.multiple_of(TOK + core * TOK, TOK), TOK)
        oth_at = pl.ds(pl.multiple_of(2 * TOK - core * TOK, TOK), TOK)
        for at, part in ((own_at, kv_own), (oth_at, kv_oth)):
            kext[at, :] = part[:, :HD]
            vext[at, :HD] = part[:, HD:]

        kext[:TOK, :] = kv_before[:, :HD]
        vext[:TOK, :HD] = kv_before[:, HD:]
        vext[:, HD:] = jnp.ones((vext.shape[0], HD), jnp.bfloat16)

    line = offs[pl.ds(core * GRP + h, 1), :]
    spread = jnp.broadcast_to(line.astype(jnp.float32), (BLK, BLK)).T
    lane = lax.broadcasted_iota(jnp.int32, (BLK, BLK), 1)
    marks = []
    for k in range(SPAN // BLK):
        hit = spread == (WIN - k * BLK - lane).astype(jnp.float32)
        marks.append(jnp.max(jnp.where(hit, 0.0, NEG), axis=0, keepdims=True))
    pattern = jnp.concatenate(marks, axis=1)
    bias = pltpu.roll(
        jnp.broadcast_to(pattern, (TILE, SPAN)), 0, 1, stride=1, stride_axis=0
    )
    rows = lax.broadcasted_iota(jnp.int32, (TILE, TILE), 0)
    lanes = lax.broadcasted_iota(jnp.int32, (TILE, TILE), 1)
    far_side = lanes <= rows
    tile_lane = lax.broadcasted_iota(jnp.int32, (1, TILE), 1)
    span_lane = lax.broadcasted_iota(jnp.int32, (1, SPAN), 1)

    def tile_of(i):
        return 4 * (core if i < 2 else 1 - core) + 2 * (i % 2)

    def q_of(i):
        return (q_own if i < 2 else q_oth)[(i % 2) * TILE : (i % 2 + 1) * TILE, :]

    for i in range(4):
        t = tile_of(i)
        base = pl.multiple_of(t * BLK, BLK)
        s = dot_t(q_of(i), kext[pl.ds(base, SPAN), :])
        flag = NEAR_FLAGS + h * 8 + t
        la = jnp.where(sc[flag] > 0, 0.0, NEG).astype(jnp.float32)
        lb = jnp.where(sc[flag + 1] > 0, 0.0, NEG).astype(jnp.float32)
        first = jnp.where(far_side, jnp.where(tile_lane < BLK, la, lb), bias[:, :TILE])
        absent = jnp.where(sc[1] > 0, BLK * (WINB - t), 0)
        edge = jnp.where(span_lane < absent, NEG, 0.0).astype(jnp.float32)
        s = s + jnp.concatenate([first, bias[:, TILE:]], axis=1) + edge
        m = jnp.max(s, axis=1, keepdims=True)
        p = jnp.exp2((s - m) * LOG2).astype(jnp.bfloat16)
        acc_s[i] = jnp.dot(p, vext[pl.ds(base, SPAN), :], preferred_element_type=jnp.float32)
        m_s[i] = jnp.broadcast_to(m, (TILE, HD))

    ex = NEAR_EXTRA + 4 * h
    lowest = jnp.minimum(jnp.minimum(sc[ex], sc[ex + 1]), jnp.minimum(sc[ex + 2], sc[ex + 3]))

    @pl.when(lowest < 6)
    def _():
        for i in range(4):
            t = tile_of(i)
            for g in range(2):
                wa, wb = sc[ex + 2 * g], sc[ex + 2 * g + 1]

                @pl.when((wa < t) | (wb < t))
                def _():
                    ra = pl.multiple_of(jnp.minimum(wa, 11) * BLK, BLK)
                    rb = pl.multiple_of(jnp.minimum(wb, 11) * BLK, BLK)
                    ks = jnp.concatenate([kext[pl.ds(ra, BLK), :], kext[pl.ds(rb, BLK), :]], 0)
                    vs = jnp.concatenate([vext[pl.ds(ra, BLK), :], vext[pl.ds(rb, BLK), :]], 0)
                    s = dot_t(q_of(i), ks)
                    ba = jnp.where(wa < t, 0.0, NEG).astype(jnp.float32)
                    bb = jnp.where(wb < t, 0.0, NEG).astype(jnp.float32)
                    s = s + jnp.where(tile_lane < BLK, ba, bb)
                    m_old = m_s[i]
                    m_new = jnp.maximum(m_old, jnp.max(s, axis=1, keepdims=True))
                    scale = jnp.exp2((m_old - m_new) * LOG2)
                    p = jnp.exp2((s - jnp.concatenate([m_new, m_new], 1)) * LOG2)
                    acc_s[i] = acc_s[i] * jnp.concatenate([scale, scale], 1) + jnp.dot(
                        p.astype(jnp.bfloat16), vs, preferred_element_type=jnp.float32
                    )
                    m_s[i] = m_new

    for i in range(4):
        total = acc_s[i, :, HD:]
        o_ref[0, i * TILE : (i + 1) * TILE, :] = acc_s[i, :, :HD] / total
        l_ref[0, i * TILE : (i + 1) * TILE, :] = m_s[i] * LOG2 + jnp.log2(total)


def near_attention(scalars, queries, q_oth, parts, offsets):
    rows = 2 * TOK
    state = jax.ShapeDtypeStruct((GRP, rows, HD), jnp.float32)
    q_spec = pl.BlockSpec((TOK, HD), lambda h, sc: (0, sc[0] * GRP + h))
    return pl.pallas_call(
        near_kernel,
        grid_spec=pltpu.PrefetchScalarGridSpec(
            num_scalar_prefetch=1,
            grid=(GRP,),
            in_specs=[
                q_spec,
                q_spec,
                *[pl.BlockSpec((TOK, 2 * HD), lambda h, sc: (0, 0))] * 3,
                pl.BlockSpec(offsets.shape, lambda h, sc: (0, 0)),
            ],
            out_specs=[
                pl.BlockSpec((1, rows, HD), lambda h, sc: (h, 0, 0)),
                pl.BlockSpec((1, rows, HD), lambda h, sc: (h, 0, 0)),
            ],
            scratch_shapes=[
                pltpu.VMEM((3 * TOK, HD), jnp.bfloat16),
                pltpu.VMEM((3 * TOK, 2 * HD), jnp.bfloat16),
                pltpu.VMEM((4, TILE, 2 * HD), jnp.float32),
                pltpu.VMEM((4, TILE, HD), jnp.float32),
            ],
        ),
        out_shape=[state, state],
        compiler_params=pltpu.CompilerParams(vmem_limit_bytes=40 << 20),
        name="near_attention",
    )(scalars, queries, q_oth, *parts, offsets)


def pack_kernel(sc, lists, keys, values, own_slots, kv_own, sent):
    core, me = sc[0], sc[1]
    group = lax.broadcasted_iota(jnp.int32, lists.shape, 0) // GRP
    table = lists[...]

    def head_of(source, head, rows):
        low, high = source[rows, :HD], source[rows, HD:]
        return jnp.where(head == 0, low, high)

    for head, slots in ((core, own_slots), (1 - core, sent)):
        pick = [jnp.int32(0)] * CAP
        seen = jnp.int32(0)
        for b in range(TOK // BLK):
            hit = jnp.max(jnp.where((group == head) & (table == me * (TOK // BLK) + b), 1, 0))
            for k in range(CAP):
                pick[k] = jnp.where((hit > 0) & (seen == k), b, pick[k])
            seen = seen + hit
        for k in range(CAP):
            rows = pl.ds(pl.multiple_of(pick[k] * BLK, BLK), BLK)
            slots[k * BLK : (k + 1) * BLK, :HD] = head_of(keys, head, rows)
            slots[k * BLK : (k + 1) * BLK, HD:] = head_of(values, head, rows)
    whole = slice(0, TOK)
    for head, target, at in ((core, kv_own, 0), (1 - core, sent, CAP * BLK)):
        target[at : at + TOK, :HD] = head_of(keys, head, whole)
        target[at : at + TOK, HD:] = head_of(values, head, whole)


def pack(scalars, columns, keys, values):
    slots = jax.ShapeDtypeStruct((CAP * BLK, 2 * HD), jnp.bfloat16)
    whole = jax.ShapeDtypeStruct((TOK, 2 * HD), jnp.bfloat16)
    sent = jax.ShapeDtypeStruct((CAP * BLK + TOK, 2 * HD), jnp.bfloat16)

    def full(shape):
        return pl.BlockSpec(shape, lambda i, sc: (0, 0))

    return pl.pallas_call(
        pack_kernel,
        grid_spec=pltpu.PrefetchScalarGridSpec(
            num_scalar_prefetch=1,
            grid=(1,),
            in_specs=[full(columns.shape), full(keys.shape), full(values.shape)],
            out_specs=[full(a.shape) for a in (slots, whole, sent)],
        ),
        out_shape=[slots, whole, sent],
        name="pack_blocks",
    )(scalars, columns, keys, values)


SIZES = (8, 16)


def far_kernel(sc, q_own, q_oth, o_ref, l_ref, *rest):
    pieces, (out_own, out_oth, buf, sem) = rest[:PIECES], rest[PIECES:]
    h = pl.program_id(0)

    def fetch(head, slot):
        for k in range(PIECES):
            at = FAR_OFF + head * (PIECES + 1) + k

            def start(i, _, k=k):
                code = sc[FAR_CODE + head * NV + i]
                pltpu.make_async_copy(
                    pieces[k].at[pl.ds(pl.multiple_of(code * BLK, BLK), BLK), :],
                    buf.at[slot, pl.ds(pl.multiple_of(i * BLK, BLK), BLK), pl.ds(0, 2 * HD)],
                    sem.at[slot],
                ).start()
                return 0

            lax.fori_loop(sc[at], sc[at + 1], start, 0)

    slot = h % 2

    @pl.when(h == 0)
    def _():
        fetch(0, 0)

    @pl.when(h + 1 < GRP)
    def _():
        fetch(h + 1, 1 - slot)

    n = sc[1 + h]

    def arrived(i, _):
        pltpu.make_async_copy(
            pieces[0].at[pl.ds(0, BLK), :],
            buf.at[slot, pl.ds(0, BLK), pl.ds(0, 2 * HD)],
            sem.at[slot],
        ).wait()
        return 0

    lax.fori_loop(0, n, arrived, 0)
    buf[slot, :, 2 * HD :] = jnp.ones((NV * BLK, HD), jnp.bfloat16)

    def fill(i, _):
        rows = pl.ds(pl.multiple_of(i * BLK, BLK), BLK)
        buf[slot, rows, :HD] = buf[slot, :BLK, :HD]
        buf[slot, rows, HD:] = jnp.zeros((BLK, 2 * HD), jnp.bfloat16)
        return 0

    lax.fori_loop(jnp.where(n > 0, n, NV), NV, fill, 0)
    below = 0
    for size in SIZES:

        @pl.when((n > below) & (n <= size))
        def _(size=size):
            keys = size * BLK
            for i in range(4):
                q_ref, out = ((q_own, out_own), (q_oth, out_oth))[i // 2]
                rows = slice((i % 2) * TILE, (i % 2 + 1) * TILE)
                state = slice(i * TILE, (i + 1) * TILE)
                s = dot_t(q_ref[rows, :], buf[slot, :keys, :HD])
                m = jnp.max(s, axis=1, keepdims=True)
                p = jnp.exp2((s - m) * LOG2).astype(jnp.bfloat16)
                acc = jnp.dot(p, buf[slot, :keys, HD:], preferred_element_type=jnp.float32)
                top = jnp.broadcast_to(m * LOG2, (TILE, HD))
                o, l = o_ref[0, state, :], l_ref[0, state, :]
                both = jnp.maximum(l, top)
                wn = jnp.exp2(l - both)
                wf = jnp.exp2(top - both)
                out[rows, :] = (
                    (o * wn + acc[:, :HD] * wf) / (wn + acc[:, HD:] * wf)
                ).astype(jnp.bfloat16)

        below = size

    @pl.when(n == 0)
    def _():
        out_own[...] = o_ref[0, :TOK, :].astype(jnp.bfloat16)
        out_oth[...] = o_ref[0, TOK:, :].astype(jnp.bfloat16)


def far_attention(scalars, queries, q_oth, o, l, pieces):
    q_spec = pl.BlockSpec((TOK, HD), lambda h, sc: (0, sc[0] * GRP + h))
    state = pl.BlockSpec((1, 2 * TOK, HD), lambda h, sc: (h, 0, 0))
    flat = pl.BlockSpec((TOK, HD), lambda h, sc: (0, h))
    return pl.pallas_call(
        far_kernel,
        grid_spec=pltpu.PrefetchScalarGridSpec(
            num_scalar_prefetch=1,
            grid=(GRP,),
            in_specs=[
                q_spec,
                q_spec,
                state,
                state,
                *[pl.BlockSpec(memory_space=pl.ANY)] * PIECES,
            ],
            out_specs=[flat, flat],
            scratch_shapes=[
                pltpu.VMEM((2, NV * BLK, 3 * HD), jnp.bfloat16),
                pltpu.SemaphoreType.DMA((2,)),
            ],
        ),
        out_shape=[jax.ShapeDtypeStruct((TOK, GW), jnp.bfloat16)] * 2,
        compiler_params=pltpu.CompilerParams(vmem_limit_bytes=48 << 20),
        name="far_attention",
    )(scalars, queries, q_oth, o, l, *pieces)


def shards(queries, keys, values, columns, offsets, out_weight):
    me = lax.axis_index("ctx")
    core = me % 2
    half = lax.axis_index("kvh")
    i32 = jnp.int32

    def cut(value, which, width, axis=1):
        return lax.dynamic_slice_in_dim(value, which * width, width, axis)

    own_slots, kv_own, sent = pack(jnp.stack([core, me]).astype(i32), columns, keys, values)
    got = permute(sent, send_core)
    q_oth = permute(queries, send_core)
    slots = CAP * BLK
    kv_oth = got[slots:]
    both = jnp.concatenate([own_slots, got[:slots]], axis=0)
    far_y = permute(both, send_y)
    held = jnp.where(core == 1, kv_own, kv_oth)
    kv_before = lax.ppermute(held, "ctx", [(i, i + 2) for i in range(62)])
    pool_a = jnp.concatenate([both[:slots], far_y[:slots]], axis=0)
    pool_b = jnp.concatenate([both[slots:], far_y[slots:]], axis=0)
    pool_a, pool_b, kv_before, q_oth, columns = lax.optimization_barrier(
        (pool_a, pool_b, kv_before, q_oth, columns)
    )
    near_scalars, far_scalars = tables(me[None].astype(i32), columns)
    pool_a = jnp.concatenate(ring(pool_a, send_z), axis=0)
    pool_b = jnp.concatenate(ring(pool_b, send_x), axis=0)
    pool_a, pool_b, near_scalars = lax.optimization_barrier((pool_a, pool_b, near_scalars))
    pieces = ring_halves(pool_a, send_x) + ring_halves(pool_b, send_z)
    o, l = near_attention(near_scalars, queries, q_oth, (kv_own, kv_oth, kv_before), offsets)
    own, oth = far_attention(far_scalars, queries, q_oth, o, l, pieces)

    columns_out = out_weight.shape[1] // 2
    weight_kept = cut(out_weight, half, columns_out)
    weight_sent = cut(out_weight, 1 - half, columns_out)
    results = []
    parts = [slice(0, BLK), slice(BLK, TOK)]
    first, others = [permute(oth[rows], send_core) for rows in parts]
    for at in range(0, TOK, BLK):
        rows = slice(at, at + BLK)
        got = first if at == 0 else others[at - BLK : at]
        attended = jnp.where(
            core == 0,
            jnp.concatenate([own[rows], got], 1),
            jnp.concatenate([got, own[rows]], 1),
        )
        sent = jnp.dot(attended, weight_sent, preferred_element_type=jnp.float32)
        taken = permute(sent.astype(jnp.bfloat16), lambda i: 1 - i, "kvh")
        kept = jnp.dot(attended, weight_kept, preferred_element_type=jnp.float32)
        results.append((kept + taken.astype(jnp.float32)).astype(jnp.bfloat16))
    return jnp.concatenate(results, axis=0)


def solution(mesh):
    placed = (
        P("ctx", "kvh"),
        P("ctx", "kvh"),
        P("ctx", "kvh"),
        P("kvh", None),
        P("kvh", None),
        P("kvh", None),
    )
    return jax.shard_map(
        shards, mesh=mesh, in_specs=placed, out_specs=P("ctx", "kvh"), check_vma=False
    )
```

```python
import functools
import math

import jax
import jax.numpy as jnp
from jax import lax
from jax.experimental import pallas as pl
from jax.experimental.pallas import tpu as pltpu
from jax.sharding import PartitionSpec as P

HD = 128
BLK = 128
NV = 16
CAP = 2
WIN = 512
TOK = 512
GRP = 7
GW = GRP * HD
WINB = WIN // BLK
NEG = -1e30
LOG2 = math.log2(math.e) / math.sqrt(HD)


def coords(i):
    return i // 16, i // 4 % 4, i // 2 % 2, i % 2


def index(x, z, y, c):
    return (x % 4) * 16 + (z % 4) * 4 + (y % 2) * 2 + c % 2


def send_x(by):
    def to(i):
        x, z, y, c = coords(i)
        return index(x + by, z, y, c)

    return to


def send_z(by):
    def to(i):
        x, z, y, c = coords(i)
        return index(x, z + by, y, c)

    return to


def send_y(i):
    x, z, y, c = coords(i)
    return index(x, z, y + 1, c)


def send_core(i):
    return i ^ 1


def permute(value, to, axis="ctx"):
    return lax.ppermute(value, axis, [(i, to(i)) for i in range(lax.axis_size(axis))])


def ring(piece, send):
    return [piece] + [permute(piece, send(by)) for by in (1, -1, 2)]


def to_rows(value):
    return [value[k * BLK : (k + 1) * BLK, :].T[0:1, :] for k in range(2)]


def from_rows(ref, i):
    return jnp.concatenate(
        [jnp.broadcast_to(ref[0, 2 * i + k : 2 * i + k + 1, :], (BLK, BLK)).T for k in range(2)], 0
    )


def dot_t(a, b):
    return lax.dot_general(a, b, (((1,), (1,)), ((), ())), preferred_element_type=jnp.float32)


TILE = 2 * BLK
SPAN = WIN + TILE
NEAR_FLAGS = 2
NEAR_EXTRA = NEAR_FLAGS + 8 * GRP
NEAR_SIZE = NEAR_EXTRA + 4 * GRP
PIECES = 10
FAR_OFF = 1 + GRP
FAR_CODE = FAR_OFF + GRP * (PIECES + 1)
FAR_SIZE = FAR_CODE + GRP * NV


def table_kernel(sc, lists, near, far, marks, codes, heads):
    me = sc[0]
    core, chip = me & 1, me >> 1
    x, z, y = chip >> 3, (chip >> 1) & 3, chip & 1
    start = chip * 8
    near[0] = core
    near[1] = (chip == 0).astype(jnp.int32)
    far[0] = core

    def clear(i, _):
        for k in range(4):
            marks[4 * i + k] = 0
        return 0

    lax.fori_loop(0, 64, clear, 0)

    def clear_near(i, _):
        for k in range(8):
            near[NEAR_FLAGS + 8 * i + k] = 0
        for k in range(4):
            near[NEAR_EXTRA + 4 * i + k] = 99
        return 0

    lax.fori_loop(0, GRP, clear_near, 0)

    def mark(h, _):
        for j in range(NV):
            marks[lists[core * GRP + h, j]] = 1
        return 0

    lax.fori_loop(0, GRP, mark, 0)

    def place(step):
        return jnp.where(step == 0, 0, jnp.where(step == 3, 1, step + 1))

    def one_head(h, _):
        for k in range(PIECES):
            heads[k] = 0

        def classify(j, _):
            b = lists[core * GRP + h, j]
            run = b >> 2
            at = b & 3
            base = b - at
            slot = jnp.where(at > 0, marks[base], 0)
            slot = slot + jnp.where(at > 1, marks[base + 1], 0)
            slot = slot + jnp.where(at > 2, marks[base + 2], 0)
            cx = place(((run >> 4) - x) & 3)
            cz = place(((run >> 2) - z) & 3)
            same = (run & 1) == core
            ring = jnp.where(same, cx, cz)
            low = jnp.where(((run >> 1) & 1) == y, 0, 2) + jnp.minimum(slot, 1)
            within = jnp.where(same, cz, cx) * 4 + low
            upper = (ring == 3) & (within > 7)
            piece = jnp.where(
                ring == 3,
                jnp.where(same, 6, 8) + upper.astype(jnp.int32),
                jnp.where(same, 0, 3) + ring,
            )
            within = within - jnp.where(upper, 8, 0)
            far_block = b <= start - 5
            codes[j] = jnp.where(far_block, piece * 16 + within, -1)
            heads[piece] = heads[piece] + far_block.astype(jnp.int32)
            w = b - (start - WINB)

            @pl.when((w >= 0) & (w < 8))
            def _():
                near[NEAR_FLAGS + h * 8 + w] = 1
                pair = NEAR_EXTRA + h * 4 + (w >> 2) * 2
                second = (near[pair] < 99).astype(jnp.int32)
                near[pair + second] = w

            return 0

        lax.fori_loop(0, NV, classify, 0)
        total = jnp.int32(0)
        for k in range(PIECES):
            far[FAR_OFF + h * (PIECES + 1) + k] = total
            held = heads[k]
            heads[k] = total
            total = total + held
        far[FAR_OFF + h * (PIECES + 1) + PIECES] = total
        far[1 + h] = total

        def store(j, _):
            code = codes[j]

            @pl.when(code >= 0)
            def _():
                k = code >> 4
                far[FAR_CODE + h * NV + heads[k]] = code & 15
                heads[k] = heads[k] + 1

            return 0

        lax.fori_loop(0, NV, store, 0)
        return 0

    lax.fori_loop(0, GRP, one_head, 0)


def tables(me, columns):
    smem = pltpu.MemorySpace.SMEM
    return pl.pallas_call(
        table_kernel,
        in_specs=[pl.BlockSpec(memory_space=smem)] * 2,
        out_specs=[pl.BlockSpec(memory_space=smem)] * 2,
        out_shape=[
            jax.ShapeDtypeStruct((NEAR_SIZE,), jnp.int32),
            jax.ShapeDtypeStruct((FAR_SIZE,), jnp.int32),
        ],
        scratch_shapes=[
            pltpu.SMEM((256,), jnp.int32),
            pltpu.SMEM((NV,), jnp.int32),
            pltpu.SMEM((PIECES,), jnp.int32),
        ],
        name="index_tables",
    )(me, columns)


def near_kernel(
    sc, q_own, q_oth, kv_own, kv_oth, kv_before, offs, o_ref, l_ref, kext, vext, acc_s, m_s
):
    h = pl.program_id(0)
    core = sc[0]

    @pl.when(h == 0)
    def _():
        own_at = pl.ds(pl.multiple_of(TOK + core * TOK, TOK), TOK)
        oth_at = pl.ds(pl.multiple_of(2 * TOK - core * TOK, TOK), TOK)
        for at, part in ((own_at, kv_own), (oth_at, kv_oth)):
            kext[at, :] = part[:, :HD]
            vext[at, :HD] = part[:, HD:]

        kext[:TOK, :] = kv_before[:, :HD]
        vext[:TOK, :HD] = kv_before[:, HD:]
        vext[:, HD:] = jnp.ones((vext.shape[0], HD), jnp.bfloat16)

    line = offs[pl.ds(core * GRP + h, 1), :]
    spread = jnp.broadcast_to(line.astype(jnp.float32), (BLK, BLK)).T
    lane = lax.broadcasted_iota(jnp.int32, (BLK, BLK), 1)
    marks = []
    for k in range(SPAN // BLK):
        hit = spread == (WIN - k * BLK - lane).astype(jnp.float32)
        marks.append(jnp.max(jnp.where(hit, 0.0, NEG), axis=0, keepdims=True))
    pattern = jnp.concatenate(marks, axis=1)
    bias = pltpu.roll(
        jnp.broadcast_to(pattern, (TILE, SPAN)), 0, 1, stride=1, stride_axis=0
    )
    rows = lax.broadcasted_iota(jnp.int32, (TILE, TILE), 0)
    lanes = lax.broadcasted_iota(jnp.int32, (TILE, TILE), 1)
    far_side = lanes <= rows
    tile_lane = lax.broadcasted_iota(jnp.int32, (1, TILE), 1)
    span_lane = lax.broadcasted_iota(jnp.int32, (1, SPAN), 1)

    def tile_of(i):
        return 4 * (core if i < 2 else 1 - core) + 2 * (i % 2)

    def q_of(i):
        return (q_own if i < 2 else q_oth)[(i % 2) * TILE : (i % 2 + 1) * TILE, :]

    for i in range(4):
        t = tile_of(i)
        base = pl.multiple_of(t * BLK, BLK)
        s = dot_t(q_of(i), kext[pl.ds(base, SPAN), :])
        flag = NEAR_FLAGS + h * 8 + t
        la = jnp.where(sc[flag] > 0, 0.0, NEG).astype(jnp.float32)
        lb = jnp.where(sc[flag + 1] > 0, 0.0, NEG).astype(jnp.float32)
        first = jnp.where(far_side, jnp.where(tile_lane < BLK, la, lb), bias[:, :TILE])
        absent = jnp.where(sc[1] > 0, BLK * (WINB - t), 0)
        edge = jnp.where(span_lane < absent, NEG, 0.0).astype(jnp.float32)
        s = s + jnp.concatenate([first, bias[:, TILE:]], axis=1) + edge
        m = jnp.max(s, axis=1, keepdims=True)
        p = jnp.exp2((s - m) * LOG2).astype(jnp.bfloat16)
        acc_s[i] = jnp.dot(p, vext[pl.ds(base, SPAN), :], preferred_element_type=jnp.float32)
        m_s[i] = jnp.broadcast_to(m, (TILE, HD))

    ex = NEAR_EXTRA + 4 * h
    lowest = jnp.minimum(jnp.minimum(sc[ex], sc[ex + 1]), jnp.minimum(sc[ex + 2], sc[ex + 3]))

    @pl.when(lowest < 6)
    def _():
        for i in range(4):
            t = tile_of(i)
            for g in range(2):
                wa, wb = sc[ex + 2 * g], sc[ex + 2 * g + 1]

                @pl.when((wa < t) | (wb < t))
                def _():
                    ra = pl.multiple_of(jnp.minimum(wa, 11) * BLK, BLK)
                    rb = pl.multiple_of(jnp.minimum(wb, 11) * BLK, BLK)
                    ks = jnp.concatenate([kext[pl.ds(ra, BLK), :], kext[pl.ds(rb, BLK), :]], 0)
                    vs = jnp.concatenate([vext[pl.ds(ra, BLK), :], vext[pl.ds(rb, BLK), :]], 0)
                    s = dot_t(q_of(i), ks)
                    ba = jnp.where(wa < t, 0.0, NEG).astype(jnp.float32)
                    bb = jnp.where(wb < t, 0.0, NEG).astype(jnp.float32)
                    s = s + jnp.where(tile_lane < BLK, ba, bb)
                    m_old = m_s[i]
                    m_new = jnp.maximum(m_old, jnp.max(s, axis=1, keepdims=True))
                    scale = jnp.exp2((m_old - m_new) * LOG2)
                    p = jnp.exp2((s - jnp.concatenate([m_new, m_new], 1)) * LOG2)
                    acc_s[i] = acc_s[i] * jnp.concatenate([scale, scale], 1) + jnp.dot(
                        p.astype(jnp.bfloat16), vs, preferred_element_type=jnp.float32
                    )
                    m_s[i] = m_new

    for i in range(4):
        total = acc_s[i, :, HD:]
        o_ref[0, i * TILE : (i + 1) * TILE, :] = acc_s[i, :, :HD] / total
        for k, line in enumerate(to_rows(m_s[i] * LOG2 + jnp.log2(total))):
            l_ref[0, 2 * i + k : 2 * i + k + 1, :] = line


def near_attention(scalars, queries, q_oth, parts, offsets):
    rows = 2 * TOK
    state = jax.ShapeDtypeStruct((GRP, rows, HD), jnp.float32)
    sums = jax.ShapeDtypeStruct((GRP, 8, HD), jnp.float32)
    q_spec = pl.BlockSpec((TOK, HD), lambda h, sc: (0, sc[0] * GRP + h))
    return pl.pallas_call(
        near_kernel,
        grid_spec=pltpu.PrefetchScalarGridSpec(
            num_scalar_prefetch=1,
            grid=(GRP,),
            in_specs=[
                q_spec,
                q_spec,
                *[pl.BlockSpec((TOK, 2 * HD), lambda h, sc: (0, 0))] * 3,
                pl.BlockSpec(offsets.shape, lambda h, sc: (0, 0)),
            ],
            out_specs=[
                pl.BlockSpec((1, rows, HD), lambda h, sc: (h, 0, 0)),
                pl.BlockSpec((1, 8, HD), lambda h, sc: (h, 0, 0)),
            ],
            scratch_shapes=[
                pltpu.VMEM((3 * TOK, HD), jnp.bfloat16),
                pltpu.VMEM((3 * TOK, 2 * HD), jnp.bfloat16),
                pltpu.VMEM((4, TILE, 2 * HD), jnp.float32),
                pltpu.VMEM((4, TILE, HD), jnp.float32),
            ],
        ),
        out_shape=[state, sums],
        compiler_params=pltpu.CompilerParams(vmem_limit_bytes=40 << 20),
        name="near_attention",
    )(scalars, queries, q_oth, *parts, offsets)


def pack_kernel(sc, lists, keys, values, own_slots, kv_own, sent):
    core, me = sc[0], sc[1]
    group = lax.broadcasted_iota(jnp.int32, lists.shape, 0) // GRP
    table = lists[...]

    def head_of(source, head, rows):
        low, high = source[rows, :HD], source[rows, HD:]
        return jnp.where(head == 0, low, high)

    for head, slots in ((core, own_slots), (1 - core, sent)):
        pick = [jnp.int32(0)] * CAP
        seen = jnp.int32(0)
        for b in range(TOK // BLK):
            hit = jnp.max(jnp.where((group == head) & (table == me * (TOK // BLK) + b), 1, 0))
            for k in range(CAP):
                pick[k] = jnp.where((hit > 0) & (seen == k), b, pick[k])
            seen = seen + hit
        for k in range(CAP):
            rows = pl.ds(pl.multiple_of(pick[k] * BLK, BLK), BLK)
            slots[k * BLK : (k + 1) * BLK, :HD] = head_of(keys, head, rows)
            slots[k * BLK : (k + 1) * BLK, HD:] = head_of(values, head, rows)
    whole = slice(0, TOK)
    for head, target, at in ((core, kv_own, 0), (1 - core, sent, CAP * BLK)):
        target[at : at + TOK, :HD] = head_of(keys, head, whole)
        target[at : at + TOK, HD:] = head_of(values, head, whole)


def pack(scalars, columns, keys, values):
    slots = jax.ShapeDtypeStruct((CAP * BLK, 2 * HD), jnp.bfloat16)
    whole = jax.ShapeDtypeStruct((TOK, 2 * HD), jnp.bfloat16)
    sent = jax.ShapeDtypeStruct((CAP * BLK + TOK, 2 * HD), jnp.bfloat16)

    def full(shape):
        return pl.BlockSpec(shape, lambda i, sc: (0, 0))

    return pl.pallas_call(
        pack_kernel,
        grid_spec=pltpu.PrefetchScalarGridSpec(
            num_scalar_prefetch=1,
            grid=(1,),
            in_specs=[full(columns.shape), full(keys.shape), full(values.shape)],
            out_specs=[full(a.shape) for a in (slots, whole, sent)],
        ),
        out_shape=[slots, whole, sent],
        name="pack_blocks",
    )(scalars, columns, keys, values)


def far_kernel(low, high, sizes, last, sc, q_own, q_oth, o_ref, l_ref, *rest):
    pieces, (out_a, out_b, buf, sem) = rest[: high - low], rest[high - low :]
    h = pl.program_id(0)

    def bound(head, k):
        return sc[FAR_OFF + head * (PIECES + 1) + k]

    def fetch(head, slot):
        base = bound(head, low)
        for k in range(low, high):

            def start(i, _, k=k):
                code = sc[FAR_CODE + head * NV + i]
                pltpu.make_async_copy(
                    pieces[k - low].at[pl.ds(pl.multiple_of(code * BLK, BLK), BLK), :],
                    buf.at[
                        slot, pl.ds(pl.multiple_of((i - base) * BLK, BLK), BLK), pl.ds(0, 2 * HD)
                    ],
                    sem.at[slot],
                ).start()
                return 0

            lax.fori_loop(bound(head, k), bound(head, k + 1), start, 0)

    slot = h % 2

    @pl.when(h == 0)
    def _():
        fetch(0, 0)

    @pl.when(h + 1 < GRP)
    def _():
        fetch(h + 1, 1 - slot)

    n = bound(h, high) - bound(h, low)

    def arrived(i, _):
        pltpu.make_async_copy(
            pieces[0].at[pl.ds(0, BLK), :],
            buf.at[slot, pl.ds(0, BLK), pl.ds(0, 2 * HD)],
            sem.at[slot],
        ).wait()
        return 0

    lax.fori_loop(0, n, arrived, 0)
    buf[slot, :, 2 * HD :] = jnp.ones((NV * BLK, HD), jnp.bfloat16)

    def fill(i, _):
        rows = pl.ds(pl.multiple_of(i * BLK, BLK), BLK)
        buf[slot, rows, :HD] = buf[slot, :BLK, :HD]
        buf[slot, rows, HD:] = jnp.zeros((BLK, 2 * HD), jnp.bfloat16)
        return 0

    wanted = jnp.int32(0)
    for size in sizes[::-1]:
        wanted = jnp.where(n <= size, size, wanted)
    lax.fori_loop(jnp.where(n > 0, n, NV), wanted, fill, 0)

    def put(i, o):
        if last:
            out = (out_a, out_b)[i // 2]
            out[(i % 2) * TILE : (i % 2 + 1) * TILE, :] = o.astype(jnp.bfloat16)
        else:
            out_a[0, i * TILE : (i + 1) * TILE, :] = o

    below = 0
    for size in sizes:

        @pl.when((n > below) & (n <= size))
        def _(size=size):
            keys = size * BLK
            for i in range(4):
                q_ref = (q_own, q_oth)[i // 2]
                s = dot_t(q_ref[(i % 2) * TILE : (i % 2 + 1) * TILE, :], buf[slot, :keys, :HD])
                m = jnp.max(s, axis=1, keepdims=True)
                p = jnp.exp2((s - m) * LOG2).astype(jnp.bfloat16)
                acc = jnp.dot(p, buf[slot, :keys, HD:], preferred_element_type=jnp.float32)
                top = jnp.broadcast_to(m * LOG2, (TILE, HD))
                o, l = o_ref[0, i * TILE : (i + 1) * TILE, :], from_rows(l_ref, i)
                both = jnp.maximum(l, top)
                wn = jnp.exp2(l - both)
                wf = jnp.exp2(top - both)
                weight = wn + acc[:, HD:] * wf
                put(i, (o * wn + acc[:, :HD] * wf) / weight)
                if not last:
                    for k, line in enumerate(to_rows(both + jnp.log2(weight))):
                        out_b[0, 2 * i + k : 2 * i + k + 1, :] = line

        below = size

    @pl.when(n == 0)
    def _():
        for i in range(4):
            put(i, o_ref[0, i * TILE : (i + 1) * TILE, :])
        if not last:
            out_b[...] = l_ref[...]


def far_attention(low, high, sizes, last, scalars, queries, q_oth, o, l, pieces):
    q_spec = pl.BlockSpec((TOK, HD), lambda h, sc: (0, sc[0] * GRP + h))
    state = pl.BlockSpec((1, 2 * TOK, HD), lambda h, sc: (h, 0, 0))
    sums = pl.BlockSpec((1, 8, HD), lambda h, sc: (h, 0, 0))
    flat = pl.BlockSpec((TOK, HD), lambda h, sc: (0, h))
    if last:
        out_shape = [jax.ShapeDtypeStruct((TOK, GW), jnp.bfloat16)] * 2
    else:
        out_shape = [
            jax.ShapeDtypeStruct((GRP, 2 * TOK, HD), jnp.float32),
            jax.ShapeDtypeStruct((GRP, 8, HD), jnp.float32),
        ]
    return pl.pallas_call(
        functools.partial(far_kernel, low, high, sizes, last),
        grid_spec=pltpu.PrefetchScalarGridSpec(
            num_scalar_prefetch=1,
            grid=(GRP,),
            in_specs=[
                q_spec,
                q_spec,
                state,
                sums,
                *[pl.BlockSpec(memory_space=pl.ANY)] * (high - low),
            ],
            out_specs=[flat, flat] if last else [state, sums],
            scratch_shapes=[
                pltpu.VMEM((2, NV * BLK, 3 * HD), jnp.bfloat16),
                pltpu.SemaphoreType.DMA((2,)),
            ],
        ),
        out_shape=out_shape,
        compiler_params=pltpu.CompilerParams(vmem_limit_bytes=48 << 20),
        name="far_last" if last else "far_first",
    )(scalars, queries, q_oth, o, l, *pieces)


def shards(queries, keys, values, columns, offsets, out_weight):
    me = lax.axis_index("ctx")
    core = me % 2
    half = lax.axis_index("kvh")
    i32 = jnp.int32

    def cut(value, which, width, axis=1):
        return lax.dynamic_slice_in_dim(value, which * width, width, axis)

    own_slots, kv_own, sent = pack(jnp.stack([core, me]).astype(i32), columns, keys, values)
    got = permute(sent, send_core)
    q_oth = permute(queries, send_core)
    slots = CAP * BLK
    kv_oth = got[slots:]
    both = jnp.concatenate([own_slots, got[:slots]], axis=0)
    far_y = permute(both, send_y)
    held = jnp.where(core == 1, kv_own, kv_oth)
    kv_before = lax.ppermute(held, "ctx", [(i, i + 2) for i in range(62)])
    pool_a = jnp.concatenate([both[:slots], far_y[:slots]], axis=0)
    pool_b = jnp.concatenate([both[slots:], far_y[slots:]], axis=0)
    pool_a, pool_b, kv_before, q_oth, columns = lax.optimization_barrier(
        (pool_a, pool_b, kv_before, q_oth, columns)
    )
    near_scalars, far_scalars = tables(me[None].astype(i32), columns)
    pool_a = jnp.concatenate(ring(pool_a, send_z), axis=0)
    pool_b = jnp.concatenate(ring(pool_b, send_x), axis=0)
    pool_a, pool_b, near_scalars = lax.optimization_barrier((pool_a, pool_b, near_scalars))
    low_a, high_a = permute(pool_a, send_x(1)), permute(pool_a, send_x(-1))
    low_b, high_b = permute(pool_b, send_z(1)), permute(pool_b, send_z(-1))
    o, l = near_attention(near_scalars, queries, q_oth, (kv_own, kv_oth, kv_before), offsets)
    low_a, high_a, low_b, high_b, o = lax.optimization_barrier((low_a, high_a, low_b, high_b, o))
    middle = pool_a.shape[0] // 2
    second = [
        permute(low_a[:middle], send_x(1)),
        permute(high_a[middle:], send_x(-1)),
        permute(low_b[:middle], send_z(1)),
        permute(high_b[middle:], send_z(-1)),
    ]
    first = [pool_a, low_a, high_a, pool_b, low_b, high_b]
    o, l = far_attention(0, 6, (8, 12, 16), False, far_scalars, queries, q_oth, o, l, first)
    own, oth = far_attention(6, 10, (4, 8, 16), True, far_scalars, queries, q_oth, o, l, second)

    columns_out = out_weight.shape[1] // 2
    weight_kept = cut(out_weight, half, columns_out)
    weight_sent = cut(out_weight, 1 - half, columns_out)
    results = []
    parts = [slice(0, BLK), slice(BLK, TOK)]
    first, others = [permute(oth[rows], send_core) for rows in parts]
    for at in range(0, TOK, BLK):
        rows = slice(at, at + BLK)
        got = first if at == 0 else others[at - BLK : at]
        attended = jnp.where(
            core == 0,
            jnp.concatenate([own[rows], got], 1),
            jnp.concatenate([got, own[rows]], 1),
        )
        sent = jnp.dot(attended, weight_sent, preferred_element_type=jnp.float32)
        taken = permute(sent.astype(jnp.bfloat16), lambda i: 1 - i, "kvh")
        kept = jnp.dot(attended, weight_kept, preferred_element_type=jnp.float32)
        results.append((kept + taken.astype(jnp.float32)).astype(jnp.bfloat16))
    return jnp.concatenate(results, axis=0)


def solution(mesh):
    placed = (
        P("ctx", "kvh"),
        P("ctx", "kvh"),
        P("ctx", "kvh"),
        P("kvh", None),
        P("kvh", None),
        P("kvh", None),
    )
    return jax.shard_map(
        shards, mesh=mesh, in_specs=placed, out_specs=P("ctx", "kvh"), check_vma=False
    )
```

```python
import functools
import math

import jax
import jax.numpy as jnp
from jax import lax
from jax.experimental import pallas as pl
from jax.experimental.pallas import tpu as pltpu
from jax.sharding import PartitionSpec as P

HD = 128
BLK = 128
NV = 16
CAP = 2
WIN = 512
TOK = 512
GRP = 7
GW = GRP * HD
WINB = WIN // BLK
NEG = -1e30
LOG2 = math.log2(math.e) / math.sqrt(HD)


def coords(i):
    return i // 16, i // 4 % 4, i // 2 % 2, i % 2


def index(x, z, y, c):
    return (x % 4) * 16 + (z % 4) * 4 + (y % 2) * 2 + c % 2


def send_x(by):
    def to(i):
        x, z, y, c = coords(i)
        return index(x + by, z, y, c)

    return to


def send_z(by):
    def to(i):
        x, z, y, c = coords(i)
        return index(x, z + by, y, c)

    return to


def send_y(i):
    x, z, y, c = coords(i)
    return index(x, z, y + 1, c)


def send_core(i):
    return i ^ 1


def permute(value, to, axis="ctx"):
    return lax.ppermute(value, axis, [(i, to(i)) for i in range(lax.axis_size(axis))])


def ring(piece, send):
    return [piece] + [permute(piece, send(by)) for by in (1, -1, 2)]


def to_rows(value):
    return [value[k * BLK : (k + 1) * BLK, :].T[0:1, :] for k in range(2)]


def from_rows(ref, i):
    return jnp.concatenate(
        [jnp.broadcast_to(ref[0, pl.ds(2 * i + k, 1), :], (BLK, BLK)).T for k in range(2)], 0
    )


def dot_t(a, b):
    return lax.dot_general(a, b, (((1,), (1,)), ((), ())), preferred_element_type=jnp.float32)


TILE = 2 * BLK
SPAN = WIN + TILE
NEAR_FLAGS = 2
NEAR_EXTRA = NEAR_FLAGS + 8 * GRP
NEAR_SIZE = NEAR_EXTRA + 4 * GRP
PIECES = 10
FAR_OFF = 1 + GRP
FAR_CODE = FAR_OFF + GRP * (PIECES + 1)
FAR_SIZE = FAR_CODE + GRP * NV


def table_kernel(sc, lists, near, far, marks, codes, heads):
    me = sc[0]
    core, chip = me & 1, me >> 1
    x, z, y = chip >> 3, (chip >> 1) & 3, chip & 1
    start = chip * 8
    near[0] = core
    near[1] = (chip == 0).astype(jnp.int32)
    far[0] = core

    def clear(i, _):
        for k in range(4):
            marks[4 * i + k] = 0
        return 0

    lax.fori_loop(0, 64, clear, 0)

    def clear_near(i, _):
        for k in range(8):
            near[NEAR_FLAGS + 8 * i + k] = 0
        for k in range(4):
            near[NEAR_EXTRA + 4 * i + k] = 99
        return 0

    lax.fori_loop(0, GRP, clear_near, 0)

    def mark(h, _):
        for j in range(NV):
            marks[lists[core * GRP + h, j]] = 1
        return 0

    lax.fori_loop(0, GRP, mark, 0)

    def place(step):
        return jnp.where(step == 0, 0, jnp.where(step == 3, 1, step + 1))

    def one_head(h, _):
        for k in range(PIECES):
            heads[k] = 0

        def classify(j, _):
            b = lists[core * GRP + h, j]
            run = b >> 2
            at = b & 3
            base = b - at
            slot = jnp.where(at > 0, marks[base], 0)
            slot = slot + jnp.where(at > 1, marks[base + 1], 0)
            slot = slot + jnp.where(at > 2, marks[base + 2], 0)
            cx = place(((run >> 4) - x) & 3)
            cz = place(((run >> 2) - z) & 3)
            same = (run & 1) == core
            ring = jnp.where(same, cx, cz)
            low = jnp.where(((run >> 1) & 1) == y, 0, 2) + jnp.minimum(slot, 1)
            within = jnp.where(same, cz, cx) * 4 + low
            upper = (ring == 3) & (within > 7)
            piece = jnp.where(
                ring == 3,
                jnp.where(same, 6, 8) + upper.astype(jnp.int32),
                jnp.where(same, 0, 3) + ring,
            )
            within = within - jnp.where(upper, 8, 0)
            far_block = b <= start - 5
            codes[j] = jnp.where(far_block, piece * 16 + within, -1)
            heads[piece] = heads[piece] + far_block.astype(jnp.int32)
            w = b - (start - WINB)

            @pl.when((w >= 0) & (w < 8))
            def _():
                near[NEAR_FLAGS + h * 8 + w] = 1
                pair = NEAR_EXTRA + h * 4 + (w >> 2) * 2
                second = (near[pair] < 99).astype(jnp.int32)
                near[pair + second] = w

            return 0

        lax.fori_loop(0, NV, classify, 0)
        total = jnp.int32(0)
        for k in range(PIECES):
            far[FAR_OFF + h * (PIECES + 1) + k] = total
            held = heads[k]
            heads[k] = total
            total = total + held
        far[FAR_OFF + h * (PIECES + 1) + PIECES] = total
        far[1 + h] = total

        def store(j, _):
            code = codes[j]

            @pl.when(code >= 0)
            def _():
                k = code >> 4
                far[FAR_CODE + h * NV + heads[k]] = code & 15
                heads[k] = heads[k] + 1

            return 0

        lax.fori_loop(0, NV, store, 0)
        return 0

    lax.fori_loop(0, GRP, one_head, 0)


def tables(me, columns):
    smem = pltpu.MemorySpace.SMEM
    return pl.pallas_call(
        table_kernel,
        in_specs=[pl.BlockSpec(memory_space=smem)] * 2,
        out_specs=[pl.BlockSpec(memory_space=smem)] * 2,
        out_shape=[
            jax.ShapeDtypeStruct((NEAR_SIZE,), jnp.int32),
            jax.ShapeDtypeStruct((FAR_SIZE,), jnp.int32),
        ],
        scratch_shapes=[
            pltpu.SMEM((256,), jnp.int32),
            pltpu.SMEM((NV,), jnp.int32),
            pltpu.SMEM((PIECES,), jnp.int32),
        ],
        name="index_tables",
    )(me, columns)


def near_kernel(
    sc, q_own, q_oth, kv_own, kv_oth, kv_before, offs, o_ref, l_ref, kext, vext, acc_s, m_s
):
    h = pl.program_id(0)
    core = sc[0]

    @pl.when(h == 0)
    def _():
        own_at = pl.ds(pl.multiple_of(TOK + core * TOK, TOK), TOK)
        oth_at = pl.ds(pl.multiple_of(2 * TOK - core * TOK, TOK), TOK)
        for at, part in ((own_at, kv_own), (oth_at, kv_oth)):
            kext[at, :] = part[:, :HD]
            vext[at, :HD] = part[:, HD:]

        kext[:TOK, :] = kv_before[:, :HD]
        vext[:TOK, :HD] = kv_before[:, HD:]
        vext[:, HD:] = jnp.ones((vext.shape[0], HD), jnp.bfloat16)

    line = offs[pl.ds(core * GRP + h, 1), :]
    spread = jnp.broadcast_to(line.astype(jnp.float32), (BLK, BLK)).T
    lane = lax.broadcasted_iota(jnp.int32, (BLK, BLK), 1)
    marks = []
    for k in range(SPAN // BLK):
        hit = spread == (WIN - k * BLK - lane).astype(jnp.float32)
        marks.append(jnp.max(jnp.where(hit, 0.0, NEG), axis=0, keepdims=True))
    pattern = jnp.concatenate(marks, axis=1)
    bias = pltpu.roll(
        jnp.broadcast_to(pattern, (TILE, SPAN)), 0, 1, stride=1, stride_axis=0
    )
    rows = lax.broadcasted_iota(jnp.int32, (TILE, TILE), 0)
    lanes = lax.broadcasted_iota(jnp.int32, (TILE, TILE), 1)
    far_side = lanes <= rows
    tile_lane = lax.broadcasted_iota(jnp.int32, (1, TILE), 1)
    span_lane = lax.broadcasted_iota(jnp.int32, (1, SPAN), 1)

    def tile_of(i):
        return 4 * (core if i < 2 else 1 - core) + 2 * (i % 2)

    def q_of(i):
        return (q_own if i < 2 else q_oth)[(i % 2) * TILE : (i % 2 + 1) * TILE, :]

    for i in range(4):
        t = tile_of(i)
        base = pl.multiple_of(t * BLK, BLK)
        s = dot_t(q_of(i), kext[pl.ds(base, SPAN), :])
        flag = NEAR_FLAGS + h * 8 + t
        la = jnp.where(sc[flag] > 0, 0.0, NEG).astype(jnp.float32)
        lb = jnp.where(sc[flag + 1] > 0, 0.0, NEG).astype(jnp.float32)
        first = jnp.where(far_side, jnp.where(tile_lane < BLK, la, lb), bias[:, :TILE])
        absent = jnp.where(sc[1] > 0, BLK * (WINB - t), 0)
        edge = jnp.where(span_lane < absent, NEG, 0.0).astype(jnp.float32)
        s = s + jnp.concatenate([first, bias[:, TILE:]], axis=1) + edge
        m = jnp.max(s, axis=1, keepdims=True)
        p = jnp.exp2((s - m) * LOG2).astype(jnp.bfloat16)
        acc_s[i] = jnp.dot(p, vext[pl.ds(base, SPAN), :], preferred_element_type=jnp.float32)
        m_s[i] = jnp.broadcast_to(m, (TILE, HD))

    ex = NEAR_EXTRA + 4 * h
    lowest = jnp.minimum(jnp.minimum(sc[ex], sc[ex + 1]), jnp.minimum(sc[ex + 2], sc[ex + 3]))

    @pl.when(lowest < 6)
    def _():
        for i in range(4):
            t = tile_of(i)
            for g in range(2):
                wa, wb = sc[ex + 2 * g], sc[ex + 2 * g + 1]

                @pl.when((wa < t) | (wb < t))
                def _():
                    ra = pl.multiple_of(jnp.minimum(wa, 11) * BLK, BLK)
                    rb = pl.multiple_of(jnp.minimum(wb, 11) * BLK, BLK)
                    ks = jnp.concatenate([kext[pl.ds(ra, BLK), :], kext[pl.ds(rb, BLK), :]], 0)
                    vs = jnp.concatenate([vext[pl.ds(ra, BLK), :], vext[pl.ds(rb, BLK), :]], 0)
                    s = dot_t(q_of(i), ks)
                    ba = jnp.where(wa < t, 0.0, NEG).astype(jnp.float32)
                    bb = jnp.where(wb < t, 0.0, NEG).astype(jnp.float32)
                    s = s + jnp.where(tile_lane < BLK, ba, bb)
                    m_old = m_s[i]
                    m_new = jnp.maximum(m_old, jnp.max(s, axis=1, keepdims=True))
                    scale = jnp.exp2((m_old - m_new) * LOG2)
                    p = jnp.exp2((s - jnp.concatenate([m_new, m_new], 1)) * LOG2)
                    acc_s[i] = acc_s[i] * jnp.concatenate([scale, scale], 1) + jnp.dot(
                        p.astype(jnp.bfloat16), vs, preferred_element_type=jnp.float32
                    )
                    m_s[i] = m_new

    for i in range(4):
        total = acc_s[i, :, HD:]
        o_ref[0, i * TILE : (i + 1) * TILE, :] = acc_s[i, :, :HD] / total
        for k, line in enumerate(to_rows(m_s[i] * LOG2 + jnp.log2(total))):
            l_ref[0, 2 * i + k : 2 * i + k + 1, :] = line


def near_attention(scalars, queries, q_oth, parts, offsets):
    rows = 2 * TOK
    state = jax.ShapeDtypeStruct((GRP, rows, HD), jnp.float32)
    sums = jax.ShapeDtypeStruct((GRP, 8, HD), jnp.float32)
    q_spec = pl.BlockSpec((TOK, HD), lambda h, sc: (0, sc[0] * GRP + h))
    return pl.pallas_call(
        near_kernel,
        grid_spec=pltpu.PrefetchScalarGridSpec(
            num_scalar_prefetch=1,
            grid=(GRP,),
            in_specs=[
                q_spec,
                q_spec,
                *[pl.BlockSpec((TOK, 2 * HD), lambda h, sc: (0, 0))] * 3,
                pl.BlockSpec(offsets.shape, lambda h, sc: (0, 0)),
            ],
            out_specs=[
                pl.BlockSpec((1, rows, HD), lambda h, sc: (h, 0, 0)),
                pl.BlockSpec((1, 8, HD), lambda h, sc: (h, 0, 0)),
            ],
            scratch_shapes=[
                pltpu.VMEM((3 * TOK, HD), jnp.bfloat16),
                pltpu.VMEM((3 * TOK, 2 * HD), jnp.bfloat16),
                pltpu.VMEM((4, TILE, 2 * HD), jnp.float32),
                pltpu.VMEM((4, TILE, HD), jnp.float32),
            ],
        ),
        out_shape=[state, sums],
        compiler_params=pltpu.CompilerParams(vmem_limit_bytes=40 << 20),
        name="near_attention",
    )(scalars, queries, q_oth, *parts, offsets)


def pack_kernel(sc, lists, keys, values, own_slots, kv_own, sent):
    core, me = sc[0], sc[1]
    group = lax.broadcasted_iota(jnp.int32, lists.shape, 0) // GRP
    table = lists[...]

    def head_of(source, head, rows):
        low, high = source[rows, :HD], source[rows, HD:]
        return jnp.where(head == 0, low, high)

    for head, slots in ((core, own_slots), (1 - core, sent)):
        pick = [jnp.int32(0)] * CAP
        seen = jnp.int32(0)
        for b in range(TOK // BLK):
            hit = jnp.max(jnp.where((group == head) & (table == me * (TOK // BLK) + b), 1, 0))
            for k in range(CAP):
                pick[k] = jnp.where((hit > 0) & (seen == k), b, pick[k])
            seen = seen + hit
        for k in range(CAP):
            rows = pl.ds(pl.multiple_of(pick[k] * BLK, BLK), BLK)
            slots[k * BLK : (k + 1) * BLK, :HD] = head_of(keys, head, rows)
            slots[k * BLK : (k + 1) * BLK, HD:] = head_of(values, head, rows)
    whole = slice(0, TOK)
    for head, target, at in ((core, kv_own, 0), (1 - core, sent, CAP * BLK)):
        target[at : at + TOK, :HD] = head_of(keys, head, whole)
        target[at : at + TOK, HD:] = head_of(values, head, whole)


def pack(scalars, columns, keys, values):
    slots = jax.ShapeDtypeStruct((CAP * BLK, 2 * HD), jnp.bfloat16)
    whole = jax.ShapeDtypeStruct((TOK, 2 * HD), jnp.bfloat16)
    sent = jax.ShapeDtypeStruct((CAP * BLK + TOK, 2 * HD), jnp.bfloat16)

    def full(shape):
        return pl.BlockSpec(shape, lambda i, sc: (0, 0))

    return pl.pallas_call(
        pack_kernel,
        grid_spec=pltpu.PrefetchScalarGridSpec(
            num_scalar_prefetch=1,
            grid=(1,),
            in_specs=[full(columns.shape), full(keys.shape), full(values.shape)],
            out_specs=[full(a.shape) for a in (slots, whole, sent)],
        ),
        out_shape=[slots, whole, sent],
        name="pack_blocks",
    )(scalars, columns, keys, values)


def far_kernel(low, high, sizes, part, sc, q_own, q_oth, oa, ob, l_ref, *rest):
    pieces, (out_a, out_b, buf, sem) = rest[: high - low], rest[high - low :]
    last = part is not None
    h = pl.program_id(0)

    def bound(head, k):
        return sc[FAR_OFF + head * (PIECES + 1) + k]

    def fetch(head, slot):
        base = bound(head, low)
        for k in range(low, high):

            def start(i, _, k=k):
                code = sc[FAR_CODE + head * NV + i]
                pltpu.make_async_copy(
                    pieces[k - low].at[pl.ds(pl.multiple_of(code * BLK, BLK), BLK), :],
                    buf.at[
                        slot, pl.ds(pl.multiple_of((i - base) * BLK, BLK), BLK), pl.ds(0, 2 * HD)
                    ],
                    sem.at[slot],
                ).start()
                return 0

            lax.fori_loop(bound(head, k), bound(head, k + 1), start, 0)

    slot = h % 2

    @pl.when(h == 0)
    def _():
        fetch(0, 0)

    @pl.when(h + 1 < GRP)
    def _():
        fetch(h + 1, 1 - slot)

    n = bound(h, high) - bound(h, low)

    def arrived(i, _):
        pltpu.make_async_copy(
            pieces[0].at[pl.ds(0, BLK), :],
            buf.at[slot, pl.ds(0, BLK), pl.ds(0, 2 * HD)],
            sem.at[slot],
        ).wait()
        return 0

    lax.fori_loop(0, n, arrived, 0)
    buf[slot, :, 2 * HD :] = jnp.ones((NV * BLK, HD), jnp.bfloat16)

    def fill(i, _):
        rows = pl.ds(pl.multiple_of(i * BLK, BLK), BLK)
        buf[slot, rows, :HD] = buf[slot, :BLK, :HD]
        buf[slot, rows, HD:] = jnp.zeros((BLK, 2 * HD), jnp.bfloat16)
        return 0

    wanted = jnp.int32(0)
    for size in sizes[::-1]:
        wanted = jnp.where(n <= size, size, wanted)
    lax.fori_loop(jnp.where(n > 0, n, NV), wanted, fill, 0)

    def update(k, size):
        keys = size * BLK
        rows = pl.ds(0, TILE) if last else pl.ds(pl.multiple_of(k * TILE, TILE), TILE)
        for side, q_ref, o_ref in ((0, q_own, oa), (1, q_oth, ob)):
            i = 2 * side + k
            o = o_ref[0, rows, :]
            if size > 0:
                s = dot_t(q_ref[rows, :], buf[slot, :keys, :HD])
                m = jnp.max(s, axis=1, keepdims=True)
                p = jnp.exp2((s - m) * LOG2).astype(jnp.bfloat16)
                acc = jnp.dot(p, buf[slot, :keys, HD:], preferred_element_type=jnp.float32)
                top = jnp.broadcast_to(m * LOG2, (TILE, HD))
                l = from_rows(l_ref, i)
                both = jnp.maximum(l, top)
                wn = jnp.exp2(l - both)
                wf = jnp.exp2(top - both)
                weight = wn + acc[:, HD:] * wf
                o = (o * wn + acc[:, :HD] * wf) / weight
                if not last:
                    for j, line in enumerate(to_rows(both + jnp.log2(weight))):
                        out_b[0, pl.ds(2 * i + j, 1), :] = line
            if last:
                (out_a, out_b)[side][...] = o.astype(jnp.bfloat16)
            else:
                at = pl.multiple_of(i * TILE, TILE)
                out_a[0, pl.ds(at, TILE), :] = o

    def all_rows(size):
        if last:
            update(part, size)
        else:

            def step(k, _):
                update(k, size)
                return 0

            lax.fori_loop(0, 2, step, 0)

    below = 0
    for size in sizes:

        @pl.when((n > below) & (n <= size))
        def _(size=size):
            all_rows(size)

        below = size

    @pl.when(n == 0)
    def _():
        all_rows(0)
        if not last:
            out_b[...] = l_ref[...]


def far_attention(low, high, sizes, part, scalars, queries, q_oth, o, l, pieces):
    last = part is not None
    rows = TILE if last else TOK
    at = part if last else 0
    q_spec = pl.BlockSpec((rows, HD), lambda h, sc: (at, sc[0] * GRP + h))
    own = pl.BlockSpec((1, rows, HD), lambda h, sc: (h, at, 0))
    oth = pl.BlockSpec((1, rows, HD), lambda h, sc: (h, TOK // rows + at, 0))
    state = pl.BlockSpec((1, 2 * TOK, HD), lambda h, sc: (h, 0, 0))
    sums = pl.BlockSpec((1, 8, HD), lambda h, sc: (h, 0, 0))
    flat = pl.BlockSpec((rows, HD), lambda h, sc: (0, h))
    if last:
        out_shape = [jax.ShapeDtypeStruct((rows, GW), jnp.bfloat16)] * 2
    else:
        out_shape = [
            jax.ShapeDtypeStruct((GRP, 2 * TOK, HD), jnp.float32),
            jax.ShapeDtypeStruct((GRP, 8, HD), jnp.float32),
        ]
    return pl.pallas_call(
        functools.partial(far_kernel, low, high, sizes, part),
        grid_spec=pltpu.PrefetchScalarGridSpec(
            num_scalar_prefetch=1,
            grid=(GRP,),
            in_specs=[
                q_spec,
                q_spec,
                own,
                oth,
                sums,
                *[pl.BlockSpec(memory_space=pl.ANY)] * (high - low),
            ],
            out_specs=[flat, flat] if last else [state, sums],
            scratch_shapes=[
                pltpu.VMEM((2, NV * BLK, 3 * HD), jnp.bfloat16),
                pltpu.SemaphoreType.DMA((2,)),
            ],
        ),
        out_shape=out_shape,
        compiler_params=pltpu.CompilerParams(vmem_limit_bytes=48 << 20),
        name="far_last" if last else "far_first",
    )(scalars, queries, q_oth, o, o, l, *pieces)


def shards(queries, keys, values, columns, offsets, out_weight):
    me = lax.axis_index("ctx")
    core = me % 2
    half = lax.axis_index("kvh")
    i32 = jnp.int32

    def cut(value, which, width, axis=1):
        return lax.dynamic_slice_in_dim(value, which * width, width, axis)

    own_slots, kv_own, sent = pack(jnp.stack([core, me]).astype(i32), columns, keys, values)
    got = permute(sent, send_core)
    q_oth = permute(queries, send_core)
    slots = CAP * BLK
    kv_oth = got[slots:]
    both = jnp.concatenate([own_slots, got[:slots]], axis=0)
    both, columns = lax.optimization_barrier((both, columns))
    far_y = permute(both, send_y)
    near_scalars, far_scalars = tables(me[None].astype(i32), columns)
    held = jnp.where(core == 1, kv_own, kv_oth)
    kv_before = lax.ppermute(held, "ctx", [(i, i + 2) for i in range(62)])
    pool_a = jnp.concatenate([both[:slots], far_y[:slots]], axis=0)
    pool_b = jnp.concatenate([both[slots:], far_y[slots:]], axis=0)
    pool_a, pool_b, kv_before, q_oth, near_scalars = lax.optimization_barrier(
        (pool_a, pool_b, kv_before, q_oth, near_scalars)
    )
    pool_a = jnp.concatenate(ring(pool_a, send_z), axis=0)
    pool_b = jnp.concatenate(ring(pool_b, send_x), axis=0)
    low_a, high_a = permute(pool_a, send_x(1)), permute(pool_a, send_x(-1))
    low_b, high_b = permute(pool_b, send_z(1)), permute(pool_b, send_z(-1))
    o, l = near_attention(near_scalars, queries, q_oth, (kv_own, kv_oth, kv_before), offsets)
    low_a, high_a, low_b, high_b, o = lax.optimization_barrier((low_a, high_a, low_b, high_b, o))
    middle = pool_a.shape[0] // 2
    second = [
        permute(low_a[:middle], send_x(1)),
        permute(high_a[middle:], send_x(-1)),
        permute(low_b[:middle], send_z(1)),
        permute(high_b[middle:], send_z(-1)),
    ]
    first = [pool_a, low_a, high_a, pool_b, low_b, high_b]
    o, l = far_attention(
        0, 6, (8, 10, 12, 14, 16), None, far_scalars, queries, q_oth, o, l, first
    )

    columns_out = out_weight.shape[1] // 2
    weight_kept = cut(out_weight, half, columns_out)
    weight_sent = cut(out_weight, 1 - half, columns_out)
    results = []
    for part in range(2):
        own, oth = far_attention(
            6, 10, (2, 4, 6, 8, 16), part, far_scalars, queries, q_oth, o, l, second
        )
        got = permute(oth, send_core)
        attended = jnp.where(
            core == 0, jnp.concatenate([own, got], 1), jnp.concatenate([got, own], 1)
        )
        sent = jnp.dot(attended, weight_sent, preferred_element_type=jnp.float32)
        sent = sent.astype(jnp.bfloat16)
        if part == 0:
            sent, far_scalars = lax.optimization_barrier((sent, far_scalars))
        taken = permute(sent, lambda i: 1 - i, "kvh")
        kept = jnp.dot(attended, weight_kept, preferred_element_type=jnp.float32)
        results.append((kept + taken.astype(jnp.float32)).astype(jnp.bfloat16))
    return jnp.concatenate(results, axis=0)


def solution(mesh):
    placed = (
        P("ctx", "kvh"),
        P("ctx", "kvh"),
        P("ctx", "kvh"),
        P("kvh", None),
        P("kvh", None),
        P("kvh", None),
    )
    return jax.shard_map(
        shards, mesh=mesh, in_specs=placed, out_specs=P("ctx", "kvh"), check_vma=False
    )
```

```python
import functools
import math

import jax
import jax.numpy as jnp
from jax import lax
from jax.experimental import pallas as pl
from jax.experimental.pallas import tpu as pltpu
from jax.sharding import PartitionSpec as P

HD = 128
BLK = 128
NV = 16
CAP = 2
WIN = 512
TOK = 512
GRP = 7
GW = GRP * HD
WINB = WIN // BLK
NEG = -1e30
LOG2 = math.log2(math.e) / math.sqrt(HD)


def coords(i):
    return i // 16, i // 4 % 4, i // 2 % 2, i % 2


def index(x, z, y, c):
    return (x % 4) * 16 + (z % 4) * 4 + (y % 2) * 2 + c % 2


def send_x(by):
    def to(i):
        x, z, y, c = coords(i)
        return index(x + by, z, y, c)

    return to


def send_z(by):
    def to(i):
        x, z, y, c = coords(i)
        return index(x, z + by, y, c)

    return to


def send_y(i):
    x, z, y, c = coords(i)
    return index(x, z, y + 1, c)


def send_core(i):
    return i ^ 1


def permute(value, to, axis="ctx"):
    return lax.ppermute(value, axis, [(i, to(i)) for i in range(lax.axis_size(axis))])


def ring(piece, send):
    return [piece] + [permute(piece, send(by)) for by in (1, -1, 2)]


def to_rows(value):
    return [value[k * BLK : (k + 1) * BLK, :].T[0:1, :] for k in range(2)]


def from_rows(ref, i):
    return jnp.concatenate(
        [jnp.broadcast_to(ref[0, 2 * i + k : 2 * i + k + 1, :], (BLK, BLK)).T for k in range(2)], 0
    )


def dot_t(a, b):
    return lax.dot_general(a, b, (((1,), (1,)), ((), ())), preferred_element_type=jnp.float32)


TILE = 2 * BLK
SPAN = WIN + TILE
NEAR_FLAGS = 2
NEAR_EXTRA = NEAR_FLAGS + 8 * GRP
NEAR_SIZE = NEAR_EXTRA + 4 * GRP
PIECES = 10
FAR_OFF = 1 + GRP
FAR_CODE = FAR_OFF + GRP * (PIECES + 1)
FAR_SIZE = FAR_CODE + GRP * NV


def table_kernel(sc, lists, near, far, marks, codes, heads):
    me = sc[0]
    core, chip = me & 1, me >> 1
    x, z, y = chip >> 3, (chip >> 1) & 3, chip & 1
    start = chip * 8
    near[0] = core
    near[1] = (chip == 0).astype(jnp.int32)
    far[0] = core

    def clear(i, _):
        for k in range(4):
            marks[4 * i + k] = 0
        return 0

    lax.fori_loop(0, 64, clear, 0)

    def clear_near(i, _):
        for k in range(8):
            near[NEAR_FLAGS + 8 * i + k] = 0
        for k in range(4):
            near[NEAR_EXTRA + 4 * i + k] = 99
        return 0

    lax.fori_loop(0, GRP, clear_near, 0)

    def mark(h, _):
        for j in range(NV):
            marks[lists[core * GRP + h, j]] = 1
        return 0

    lax.fori_loop(0, GRP, mark, 0)

    def place(step):
        return jnp.where(step == 0, 0, jnp.where(step == 3, 1, step + 1))

    def one_head(h, _):
        for k in range(PIECES):
            heads[k] = 0

        def classify(j, _):
            b = lists[core * GRP + h, j]
            run = b >> 2
            at = b & 3
            base = b - at
            slot = jnp.where(at > 0, marks[base], 0)
            slot = slot + jnp.where(at > 1, marks[base + 1], 0)
            slot = slot + jnp.where(at > 2, marks[base + 2], 0)
            cx = place(((run >> 4) - x) & 3)
            cz = place(((run >> 2) - z) & 3)
            same = (run & 1) == core
            ring = jnp.where(same, cx, cz)
            low = jnp.where(((run >> 1) & 1) == y, 0, 2) + jnp.minimum(slot, 1)
            within = jnp.where(same, cz, cx) * 4 + low
            upper = (ring == 3) & (within > 7)
            piece = jnp.where(
                ring == 3,
                jnp.where(same, 6, 8) + upper.astype(jnp.int32),
                jnp.where(same, 0, 3) + ring,
            )
            within = within - jnp.where(upper, 8, 0)
            far_block = b <= start - 5
            codes[j] = jnp.where(far_block, piece * 16 + within, -1)
            heads[piece] = heads[piece] + far_block.astype(jnp.int32)
            w = b - (start - WINB)

            @pl.when((w >= 0) & (w < 8))
            def _():
                near[NEAR_FLAGS + h * 8 + w] = 1
                pair = NEAR_EXTRA + h * 4 + (w >> 2) * 2
                second = (near[pair] < 99).astype(jnp.int32)
                near[pair + second] = w

            return 0

        lax.fori_loop(0, NV, classify, 0)
        total = jnp.int32(0)
        for k in range(PIECES):
            far[FAR_OFF + h * (PIECES + 1) + k] = total
            held = heads[k]
            heads[k] = total
            total = total + held
        far[FAR_OFF + h * (PIECES + 1) + PIECES] = total
        far[1 + h] = total

        def store(j, _):
            code = codes[j]

            @pl.when(code >= 0)
            def _():
                k = code >> 4
                far[FAR_CODE + h * NV + heads[k]] = code & 15
                heads[k] = heads[k] + 1

            return 0

        lax.fori_loop(0, NV, store, 0)
        return 0

    lax.fori_loop(0, GRP, one_head, 0)


def tables(me, columns):
    smem = pltpu.MemorySpace.SMEM
    return pl.pallas_call(
        table_kernel,
        in_specs=[pl.BlockSpec(memory_space=smem)] * 2,
        out_specs=[pl.BlockSpec(memory_space=smem)] * 2,
        out_shape=[
            jax.ShapeDtypeStruct((NEAR_SIZE,), jnp.int32),
            jax.ShapeDtypeStruct((FAR_SIZE,), jnp.int32),
        ],
        scratch_shapes=[
            pltpu.SMEM((256,), jnp.int32),
            pltpu.SMEM((NV,), jnp.int32),
            pltpu.SMEM((PIECES,), jnp.int32),
        ],
        name="index_tables",
    )(me, columns)


def near_kernel(
    sc, q_own, q_oth, kv_own, kv_oth, kv_before, offs, o_ref, l_ref, kext, vext, acc_s, m_s
):
    h = pl.program_id(0)
    core = sc[0]

    @pl.when(h == 0)
    def _():
        own_at = pl.ds(pl.multiple_of(TOK + core * TOK, TOK), TOK)
        oth_at = pl.ds(pl.multiple_of(2 * TOK - core * TOK, TOK), TOK)
        for at, part in ((own_at, kv_own), (oth_at, kv_oth)):
            kext[at, :] = part[:, :HD]
            vext[at, :HD] = part[:, HD:]

        kext[:TOK, :] = kv_before[:, :HD]
        vext[:TOK, :HD] = kv_before[:, HD:]
        vext[:, HD:] = jnp.ones((vext.shape[0], HD), jnp.bfloat16)

    line = offs[pl.ds(core * GRP + h, 1), :]
    spread = jnp.broadcast_to(line.astype(jnp.float32), (BLK, BLK)).T
    lane = lax.broadcasted_iota(jnp.int32, (BLK, BLK), 1)
    marks = []
    for k in range(SPAN // BLK):
        hit = spread == (WIN - k * BLK - lane).astype(jnp.float32)
        marks.append(jnp.max(jnp.where(hit, 0.0, NEG), axis=0, keepdims=True))
    pattern = jnp.concatenate(marks, axis=1)
    bias = pltpu.roll(
        jnp.broadcast_to(pattern, (TILE, SPAN)), 0, 1, stride=1, stride_axis=0
    )
    rows = lax.broadcasted_iota(jnp.int32, (TILE, TILE), 0)
    lanes = lax.broadcasted_iota(jnp.int32, (TILE, TILE), 1)
    far_side = lanes <= rows
    tile_lane = lax.broadcasted_iota(jnp.int32, (1, TILE), 1)
    span_lane = lax.broadcasted_iota(jnp.int32, (1, SPAN), 1)

    def tile_of(i):
        return 4 * (core if i < 2 else 1 - core) + 2 * (i % 2)

    def q_of(i):
        return (q_own if i < 2 else q_oth)[(i % 2) * TILE : (i % 2 + 1) * TILE, :]

    for i in range(4):
        t = tile_of(i)
        base = pl.multiple_of(t * BLK, BLK)
        s = dot_t(q_of(i), kext[pl.ds(base, SPAN), :])
        flag = NEAR_FLAGS + h * 8 + t
        la = jnp.where(sc[flag] > 0, 0.0, NEG).astype(jnp.float32)
        lb = jnp.where(sc[flag + 1] > 0, 0.0, NEG).astype(jnp.float32)
        first = jnp.where(far_side, jnp.where(tile_lane < BLK, la, lb), bias[:, :TILE])
        absent = jnp.where(sc[1] > 0, BLK * (WINB - t), 0)
        edge = jnp.where(span_lane < absent, NEG, 0.0).astype(jnp.float32)
        s = s + jnp.concatenate([first, bias[:, TILE:]], axis=1) + edge
        m = jnp.max(s, axis=1, keepdims=True)
        p = jnp.exp2((s - m) * LOG2).astype(jnp.bfloat16)
        acc_s[i] = jnp.dot(p, vext[pl.ds(base, SPAN), :], preferred_element_type=jnp.float32)
        m_s[i] = jnp.broadcast_to(m, (TILE, HD))

    ex = NEAR_EXTRA + 4 * h
    lowest = jnp.minimum(jnp.minimum(sc[ex], sc[ex + 1]), jnp.minimum(sc[ex + 2], sc[ex + 3]))

    @pl.when(lowest < 6)
    def _():
        for i in range(4):
            t = tile_of(i)
            for g in range(2):
                wa, wb = sc[ex + 2 * g], sc[ex + 2 * g + 1]

                @pl.when((wa < t) | (wb < t))
                def _():
                    ra = pl.multiple_of(jnp.minimum(wa, 11) * BLK, BLK)
                    rb = pl.multiple_of(jnp.minimum(wb, 11) * BLK, BLK)
                    ks = jnp.concatenate([kext[pl.ds(ra, BLK), :], kext[pl.ds(rb, BLK), :]], 0)
                    vs = jnp.concatenate([vext[pl.ds(ra, BLK), :], vext[pl.ds(rb, BLK), :]], 0)
                    s = dot_t(q_of(i), ks)
                    ba = jnp.where(wa < t, 0.0, NEG).astype(jnp.float32)
                    bb = jnp.where(wb < t, 0.0, NEG).astype(jnp.float32)
                    s = s + jnp.where(tile_lane < BLK, ba, bb)
                    m_old = m_s[i]
                    m_new = jnp.maximum(m_old, jnp.max(s, axis=1, keepdims=True))
                    scale = jnp.exp2((m_old - m_new) * LOG2)
                    p = jnp.exp2((s - jnp.concatenate([m_new, m_new], 1)) * LOG2)
                    acc_s[i] = acc_s[i] * jnp.concatenate([scale, scale], 1) + jnp.dot(
                        p.astype(jnp.bfloat16), vs, preferred_element_type=jnp.float32
                    )
                    m_s[i] = m_new

    for i in range(4):
        total = acc_s[i, :, HD:]
        o_ref[0, i * TILE : (i + 1) * TILE, :] = acc_s[i, :, :HD] / total
        for k, line in enumerate(to_rows(m_s[i] * LOG2 + jnp.log2(total))):
            l_ref[0, 2 * i + k : 2 * i + k + 1, :] = line


def near_attention(scalars, queries, q_oth, parts, offsets):
    rows = 2 * TOK
    state = jax.ShapeDtypeStruct((GRP, rows, HD), jnp.float32)
    sums = jax.ShapeDtypeStruct((GRP, 8, HD), jnp.float32)
    q_spec = pl.BlockSpec((TOK, HD), lambda h, sc: (0, sc[0] * GRP + h))
    return pl.pallas_call(
        near_kernel,
        grid_spec=pltpu.PrefetchScalarGridSpec(
            num_scalar_prefetch=1,
            grid=(GRP,),
            in_specs=[
                q_spec,
                q_spec,
                *[pl.BlockSpec((TOK, 2 * HD), lambda h, sc: (0, 0))] * 3,
                pl.BlockSpec(offsets.shape, lambda h, sc: (0, 0)),
            ],
            out_specs=[
                pl.BlockSpec((1, rows, HD), lambda h, sc: (h, 0, 0)),
                pl.BlockSpec((1, 8, HD), lambda h, sc: (h, 0, 0)),
            ],
            scratch_shapes=[
                pltpu.VMEM((3 * TOK, HD), jnp.bfloat16),
                pltpu.VMEM((3 * TOK, 2 * HD), jnp.bfloat16),
                pltpu.VMEM((4, TILE, 2 * HD), jnp.float32),
                pltpu.VMEM((4, TILE, HD), jnp.float32),
            ],
        ),
        out_shape=[state, sums],
        compiler_params=pltpu.CompilerParams(vmem_limit_bytes=40 << 20),
        name="near_attention",
    )(scalars, queries, q_oth, *parts, offsets)


def pack_kernel(sc, lists, keys, values, own_slots, kv_own, sent):
    core, me = sc[0], sc[1]
    group = lax.broadcasted_iota(jnp.int32, lists.shape, 0) // GRP
    table = lists[...]

    def head_of(source, head, rows):
        low, high = source[rows, :HD], source[rows, HD:]
        return jnp.where(head == 0, low, high)

    for head, slots in ((core, own_slots), (1 - core, sent)):
        pick = [jnp.int32(0)] * CAP
        seen = jnp.int32(0)
        for b in range(TOK // BLK):
            hit = jnp.max(jnp.where((group == head) & (table == me * (TOK // BLK) + b), 1, 0))
            for k in range(CAP):
                pick[k] = jnp.where((hit > 0) & (seen == k), b, pick[k])
            seen = seen + hit
        for k in range(CAP):
            rows = pl.ds(pl.multiple_of(pick[k] * BLK, BLK), BLK)
            slots[k * BLK : (k + 1) * BLK, :HD] = head_of(keys, head, rows)
            slots[k * BLK : (k + 1) * BLK, HD:] = head_of(values, head, rows)
    whole = slice(0, TOK)
    for head, target, at in ((core, kv_own, 0), (1 - core, sent, CAP * BLK)):
        target[at : at + TOK, :HD] = head_of(keys, head, whole)
        target[at : at + TOK, HD:] = head_of(values, head, whole)


def pack(scalars, columns, keys, values):
    slots = jax.ShapeDtypeStruct((CAP * BLK, 2 * HD), jnp.bfloat16)
    whole = jax.ShapeDtypeStruct((TOK, 2 * HD), jnp.bfloat16)
    sent = jax.ShapeDtypeStruct((CAP * BLK + TOK, 2 * HD), jnp.bfloat16)

    def full(shape):
        return pl.BlockSpec(shape, lambda i, sc: (0, 0))

    return pl.pallas_call(
        pack_kernel,
        grid_spec=pltpu.PrefetchScalarGridSpec(
            num_scalar_prefetch=1,
            grid=(1,),
            in_specs=[full(columns.shape), full(keys.shape), full(values.shape)],
            out_specs=[full(a.shape) for a in (slots, whole, sent)],
        ),
        out_shape=[slots, whole, sent],
        name="pack_blocks",
    )(scalars, columns, keys, values)


def far_kernel(low, high, sizes, last, sc, q_own, q_oth, o_ref, l_ref, *rest):
    pieces, (out_a, out_b, buf, sem) = rest[: high - low], rest[high - low :]
    h = pl.program_id(0)

    def bound(head, k):
        return sc[FAR_OFF + head * (PIECES + 1) + k]

    def fetch(head, slot):
        base = bound(head, low)
        for k in range(low, high):

            def start(i, _, k=k):
                code = sc[FAR_CODE + head * NV + i]
                pltpu.make_async_copy(
                    pieces[k - low].at[pl.ds(pl.multiple_of(code * BLK, BLK), BLK), :],
                    buf.at[
                        slot, pl.ds(pl.multiple_of((i - base) * BLK, BLK), BLK), pl.ds(0, 2 * HD)
                    ],
                    sem.at[slot],
                ).start()
                return 0

            lax.fori_loop(bound(head, k), bound(head, k + 1), start, 0)

    slot = h % 2

    @pl.when(h == 0)
    def _():
        fetch(0, 0)

    @pl.when(h + 1 < GRP)
    def _():
        fetch(h + 1, 1 - slot)

    n = bound(h, high) - bound(h, low)

    def arrived(i, _):
        pltpu.make_async_copy(
            pieces[0].at[pl.ds(0, BLK), :],
            buf.at[slot, pl.ds(0, BLK), pl.ds(0, 2 * HD)],
            sem.at[slot],
        ).wait()
        return 0

    lax.fori_loop(0, n, arrived, 0)
    buf[slot, :, 2 * HD :] = jnp.ones((NV * BLK, HD), jnp.bfloat16)

    def fill(i, _):
        rows = pl.ds(pl.multiple_of(i * BLK, BLK), BLK)
        buf[slot, rows, :HD] = buf[slot, :BLK, :HD]
        buf[slot, rows, HD:] = jnp.zeros((BLK, 2 * HD), jnp.bfloat16)
        return 0

    wanted = jnp.int32(0)
    for size in sizes[::-1]:
        wanted = jnp.where(n <= size, size, wanted)
    lax.fori_loop(jnp.where(n > 0, n, NV), wanted, fill, 0)

    def put(i, o):
        if last:
            out = (out_a, out_b)[i // 2]
            out[(i % 2) * TILE : (i % 2 + 1) * TILE, :] = o.astype(jnp.bfloat16)
        else:
            out_a[0, i * TILE : (i + 1) * TILE, :] = o

    below = 0
    for size in sizes:

        @pl.when((n > below) & (n <= size))
        def _(size=size):
            keys = size * BLK
            for i in range(4):
                q_ref = (q_own, q_oth)[i // 2]
                s = dot_t(q_ref[(i % 2) * TILE : (i % 2 + 1) * TILE, :], buf[slot, :keys, :HD])
                m = jnp.max(s, axis=1, keepdims=True)
                p = jnp.exp2((s - m) * LOG2).astype(jnp.bfloat16)
                acc = jnp.dot(p, buf[slot, :keys, HD:], preferred_element_type=jnp.float32)
                top = jnp.broadcast_to(m * LOG2, (TILE, HD))
                o, l = o_ref[0, i * TILE : (i + 1) * TILE, :], from_rows(l_ref, i)
                both = jnp.maximum(l, top)
                wn = jnp.exp2(l - both)
                wf = jnp.exp2(top - both)
                weight = wn + acc[:, HD:] * wf
                put(i, (o * wn + acc[:, :HD] * wf) / weight)
                if not last:
                    for k, line in enumerate(to_rows(both + jnp.log2(weight))):
                        out_b[0, 2 * i + k : 2 * i + k + 1, :] = line

        below = size

    @pl.when(n == 0)
    def _():
        for i in range(4):
            put(i, o_ref[0, i * TILE : (i + 1) * TILE, :])
        if not last:
            out_b[...] = l_ref[...]


def far_attention(low, high, sizes, last, scalars, queries, q_oth, o, l, pieces):
    q_spec = pl.BlockSpec((TOK, HD), lambda h, sc: (0, sc[0] * GRP + h))
    state = pl.BlockSpec((1, 2 * TOK, HD), lambda h, sc: (h, 0, 0))
    sums = pl.BlockSpec((1, 8, HD), lambda h, sc: (h, 0, 0))
    flat = pl.BlockSpec((TOK, HD), lambda h, sc: (0, h))
    if last:
        out_shape = [jax.ShapeDtypeStruct((TOK, GW), jnp.bfloat16)] * 2
    else:
        out_shape = [
            jax.ShapeDtypeStruct((GRP, 2 * TOK, HD), jnp.float32),
            jax.ShapeDtypeStruct((GRP, 8, HD), jnp.float32),
        ]
    return pl.pallas_call(
        functools.partial(far_kernel, low, high, sizes, last),
        grid_spec=pltpu.PrefetchScalarGridSpec(
            num_scalar_prefetch=1,
            grid=(GRP,),
            in_specs=[
                q_spec,
                q_spec,
                state,
                sums,
                *[pl.BlockSpec(memory_space=pl.ANY)] * (high - low),
            ],
            out_specs=[flat, flat] if last else [state, sums],
            scratch_shapes=[
                pltpu.VMEM((2, NV * BLK, 3 * HD), jnp.bfloat16),
                pltpu.SemaphoreType.DMA((2,)),
            ],
        ),
        out_shape=out_shape,
        compiler_params=pltpu.CompilerParams(vmem_limit_bytes=48 << 20),
        name="far_last" if last else "far_first",
    )(scalars, queries, q_oth, o, l, *pieces)


def shards(queries, keys, values, columns, offsets, out_weight):
    me = lax.axis_index("ctx")
    core = me % 2
    half = lax.axis_index("kvh")
    i32 = jnp.int32

    def cut(value, which, width, axis=1):
        return lax.dynamic_slice_in_dim(value, which * width, width, axis)

    own_slots, kv_own, sent = pack(jnp.stack([core, me]).astype(i32), columns, keys, values)
    got = permute(sent, send_core)
    q_oth = permute(queries, send_core)
    slots = CAP * BLK
    kv_oth = got[slots:]
    both = jnp.concatenate([own_slots, got[:slots]], axis=0)
    both, columns = lax.optimization_barrier((both, columns))
    far_y = permute(both, send_y)
    near_scalars, far_scalars = tables(me[None].astype(i32), columns)
    held = jnp.where(core == 1, kv_own, kv_oth)
    kv_before = lax.ppermute(held, "ctx", [(i, i + 2) for i in range(62)])
    pool_a = jnp.concatenate([both[:slots], far_y[:slots]], axis=0)
    pool_b = jnp.concatenate([both[slots:], far_y[slots:]], axis=0)
    pool_a, pool_b, kv_before, q_oth, near_scalars = lax.optimization_barrier(
        (pool_a, pool_b, kv_before, q_oth, near_scalars)
    )
    pool_a = jnp.concatenate(ring(pool_a, send_z), axis=0)
    pool_b = jnp.concatenate(ring(pool_b, send_x), axis=0)
    low_a, high_a = permute(pool_a, send_x(1)), permute(pool_a, send_x(-1))
    low_b, high_b = permute(pool_b, send_z(1)), permute(pool_b, send_z(-1))
    o, l = near_attention(near_scalars, queries, q_oth, (kv_own, kv_oth, kv_before), offsets)
    low_a, high_a, low_b, high_b, o = lax.optimization_barrier((low_a, high_a, low_b, high_b, o))
    middle = pool_a.shape[0] // 2
    second = [
        permute(low_a[:middle], send_x(1)),
        permute(high_a[middle:], send_x(-1)),
        permute(low_b[:middle], send_z(1)),
        permute(high_b[middle:], send_z(-1)),
    ]
    first = [pool_a, low_a, high_a, pool_b, low_b, high_b]
    o, l = far_attention(0, 6, (12, 14, 16), False, far_scalars, queries, q_oth, o, l, first)
    own, oth = far_attention(6, 10, (4, 6, 16), True, far_scalars, queries, q_oth, o, l, second)

    columns_out = out_weight.shape[1] // 2
    weight_kept = cut(out_weight, half, columns_out)
    weight_sent = cut(out_weight, 1 - half, columns_out)
    results = []
    parts = [slice(0, BLK), slice(BLK, TOK)]
    first, others = [permute(oth[rows], send_core) for rows in parts]
    for at in range(0, TOK, BLK):
        rows = slice(at, at + BLK)
        got = first if at == 0 else others[at - BLK : at]
        attended = jnp.where(
            core == 0,
            jnp.concatenate([own[rows], got], 1),
            jnp.concatenate([got, own[rows]], 1),
        )
        sent = jnp.dot(attended, weight_sent, preferred_element_type=jnp.float32)
        taken = permute(sent.astype(jnp.bfloat16), lambda i: 1 - i, "kvh")
        kept = jnp.dot(attended, weight_kept, preferred_element_type=jnp.float32)
        results.append((kept + taken.astype(jnp.float32)).astype(jnp.bfloat16))
    return jnp.concatenate(results, axis=0)


def solution(mesh):
    placed = (
        P("ctx", "kvh"),
        P("ctx", "kvh"),
        P("ctx", "kvh"),
        P("kvh", None),
        P("kvh", None),
        P("kvh", None),
    )
    return jax.shard_map(
        shards, mesh=mesh, in_specs=placed, out_specs=P("ctx", "kvh"), check_vma=False
    )
```

```python
import functools
import math

import jax
import jax.numpy as jnp
from jax import lax
from jax.experimental import pallas as pl
from jax.experimental.pallas import tpu as pltpu
from jax.sharding import PartitionSpec as P

HD = 128
BLK = 128
NV = 16
CAP = 2
WIN = 512
TOK = 512
GRP = 7
GW = GRP * HD
WINB = WIN // BLK
NEG = -1e30
LOG2 = math.log2(math.e) / math.sqrt(HD)


def coords(i):
    return i // 16, i // 4 % 4, i // 2 % 2, i % 2


def index(x, z, y, c):
    return (x % 4) * 16 + (z % 4) * 4 + (y % 2) * 2 + c % 2


def send_x(by):
    def to(i):
        x, z, y, c = coords(i)
        return index(x + by, z, y, c)

    return to


def send_z(by):
    def to(i):
        x, z, y, c = coords(i)
        return index(x, z + by, y, c)

    return to


def send_y(i):
    x, z, y, c = coords(i)
    return index(x, z, y + 1, c)


def send_core(i):
    return i ^ 1


def permute(value, to, axis="ctx"):
    return lax.ppermute(value, axis, [(i, to(i)) for i in range(lax.axis_size(axis))])


def ring(piece, send):
    return [piece] + [permute(piece, send(by)) for by in (1, -1, 2)]


def to_rows(value):
    return [value[k * BLK : (k + 1) * BLK, :].T[0:1, :] for k in range(2)]


def from_rows(ref, i):
    return jnp.concatenate(
        [jnp.broadcast_to(ref[0, 2 * i + k : 2 * i + k + 1, :], (BLK, BLK)).T for k in range(2)], 0
    )


def dot_t(a, b):
    return lax.dot_general(a, b, (((1,), (1,)), ((), ())), preferred_element_type=jnp.float32)


TILE = 2 * BLK
SPAN = WIN + TILE
NEAR_FLAGS = 2
NEAR_EXTRA = NEAR_FLAGS + 8 * GRP
NEAR_SIZE = NEAR_EXTRA + 4 * GRP
PIECES = 10
FAR_OFF = 1 + GRP
FAR_CODE = FAR_OFF + GRP * (PIECES + 1)
FAR_SIZE = FAR_CODE + GRP * NV


def table_kernel(sc, lists, near, far, marks, codes, heads):
    me = sc[0]
    core, chip = me & 1, me >> 1
    x, z, y = chip >> 3, (chip >> 1) & 3, chip & 1
    start = chip * 8
    near[0] = core
    near[1] = (chip == 0).astype(jnp.int32)
    far[0] = core

    def clear(i, _):
        for k in range(4):
            marks[4 * i + k] = 0
        return 0

    lax.fori_loop(0, 64, clear, 0)

    def clear_near(i, _):
        for k in range(8):
            near[NEAR_FLAGS + 8 * i + k] = 0
        for k in range(4):
            near[NEAR_EXTRA + 4 * i + k] = 99
        return 0

    lax.fori_loop(0, GRP, clear_near, 0)

    def mark(h, _):
        for j in range(NV):
            marks[lists[core * GRP + h, j]] = 1
        return 0

    lax.fori_loop(0, GRP, mark, 0)

    def place(step):
        return jnp.where(step == 0, 0, jnp.where(step == 3, 1, step + 1))

    def one_head(h, _):
        for k in range(PIECES):
            heads[k] = 0

        def classify(j, _):
            b = lists[core * GRP + h, j]
            run = b >> 2
            at = b & 3
            base = b - at
            slot = jnp.where(at > 0, marks[base], 0)
            slot = slot + jnp.where(at > 1, marks[base + 1], 0)
            slot = slot + jnp.where(at > 2, marks[base + 2], 0)
            cx = place(((run >> 4) - x) & 3)
            cz = place(((run >> 2) - z) & 3)
            same = (run & 1) == core
            ring = jnp.where(same, cx, cz)
            low = jnp.where(((run >> 1) & 1) == y, 0, 2) + jnp.minimum(slot, 1)
            within = jnp.where(same, cz, cx) * 4 + low
            upper = (ring == 3) & (within > 7)
            piece = jnp.where(
                ring == 3,
                jnp.where(same, 6, 8) + upper.astype(jnp.int32),
                jnp.where(same, 0, 3) + ring,
            )
            within = within - jnp.where(upper, 8, 0)
            far_block = b <= start - 5
            codes[j] = jnp.where(far_block, piece * 16 + within, -1)
            heads[piece] = heads[piece] + far_block.astype(jnp.int32)
            w = b - (start - WINB)

            @pl.when((w >= 0) & (w < 8))
            def _():
                near[NEAR_FLAGS + h * 8 + w] = 1
                pair = NEAR_EXTRA + h * 4 + (w >> 2) * 2
                second = (near[pair] < 99).astype(jnp.int32)
                near[pair + second] = w

            return 0

        lax.fori_loop(0, NV, classify, 0)
        total = jnp.int32(0)
        for k in range(PIECES):
            far[FAR_OFF + h * (PIECES + 1) + k] = total
            held = heads[k]
            heads[k] = total
            total = total + held
        far[FAR_OFF + h * (PIECES + 1) + PIECES] = total
        far[1 + h] = total

        def store(j, _):
            code = codes[j]

            @pl.when(code >= 0)
            def _():
                k = code >> 4
                far[FAR_CODE + h * NV + heads[k]] = code & 15
                heads[k] = heads[k] + 1

            return 0

        lax.fori_loop(0, NV, store, 0)
        return 0

    lax.fori_loop(0, GRP, one_head, 0)


def tables(me, columns):
    smem = pltpu.MemorySpace.SMEM
    return pl.pallas_call(
        table_kernel,
        in_specs=[pl.BlockSpec(memory_space=smem)] * 2,
        out_specs=[pl.BlockSpec(memory_space=smem)] * 2,
        out_shape=[
            jax.ShapeDtypeStruct((NEAR_SIZE,), jnp.int32),
            jax.ShapeDtypeStruct((FAR_SIZE,), jnp.int32),
        ],
        scratch_shapes=[
            pltpu.SMEM((256,), jnp.int32),
            pltpu.SMEM((NV,), jnp.int32),
            pltpu.SMEM((PIECES,), jnp.int32),
        ],
        name="index_tables",
    )(me, columns)


def near_kernel(
    sc, q_own, q_oth, kv_own, kv_oth, kv_before, offs, o_ref, l_ref, kext, vext, acc_s, m_s
):
    h = pl.program_id(0)
    core = sc[0]

    @pl.when(h == 0)
    def _():
        own_at = pl.ds(pl.multiple_of(TOK + core * TOK, TOK), TOK)
        oth_at = pl.ds(pl.multiple_of(2 * TOK - core * TOK, TOK), TOK)
        for at, part in ((own_at, kv_own), (oth_at, kv_oth)):
            kext[at, :] = part[:, :HD]
            vext[at, :HD] = part[:, HD:]

        kext[:TOK, :] = kv_before[:, :HD]
        vext[:TOK, :HD] = kv_before[:, HD:]
        vext[:, HD:] = jnp.ones((vext.shape[0], HD), jnp.bfloat16)

    line = offs[pl.ds(core * GRP + h, 1), :]
    spread = jnp.broadcast_to(line.astype(jnp.float32), (BLK, BLK)).T
    lane = lax.broadcasted_iota(jnp.int32, (BLK, BLK), 1)
    marks = []
    for k in range(SPAN // BLK):
        hit = spread == (WIN - k * BLK - lane).astype(jnp.float32)
        marks.append(jnp.max(jnp.where(hit, 0.0, NEG), axis=0, keepdims=True))
    pattern = jnp.concatenate(marks, axis=1)
    bias = pltpu.roll(
        jnp.broadcast_to(pattern, (TILE, SPAN)), 0, 1, stride=1, stride_axis=0
    )
    rows = lax.broadcasted_iota(jnp.int32, (TILE, TILE), 0)
    lanes = lax.broadcasted_iota(jnp.int32, (TILE, TILE), 1)
    far_side = lanes <= rows
    tile_lane = lax.broadcasted_iota(jnp.int32, (1, TILE), 1)
    span_lane = lax.broadcasted_iota(jnp.int32, (1, SPAN), 1)

    def tile_of(i):
        return 4 * (core if i < 2 else 1 - core) + 2 * (i % 2)

    def q_of(i):
        return (q_own if i < 2 else q_oth)[(i % 2) * TILE : (i % 2 + 1) * TILE, :]

    for i in range(4):
        t = tile_of(i)
        base = pl.multiple_of(t * BLK, BLK)
        s = dot_t(q_of(i), kext[pl.ds(base, SPAN), :])
        flag = NEAR_FLAGS + h * 8 + t
        la = jnp.where(sc[flag] > 0, 0.0, NEG).astype(jnp.float32)
        lb = jnp.where(sc[flag + 1] > 0, 0.0, NEG).astype(jnp.float32)
        first = jnp.where(far_side, jnp.where(tile_lane < BLK, la, lb), bias[:, :TILE])
        absent = jnp.where(sc[1] > 0, BLK * (WINB - t), 0)
        edge = jnp.where(span_lane < absent, NEG, 0.0).astype(jnp.float32)
        s = s + jnp.concatenate([first, bias[:, TILE:]], axis=1) + edge
        m = jnp.max(s, axis=1, keepdims=True)
        p = jnp.exp2((s - m) * LOG2).astype(jnp.bfloat16)
        acc_s[i] = jnp.dot(p, vext[pl.ds(base, SPAN), :], preferred_element_type=jnp.float32)
        m_s[i] = jnp.broadcast_to(m, (TILE, HD))

    ex = NEAR_EXTRA + 4 * h
    lowest = jnp.minimum(jnp.minimum(sc[ex], sc[ex + 1]), jnp.minimum(sc[ex + 2], sc[ex + 3]))

    @pl.when(lowest < 6)
    def _():
        for i in range(4):
            t = tile_of(i)
            for g in range(2):
                wa, wb = sc[ex + 2 * g], sc[ex + 2 * g + 1]

                @pl.when((wa < t) | (wb < t))
                def _():
                    ra = pl.multiple_of(jnp.minimum(wa, 11) * BLK, BLK)
                    rb = pl.multiple_of(jnp.minimum(wb, 11) * BLK, BLK)
                    ks = jnp.concatenate([kext[pl.ds(ra, BLK), :], kext[pl.ds(rb, BLK), :]], 0)
                    vs = jnp.concatenate([vext[pl.ds(ra, BLK), :], vext[pl.ds(rb, BLK), :]], 0)
                    s = dot_t(q_of(i), ks)
                    ba = jnp.where(wa < t, 0.0, NEG).astype(jnp.float32)
                    bb = jnp.where(wb < t, 0.0, NEG).astype(jnp.float32)
                    s = s + jnp.where(tile_lane < BLK, ba, bb)
                    m_old = m_s[i]
                    m_new = jnp.maximum(m_old, jnp.max(s, axis=1, keepdims=True))
                    scale = jnp.exp2((m_old - m_new) * LOG2)
                    p = jnp.exp2((s - jnp.concatenate([m_new, m_new], 1)) * LOG2)
                    acc_s[i] = acc_s[i] * jnp.concatenate([scale, scale], 1) + jnp.dot(
                        p.astype(jnp.bfloat16), vs, preferred_element_type=jnp.float32
                    )
                    m_s[i] = m_new

    for i in range(4):
        total = acc_s[i, :, HD:]
        o_ref[0, i * TILE : (i + 1) * TILE, :] = acc_s[i, :, :HD] / total
        for k, line in enumerate(to_rows(m_s[i] * LOG2 + jnp.log2(total))):
            l_ref[0, 2 * i + k : 2 * i + k + 1, :] = line


def near_attention(scalars, queries, q_oth, parts, offsets):
    rows = 2 * TOK
    state = jax.ShapeDtypeStruct((GRP, rows, HD), jnp.float32)
    sums = jax.ShapeDtypeStruct((GRP, 8, HD), jnp.float32)
    q_spec = pl.BlockSpec((TOK, HD), lambda h, sc: (0, sc[0] * GRP + h))
    return pl.pallas_call(
        near_kernel,
        grid_spec=pltpu.PrefetchScalarGridSpec(
            num_scalar_prefetch=1,
            grid=(GRP,),
            in_specs=[
                q_spec,
                q_spec,
                *[pl.BlockSpec((TOK, 2 * HD), lambda h, sc: (0, 0))] * 3,
                pl.BlockSpec(offsets.shape, lambda h, sc: (0, 0)),
            ],
            out_specs=[
                pl.BlockSpec((1, rows, HD), lambda h, sc: (h, 0, 0)),
                pl.BlockSpec((1, 8, HD), lambda h, sc: (h, 0, 0)),
            ],
            scratch_shapes=[
                pltpu.VMEM((3 * TOK, HD), jnp.bfloat16),
                pltpu.VMEM((3 * TOK, 2 * HD), jnp.bfloat16),
                pltpu.VMEM((4, TILE, 2 * HD), jnp.float32),
                pltpu.VMEM((4, TILE, HD), jnp.float32),
            ],
        ),
        out_shape=[state, sums],
        compiler_params=pltpu.CompilerParams(vmem_limit_bytes=16 << 20),
        name="near_attention",
    )(scalars, queries, q_oth, *parts, offsets)


def pack_kernel(sc, lists, keys, values, own_slots, kv_own, sent):
    core, me = sc[0], sc[1]
    group = lax.broadcasted_iota(jnp.int32, lists.shape, 0) // GRP
    table = lists[...]

    def head_of(source, head, rows):
        low, high = source[rows, :HD], source[rows, HD:]
        return jnp.where(head == 0, low, high)

    for head, slots in ((core, own_slots), (1 - core, sent)):
        pick = [jnp.int32(0)] * CAP
        seen = jnp.int32(0)
        for b in range(TOK // BLK):
            hit = jnp.max(jnp.where((group == head) & (table == me * (TOK // BLK) + b), 1, 0))
            for k in range(CAP):
                pick[k] = jnp.where((hit > 0) & (seen == k), b, pick[k])
            seen = seen + hit
        for k in range(CAP):
            rows = pl.ds(pl.multiple_of(pick[k] * BLK, BLK), BLK)
            slots[k * BLK : (k + 1) * BLK, :HD] = head_of(keys, head, rows)
            slots[k * BLK : (k + 1) * BLK, HD:] = head_of(values, head, rows)
    whole = slice(0, TOK)
    for head, target, at in ((core, kv_own, 0), (1 - core, sent, CAP * BLK)):
        target[at : at + TOK, :HD] = head_of(keys, head, whole)
        target[at : at + TOK, HD:] = head_of(values, head, whole)


def pack(scalars, columns, keys, values):
    slots = jax.ShapeDtypeStruct((CAP * BLK, 2 * HD), jnp.bfloat16)
    whole = jax.ShapeDtypeStruct((TOK, 2 * HD), jnp.bfloat16)
    sent = jax.ShapeDtypeStruct((CAP * BLK + TOK, 2 * HD), jnp.bfloat16)

    def full(shape):
        return pl.BlockSpec(shape, lambda i, sc: (0, 0))

    return pl.pallas_call(
        pack_kernel,
        grid_spec=pltpu.PrefetchScalarGridSpec(
            num_scalar_prefetch=1,
            grid=(1,),
            in_specs=[full(columns.shape), full(keys.shape), full(values.shape)],
            out_specs=[full(a.shape) for a in (slots, whole, sent)],
        ),
        out_shape=[slots, whole, sent],
        name="pack_blocks",
    )(scalars, columns, keys, values)


def far_kernel(low, high, sizes, last, sc, q_own, q_oth, o_ref, l_ref, *rest):
    pieces, (out_a, out_b, buf, sem) = rest[: high - low], rest[high - low :]
    h = pl.program_id(0)

    def bound(head, k):
        return sc[FAR_OFF + head * (PIECES + 1) + k]

    def fetch(head, slot):
        base = bound(head, low)
        for k in range(low, high):

            def start(i, _, k=k):
                code = sc[FAR_CODE + head * NV + i]
                pltpu.make_async_copy(
                    pieces[k - low].at[pl.ds(pl.multiple_of(code * BLK, BLK), BLK), :],
                    buf.at[
                        slot, pl.ds(pl.multiple_of((i - base) * BLK, BLK), BLK), pl.ds(0, 2 * HD)
                    ],
                    sem.at[slot],
                ).start()
                return 0

            lax.fori_loop(bound(head, k), bound(head, k + 1), start, 0)

    slot = h % 2

    @pl.when(h == 0)
    def _():
        fetch(0, 0)

    @pl.when(h + 1 < GRP)
    def _():
        fetch(h + 1, 1 - slot)

    n = bound(h, high) - bound(h, low)

    def arrived(i, _):
        pltpu.make_async_copy(
            pieces[0].at[pl.ds(0, BLK), :],
            buf.at[slot, pl.ds(0, BLK), pl.ds(0, 2 * HD)],
            sem.at[slot],
        ).wait()
        return 0

    lax.fori_loop(0, n, arrived, 0)
    buf[slot, :, 2 * HD :] = jnp.ones((NV * BLK, HD), jnp.bfloat16)

    def fill(i, _):
        rows = pl.ds(pl.multiple_of(i * BLK, BLK), BLK)
        buf[slot, rows, :HD] = buf[slot, :BLK, :HD]
        buf[slot, rows, HD:] = jnp.zeros((BLK, 2 * HD), jnp.bfloat16)
        return 0

    wanted = jnp.int32(0)
    for size in sizes[::-1]:
        wanted = jnp.where(n <= size, size, wanted)
    lax.fori_loop(jnp.where(n > 0, n, NV), wanted, fill, 0)

    def put(i, o):
        if last:
            out = (out_a, out_b)[i // 2]
            out[(i % 2) * TILE : (i % 2 + 1) * TILE, :] = o.astype(jnp.bfloat16)
        else:
            out_a[0, i * TILE : (i + 1) * TILE, :] = o

    below = 0
    for size in sizes:

        @pl.when((n > below) & (n <= size))
        def _(size=size):
            keys = size * BLK
            for i in range(4):
                q_ref = (q_own, q_oth)[i // 2]
                s = dot_t(q_ref[(i % 2) * TILE : (i % 2 + 1) * TILE, :], buf[slot, :keys, :HD])
                m = jnp.max(s, axis=1, keepdims=True)
                p = jnp.exp2((s - m) * LOG2).astype(jnp.bfloat16)
                acc = jnp.dot(p, buf[slot, :keys, HD:], preferred_element_type=jnp.float32)
                top = jnp.broadcast_to(m * LOG2, (TILE, HD))
                o, l = o_ref[0, i * TILE : (i + 1) * TILE, :], from_rows(l_ref, i)
                both = jnp.maximum(l, top)
                wn = jnp.exp2(l - both)
                wf = jnp.exp2(top - both)
                weight = wn + acc[:, HD:] * wf
                put(i, (o * wn + acc[:, :HD] * wf) / weight)
                if not last:
                    for k, line in enumerate(to_rows(both + jnp.log2(weight))):
                        out_b[0, 2 * i + k : 2 * i + k + 1, :] = line

        below = size

    @pl.when(n == 0)
    def _():
        for i in range(4):
            put(i, o_ref[0, i * TILE : (i + 1) * TILE, :])
        if not last:
            out_b[...] = l_ref[...]


def far_attention(low, high, sizes, last, scalars, queries, q_oth, o, l, pieces):
    q_spec = pl.BlockSpec((TOK, HD), lambda h, sc: (0, sc[0] * GRP + h))
    state = pl.BlockSpec((1, 2 * TOK, HD), lambda h, sc: (h, 0, 0))
    sums = pl.BlockSpec((1, 8, HD), lambda h, sc: (h, 0, 0))
    flat = pl.BlockSpec((TOK, HD), lambda h, sc: (0, h))
    if last:
        out_shape = [jax.ShapeDtypeStruct((TOK, GW), jnp.bfloat16)] * 2
    else:
        out_shape = [
            jax.ShapeDtypeStruct((GRP, 2 * TOK, HD), jnp.float32),
            jax.ShapeDtypeStruct((GRP, 8, HD), jnp.float32),
        ]
    return pl.pallas_call(
        functools.partial(far_kernel, low, high, sizes, last),
        grid_spec=pltpu.PrefetchScalarGridSpec(
            num_scalar_prefetch=1,
            grid=(GRP,),
            in_specs=[
                q_spec,
                q_spec,
                state,
                sums,
                *[pl.BlockSpec(memory_space=pl.ANY)] * (high - low),
            ],
            out_specs=[flat, flat] if last else [state, sums],
            scratch_shapes=[
                pltpu.VMEM((2, NV * BLK, 3 * HD), jnp.bfloat16),
                pltpu.SemaphoreType.DMA((2,)),
            ],
        ),
        out_shape=out_shape,
        compiler_params=pltpu.CompilerParams(vmem_limit_bytes=20 << 20),
        name="far_last" if last else "far_first",
    )(scalars, queries, q_oth, o, l, *pieces)


def shards(queries, keys, values, columns, offsets, out_weight):
    me = lax.axis_index("ctx")
    core = me % 2
    half = lax.axis_index("kvh")
    i32 = jnp.int32

    def cut(value, which, width, axis=1):
        return lax.dynamic_slice_in_dim(value, which * width, width, axis)

    own_slots, kv_own, sent = pack(jnp.stack([core, me]).astype(i32), columns, keys, values)
    got = permute(sent, send_core)
    q_oth = permute(queries, send_core)
    slots = CAP * BLK
    kv_oth = got[slots:]
    both = jnp.concatenate([own_slots, got[:slots]], axis=0)
    both, columns = lax.optimization_barrier((both, columns))
    far_y = permute(both, send_y)
    near_scalars, far_scalars = tables(me[None].astype(i32), columns)
    held = jnp.where(core == 1, kv_own, kv_oth)
    kv_before = lax.ppermute(held, "ctx", [(i, i + 2) for i in range(62)])
    pool_a = jnp.concatenate([both[:slots], far_y[:slots]], axis=0)
    pool_b = jnp.concatenate([both[slots:], far_y[slots:]], axis=0)
    pool_a, pool_b, kv_before, q_oth, near_scalars = lax.optimization_barrier(
        (pool_a, pool_b, kv_before, q_oth, near_scalars)
    )
    pool_a = jnp.concatenate(ring(pool_a, send_z), axis=0)
    pool_b = jnp.concatenate(ring(pool_b, send_x), axis=0)
    low_a, high_a = permute(pool_a, send_x(1)), permute(pool_a, send_x(-1))
    low_b, high_b = permute(pool_b, send_z(1)), permute(pool_b, send_z(-1))
    o, l = near_attention(near_scalars, queries, q_oth, (kv_own, kv_oth, kv_before), offsets)
    low_a, high_a, low_b, high_b, o = lax.optimization_barrier((low_a, high_a, low_b, high_b, o))
    middle = pool_a.shape[0] // 2
    second = [
        permute(low_a[:middle], send_x(1)),
        permute(high_a[middle:], send_x(-1)),
        permute(low_b[:middle], send_z(1)),
        permute(high_b[middle:], send_z(-1)),
    ]
    first = [pool_a, low_a, high_a, pool_b, low_b, high_b]
    o, l = far_attention(0, 6, (12, 14, 16), False, far_scalars, queries, q_oth, o, l, first)
    own, oth = far_attention(6, 10, (4, 6, 16), True, far_scalars, queries, q_oth, o, l, second)

    columns_out = out_weight.shape[1] // 2
    weight_kept = cut(out_weight, half, columns_out)
    weight_sent = cut(out_weight, 1 - half, columns_out)
    results = []
    parts = [slice(0, BLK), slice(BLK, TOK)]
    first, others = [permute(oth[rows], send_core) for rows in parts]
    for at in range(0, TOK, BLK):
        rows = slice(at, at + BLK)
        got = first if at == 0 else others[at - BLK : at]
        attended = jnp.where(
            core == 0,
            jnp.concatenate([own[rows], got], 1),
            jnp.concatenate([got, own[rows]], 1),
        )
        sent = jnp.dot(attended, weight_sent, preferred_element_type=jnp.float32)
        taken = permute(sent.astype(jnp.bfloat16), lambda i: 1 - i, "kvh")
        kept = jnp.dot(attended, weight_kept, preferred_element_type=jnp.float32)
        results.append((kept + taken.astype(jnp.float32)).astype(jnp.bfloat16))
    return jnp.concatenate(results, axis=0)


def solution(mesh):
    placed = (
        P("ctx", "kvh"),
        P("ctx", "kvh"),
        P("ctx", "kvh"),
        P("kvh", None),
        P("kvh", None),
        P("kvh", None),
    )
    return jax.shard_map(
        shards, mesh=mesh, in_specs=placed, out_specs=P("ctx", "kvh"), check_vma=False
    )
```

```python
import functools
import math

import jax
import jax.numpy as jnp
from jax import lax
from jax.experimental import pallas as pl
from jax.experimental.pallas import tpu as pltpu
from jax.sharding import PartitionSpec as P

HD = 128
BLK = 128
NV = 16
CAP = 2
WIN = 512
TOK = 512
GRP = 7
GW = GRP * HD
WINB = WIN // BLK
NEG = -1e30
LOG2 = math.log2(math.e) / math.sqrt(HD)


def coords(i):
    return i // 16, i // 4 % 4, i // 2 % 2, i % 2


def index(x, z, y, c):
    return (x % 4) * 16 + (z % 4) * 4 + (y % 2) * 2 + c % 2


def send_x(by):
    def to(i):
        x, z, y, c = coords(i)
        return index(x + by, z, y, c)

    return to


def send_z(by):
    def to(i):
        x, z, y, c = coords(i)
        return index(x, z + by, y, c)

    return to


def send_y(i):
    x, z, y, c = coords(i)
    return index(x, z, y + 1, c)


def send_core(i):
    return i ^ 1


def permute(value, to, axis="ctx"):
    return lax.ppermute(value, axis, [(i, to(i)) for i in range(lax.axis_size(axis))])


def ring(piece, send):
    return [piece] + [permute(piece, send(by)) for by in (1, -1, 2)]


def to_rows(value):
    return [value[k * BLK : (k + 1) * BLK, :].T[0:1, :] for k in range(2)]


def from_rows(ref, i):
    return jnp.concatenate(
        [jnp.broadcast_to(ref[0, 2 * i + k : 2 * i + k + 1, :], (BLK, BLK)).T for k in range(2)], 0
    )


def dot_t(a, b):
    return lax.dot_general(a, b, (((1,), (1,)), ((), ())), preferred_element_type=jnp.float32)


TILE = 2 * BLK
SPAN = WIN + TILE
NEAR_FLAGS = 2
NEAR_EXTRA = NEAR_FLAGS + 8 * GRP
NEAR_SIZE = NEAR_EXTRA + 4 * GRP
PIECES = 10
FAR_OFF = 1 + GRP
FAR_CODE = FAR_OFF + GRP * (PIECES + 1)
FAR_SIZE = FAR_CODE + GRP * NV


def table_kernel(sc, lists, near, far, marks, codes, heads):
    me = sc[0]
    core, chip = me & 1, me >> 1
    x, z, y = chip >> 3, (chip >> 1) & 3, chip & 1
    start = chip * 8
    near[0] = core
    near[1] = (chip == 0).astype(jnp.int32)
    far[0] = core

    def clear(i, _):
        for k in range(4):
            marks[4 * i + k] = 0
        return 0

    lax.fori_loop(0, 64, clear, 0)

    def clear_near(i, _):
        for k in range(8):
            near[NEAR_FLAGS + 8 * i + k] = 0
        for k in range(4):
            near[NEAR_EXTRA + 4 * i + k] = 99
        return 0

    lax.fori_loop(0, GRP, clear_near, 0)

    def mark(h, _):
        for j in range(NV):
            marks[lists[core * GRP + h, j]] = 1
        return 0

    lax.fori_loop(0, GRP, mark, 0)

    def place(step):
        return jnp.where(step == 0, 0, jnp.where(step == 3, 1, step + 1))

    def one_head(h, _):
        for k in range(PIECES):
            heads[k] = 0

        def classify(j, _):
            b = lists[core * GRP + h, j]
            run = b >> 2
            at = b & 3
            base = b - at
            slot = jnp.where(at > 0, marks[base], 0)
            slot = slot + jnp.where(at > 1, marks[base + 1], 0)
            slot = slot + jnp.where(at > 2, marks[base + 2], 0)
            cx = place(((run >> 4) - x) & 3)
            cz = place(((run >> 2) - z) & 3)
            same = (run & 1) == core
            ring = jnp.where(same, cx, cz)
            low = jnp.where(((run >> 1) & 1) == y, 0, 2) + jnp.minimum(slot, 1)
            within = jnp.where(same, cz, cx) * 4 + low
            upper = (ring == 3) & (within > 7)
            piece = jnp.where(
                ring == 3,
                jnp.where(same, 6, 8) + upper.astype(jnp.int32),
                jnp.where(same, 0, 3) + ring,
            )
            within = within - jnp.where(upper, 8, 0)
            far_block = b <= start - 5
            codes[j] = jnp.where(far_block, piece * 16 + within, -1)
            heads[piece] = heads[piece] + far_block.astype(jnp.int32)
            w = b - (start - WINB)

            @pl.when((w >= 0) & (w < 8))
            def _():
                near[NEAR_FLAGS + h * 8 + w] = 1
                pair = NEAR_EXTRA + h * 4 + (w >> 2) * 2
                second = (near[pair] < 99).astype(jnp.int32)
                near[pair + second] = w

            return 0

        lax.fori_loop(0, NV, classify, 0)
        total = jnp.int32(0)
        for k in range(PIECES):
            far[FAR_OFF + h * (PIECES + 1) + k] = total
            held = heads[k]
            heads[k] = total
            total = total + held
        far[FAR_OFF + h * (PIECES + 1) + PIECES] = total
        far[1 + h] = total

        def store(j, _):
            code = codes[j]

            @pl.when(code >= 0)
            def _():
                k = code >> 4
                far[FAR_CODE + h * NV + heads[k]] = code & 15
                heads[k] = heads[k] + 1

            return 0

        lax.fori_loop(0, NV, store, 0)
        return 0

    lax.fori_loop(0, GRP, one_head, 0)


def tables(me, columns):
    smem = pltpu.MemorySpace.SMEM
    return pl.pallas_call(
        table_kernel,
        in_specs=[pl.BlockSpec(memory_space=smem)] * 2,
        out_specs=[pl.BlockSpec(memory_space=smem)] * 2,
        out_shape=[
            jax.ShapeDtypeStruct((NEAR_SIZE,), jnp.int32),
            jax.ShapeDtypeStruct((FAR_SIZE,), jnp.int32),
        ],
        scratch_shapes=[
            pltpu.SMEM((256,), jnp.int32),
            pltpu.SMEM((NV,), jnp.int32),
            pltpu.SMEM((PIECES,), jnp.int32),
        ],
        name="index_tables",
    )(me, columns)


def near_kernel(
    sc, q_own, q_oth, kv_own, kv_oth, kv_before, offs, o_ref, l_ref, kext, vext, acc_s, m_s
):
    h = pl.program_id(0)
    core = sc[0]

    @pl.when(h == 0)
    def _():
        own_at = pl.ds(pl.multiple_of(TOK + core * TOK, TOK), TOK)
        oth_at = pl.ds(pl.multiple_of(2 * TOK - core * TOK, TOK), TOK)
        for at, part in ((own_at, kv_own), (oth_at, kv_oth)):
            kext[at, :] = part[:, :HD]
            vext[at, :HD] = part[:, HD:]

        kext[:TOK, :] = kv_before[:, :HD]
        vext[:TOK, :HD] = kv_before[:, HD:]
        vext[:, HD:] = jnp.ones((vext.shape[0], HD), jnp.bfloat16)

    line = offs[pl.ds(core * GRP + h, 1), :]
    spread = jnp.broadcast_to(line.astype(jnp.float32), (BLK, BLK)).T
    lane = lax.broadcasted_iota(jnp.int32, (BLK, BLK), 1)
    marks = []
    for k in range(SPAN // BLK):
        hit = spread == (WIN - k * BLK - lane).astype(jnp.float32)
        marks.append(jnp.max(jnp.where(hit, 0.0, NEG), axis=0, keepdims=True))
    pattern = jnp.concatenate(marks, axis=1)
    bias = pltpu.roll(
        jnp.broadcast_to(pattern, (TILE, SPAN)), 0, 1, stride=1, stride_axis=0
    )
    rows = lax.broadcasted_iota(jnp.int32, (TILE, TILE), 0)
    lanes = lax.broadcasted_iota(jnp.int32, (TILE, TILE), 1)
    far_side = lanes <= rows
    tile_lane = lax.broadcasted_iota(jnp.int32, (1, TILE), 1)
    span_lane = lax.broadcasted_iota(jnp.int32, (1, SPAN), 1)

    def tile_of(i):
        return 4 * (core if i < 2 else 1 - core) + 2 * (i % 2)

    def q_of(i):
        return (q_own if i < 2 else q_oth)[(i % 2) * TILE : (i % 2 + 1) * TILE, :]

    for i in range(4):
        t = tile_of(i)
        base = pl.multiple_of(t * BLK, BLK)
        s = dot_t(q_of(i), kext[pl.ds(base, SPAN), :])
        flag = NEAR_FLAGS + h * 8 + t
        la = jnp.where(sc[flag] > 0, 0.0, NEG).astype(jnp.float32)
        lb = jnp.where(sc[flag + 1] > 0, 0.0, NEG).astype(jnp.float32)
        first = jnp.where(far_side, jnp.where(tile_lane < BLK, la, lb), bias[:, :TILE])
        absent = jnp.where(sc[1] > 0, BLK * (WINB - t), 0)
        edge = jnp.where(span_lane < absent, NEG, 0.0).astype(jnp.float32)
        s = s + jnp.concatenate([first, bias[:, TILE:]], axis=1) + edge
        m = jnp.max(s, axis=1, keepdims=True)
        p = jnp.exp2((s - m) * LOG2).astype(jnp.bfloat16)
        acc_s[i] = jnp.dot(p, vext[pl.ds(base, SPAN), :], preferred_element_type=jnp.float32)
        m_s[i] = jnp.broadcast_to(m, (TILE, HD))

    ex = NEAR_EXTRA + 4 * h
    lowest = jnp.minimum(jnp.minimum(sc[ex], sc[ex + 1]), jnp.minimum(sc[ex + 2], sc[ex + 3]))

    @pl.when(lowest < 6)
    def _():
        for i in range(4):
            t = tile_of(i)
            for g in range(2):
                wa, wb = sc[ex + 2 * g], sc[ex + 2 * g + 1]

                @pl.when((wa < t) | (wb < t))
                def _():
                    ra = pl.multiple_of(jnp.minimum(wa, 11) * BLK, BLK)
                    rb = pl.multiple_of(jnp.minimum(wb, 11) * BLK, BLK)
                    ks = jnp.concatenate([kext[pl.ds(ra, BLK), :], kext[pl.ds(rb, BLK), :]], 0)
                    vs = jnp.concatenate([vext[pl.ds(ra, BLK), :], vext[pl.ds(rb, BLK), :]], 0)
                    s = dot_t(q_of(i), ks)
                    ba = jnp.where(wa < t, 0.0, NEG).astype(jnp.float32)
                    bb = jnp.where(wb < t, 0.0, NEG).astype(jnp.float32)
                    s = s + jnp.where(tile_lane < BLK, ba, bb)
                    m_old = m_s[i]
                    m_new = jnp.maximum(m_old, jnp.max(s, axis=1, keepdims=True))
                    scale = jnp.exp2((m_old - m_new) * LOG2)
                    p = jnp.exp2((s - jnp.concatenate([m_new, m_new], 1)) * LOG2)
                    acc_s[i] = acc_s[i] * jnp.concatenate([scale, scale], 1) + jnp.dot(
                        p.astype(jnp.bfloat16), vs, preferred_element_type=jnp.float32
                    )
                    m_s[i] = m_new

    for i in range(4):
        total = acc_s[i, :, HD:]
        o_ref[0, i * TILE : (i + 1) * TILE, :] = acc_s[i, :, :HD] / total
        for k, line in enumerate(to_rows(m_s[i] * LOG2 + jnp.log2(total))):
            l_ref[0, 2 * i + k : 2 * i + k + 1, :] = line


def near_attention(scalars, queries, q_oth, parts, offsets):
    rows = 2 * TOK
    state = jax.ShapeDtypeStruct((GRP, rows, HD), jnp.float32)
    sums = jax.ShapeDtypeStruct((GRP, 8, HD), jnp.float32)
    q_spec = pl.BlockSpec((TOK, HD), lambda h, sc: (0, sc[0] * GRP + h))
    return pl.pallas_call(
        near_kernel,
        grid_spec=pltpu.PrefetchScalarGridSpec(
            num_scalar_prefetch=1,
            grid=(GRP,),
            in_specs=[
                q_spec,
                q_spec,
                *[pl.BlockSpec((TOK, 2 * HD), lambda h, sc: (0, 0))] * 3,
                pl.BlockSpec(offsets.shape, lambda h, sc: (0, 0)),
            ],
            out_specs=[
                pl.BlockSpec((1, rows, HD), lambda h, sc: (h, 0, 0)),
                pl.BlockSpec((1, 8, HD), lambda h, sc: (h, 0, 0)),
            ],
            scratch_shapes=[
                pltpu.VMEM((3 * TOK, HD), jnp.bfloat16),
                pltpu.VMEM((3 * TOK, 2 * HD), jnp.bfloat16),
                pltpu.VMEM((4, TILE, 2 * HD), jnp.float32),
                pltpu.VMEM((4, TILE, HD), jnp.float32),
            ],
        ),
        out_shape=[state, sums],
        compiler_params=pltpu.CompilerParams(vmem_limit_bytes=40 << 20),
        name="near_attention",
    )(scalars, queries, q_oth, *parts, offsets)


def pack_kernel(sc, lists, keys, values, own_slots, kv_own, sent):
    core, me = sc[0], sc[1]
    group = lax.broadcasted_iota(jnp.int32, lists.shape, 0) // GRP
    table = lists[...]

    def head_of(source, head, rows):
        low, high = source[rows, :HD], source[rows, HD:]
        return jnp.where(head == 0, low, high)

    for head, slots in ((core, own_slots), (1 - core, sent)):
        pick = [jnp.int32(0)] * CAP
        seen = jnp.int32(0)
        for b in range(TOK // BLK):
            hit = jnp.max(jnp.where((group == head) & (table == me * (TOK // BLK) + b), 1, 0))
            for k in range(CAP):
                pick[k] = jnp.where((hit > 0) & (seen == k), b, pick[k])
            seen = seen + hit
        for k in range(CAP):
            rows = pl.ds(pl.multiple_of(pick[k] * BLK, BLK), BLK)
            slots[k * BLK : (k + 1) * BLK, :HD] = head_of(keys, head, rows)
            slots[k * BLK : (k + 1) * BLK, HD:] = head_of(values, head, rows)
    whole = slice(0, TOK)
    for head, target, at in ((core, kv_own, 0), (1 - core, sent, CAP * BLK)):
        target[at : at + TOK, :HD] = head_of(keys, head, whole)
        target[at : at + TOK, HD:] = head_of(values, head, whole)


def pack(scalars, columns, keys, values):
    slots = jax.ShapeDtypeStruct((CAP * BLK, 2 * HD), jnp.bfloat16)
    whole = jax.ShapeDtypeStruct((TOK, 2 * HD), jnp.bfloat16)
    sent = jax.ShapeDtypeStruct((CAP * BLK + TOK, 2 * HD), jnp.bfloat16)

    def full(shape):
        return pl.BlockSpec(shape, lambda i, sc: (0, 0))

    return pl.pallas_call(
        pack_kernel,
        grid_spec=pltpu.PrefetchScalarGridSpec(
            num_scalar_prefetch=1,
            grid=(1,),
            in_specs=[full(columns.shape), full(keys.shape), full(values.shape)],
            out_specs=[full(a.shape) for a in (slots, whole, sent)],
        ),
        out_shape=[slots, whole, sent],
        name="pack_blocks",
    )(scalars, columns, keys, values)


def far_kernel(low, high, sizes, part, sc, q_own, q_oth, oa, ob, l_ref, *rest):
    pieces, (out_a, out_b, buf, sem) = rest[: high - low], rest[high - low :]
    last = part is not None
    whole = slice(0, TILE)
    if last:
        tiles = [(part, q_own, whole, oa, whole), (2 + part, q_oth, whole, ob, whole)]
    else:
        tiles = []
        for i in range(4):
            rows = slice((i % 2) * TILE, (i % 2 + 1) * TILE)
            tiles.append((i, (q_own, q_oth)[i // 2], rows, (oa, ob)[i // 2], rows))
    h = pl.program_id(0)

    def bound(head, k):
        return sc[FAR_OFF + head * (PIECES + 1) + k]

    def fetch(head, slot):
        base = bound(head, low)
        for k in range(low, high):

            def start(i, _, k=k):
                code = sc[FAR_CODE + head * NV + i]
                pltpu.make_async_copy(
                    pieces[k - low].at[pl.ds(pl.multiple_of(code * BLK, BLK), BLK), :],
                    buf.at[
                        slot, pl.ds(pl.multiple_of((i - base) * BLK, BLK), BLK), pl.ds(0, 2 * HD)
                    ],
                    sem.at[slot],
                ).start()
                return 0

            lax.fori_loop(bound(head, k), bound(head, k + 1), start, 0)

    slot = h % 2

    @pl.when(h == 0)
    def _():
        fetch(0, 0)

    @pl.when(h + 1 < GRP)
    def _():
        fetch(h + 1, 1 - slot)

    n = bound(h, high) - bound(h, low)

    def arrived(i, _):
        pltpu.make_async_copy(
            pieces[0].at[pl.ds(0, BLK), :],
            buf.at[slot, pl.ds(0, BLK), pl.ds(0, 2 * HD)],
            sem.at[slot],
        ).wait()
        return 0

    lax.fori_loop(0, n, arrived, 0)
    buf[slot, :, 2 * HD :] = jnp.ones((NV * BLK, HD), jnp.bfloat16)

    def fill(i, _):
        rows = pl.ds(pl.multiple_of(i * BLK, BLK), BLK)
        buf[slot, rows, :HD] = buf[slot, :BLK, :HD]
        buf[slot, rows, HD:] = jnp.zeros((BLK, 2 * HD), jnp.bfloat16)
        return 0

    wanted = jnp.int32(0)
    for size in sizes[::-1]:
        wanted = jnp.where(n <= size, size, wanted)
    lax.fori_loop(jnp.where(n > 0, n, NV), wanted, fill, 0)

    def put(i, o):
        if last:
            (out_a, out_b)[i // 2][...] = o.astype(jnp.bfloat16)
        else:
            out_a[0, i * TILE : (i + 1) * TILE, :] = o

    below = 0
    for size in sizes:

        @pl.when((n > below) & (n <= size))
        def _(size=size):
            keys = size * BLK
            for i, q_ref, q_rows, o_ref, o_rows in tiles:
                s = dot_t(q_ref[q_rows, :], buf[slot, :keys, :HD])
                m = jnp.max(s, axis=1, keepdims=True)
                p = jnp.exp2((s - m) * LOG2).astype(jnp.bfloat16)
                acc = jnp.dot(p, buf[slot, :keys, HD:], preferred_element_type=jnp.float32)
                top = jnp.broadcast_to(m * LOG2, (TILE, HD))
                o, l = o_ref[0, o_rows, :], from_rows(l_ref, i)
                both = jnp.maximum(l, top)
                wn = jnp.exp2(l - both)
                wf = jnp.exp2(top - both)
                weight = wn + acc[:, HD:] * wf
                put(i, (o * wn + acc[:, :HD] * wf) / weight)
                if not last:
                    for k, line in enumerate(to_rows(both + jnp.log2(weight))):
                        out_b[0, 2 * i + k : 2 * i + k + 1, :] = line

        below = size

    @pl.when(n == 0)
    def _():
        for i, _, _, o_ref, o_rows in tiles:
            put(i, o_ref[0, o_rows, :])
        if not last:
            out_b[...] = l_ref[...]


def far_attention(low, high, sizes, part, scalars, queries, q_oth, o, l, pieces):
    last = part is not None
    rows = TILE if last else TOK
    at = part if last else 0
    q_spec = pl.BlockSpec((rows, HD), lambda h, sc: (at, sc[0] * GRP + h))
    own = pl.BlockSpec((1, rows, HD), lambda h, sc: (h, at, 0))
    oth = pl.BlockSpec((1, rows, HD), lambda h, sc: (h, TOK // rows + at, 0))
    state = pl.BlockSpec((1, 2 * TOK, HD), lambda h, sc: (h, 0, 0))
    sums = pl.BlockSpec((1, 8, HD), lambda h, sc: (h, 0, 0))
    flat = pl.BlockSpec((rows, HD), lambda h, sc: (0, h))
    if last:
        out_shape = [jax.ShapeDtypeStruct((rows, GW), jnp.bfloat16)] * 2
    else:
        out_shape = [
            jax.ShapeDtypeStruct((GRP, 2 * TOK, HD), jnp.float32),
            jax.ShapeDtypeStruct((GRP, 8, HD), jnp.float32),
        ]
    return pl.pallas_call(
        functools.partial(far_kernel, low, high, sizes, part),
        grid_spec=pltpu.PrefetchScalarGridSpec(
            num_scalar_prefetch=1,
            grid=(GRP,),
            in_specs=[
                q_spec,
                q_spec,
                own,
                oth,
                sums,
                *[pl.BlockSpec(memory_space=pl.ANY)] * (high - low),
            ],
            out_specs=[flat, flat] if last else [state, sums],
            scratch_shapes=[
                pltpu.VMEM((2, NV * BLK, 3 * HD), jnp.bfloat16),
                pltpu.SemaphoreType.DMA((2,)),
            ],
        ),
        out_shape=out_shape,
        compiler_params=pltpu.CompilerParams(vmem_limit_bytes=48 << 20),
        name="far_last" if last else "far_first",
    )(scalars, queries, q_oth, o, o, l, *pieces)


def shards(queries, keys, values, columns, offsets, out_weight):
    me = lax.axis_index("ctx")
    core = me % 2
    half = lax.axis_index("kvh")
    i32 = jnp.int32

    def cut(value, which, width, axis=1):
        return lax.dynamic_slice_in_dim(value, which * width, width, axis)

    own_slots, kv_own, sent = pack(jnp.stack([core, me]).astype(i32), columns, keys, values)
    got = permute(sent, send_core)
    q_oth = permute(queries, send_core)
    slots = CAP * BLK
    kv_oth = got[slots:]
    both = jnp.concatenate([own_slots, got[:slots]], axis=0)
    both, columns = lax.optimization_barrier((both, columns))
    far_y = permute(both, send_y)
    near_scalars, far_scalars = tables(me[None].astype(i32), columns)
    held = jnp.where(core == 1, kv_own, kv_oth)
    kv_before = lax.ppermute(held, "ctx", [(i, i + 2) for i in range(62)])
    pool_a = jnp.concatenate([both[:slots], far_y[:slots]], axis=0)
    pool_b = jnp.concatenate([both[slots:], far_y[slots:]], axis=0)
    pool_a, pool_b, kv_before, q_oth, near_scalars = lax.optimization_barrier(
        (pool_a, pool_b, kv_before, q_oth, near_scalars)
    )
    pool_a = jnp.concatenate(ring(pool_a, send_z), axis=0)
    pool_b = jnp.concatenate(ring(pool_b, send_x), axis=0)
    low_a, high_a = permute(pool_a, send_x(1)), permute(pool_a, send_x(-1))
    low_b, high_b = permute(pool_b, send_z(1)), permute(pool_b, send_z(-1))
    o, l = near_attention(near_scalars, queries, q_oth, (kv_own, kv_oth, kv_before), offsets)
    low_a, high_a, low_b, high_b, o = lax.optimization_barrier((low_a, high_a, low_b, high_b, o))
    middle = pool_a.shape[0] // 2
    second = [
        permute(low_a[:middle], send_x(1)),
        permute(high_a[middle:], send_x(-1)),
        permute(low_b[:middle], send_z(1)),
        permute(high_b[middle:], send_z(-1)),
    ]
    first = [pool_a, low_a, high_a, pool_b, low_b, high_b]
    o, l = far_attention(
        0, 6, (12, 16), None, far_scalars, queries, q_oth, o, l, first
    )

    columns_out = out_weight.shape[1] // 2
    weight_kept = cut(out_weight, half, columns_out)
    weight_sent = cut(out_weight, 1 - half, columns_out)
    results = []
    for part in range(2):
        own, oth = far_attention(
            6, 10, (4, 6, 16), part, far_scalars, queries, q_oth, o, l, second
        )
        if part == 1:
            oth, own, taken = lax.optimization_barrier((oth, own, results[0][1]))
            results[0] = (results[0][0], taken)
        got = permute(oth, send_core)
        attended = jnp.where(
            core == 0, jnp.concatenate([own, got], 1), jnp.concatenate([got, own], 1)
        )
        for at in (0, BLK):
            rows = attended[at : at + BLK]
            sent = jnp.dot(rows, weight_sent, preferred_element_type=jnp.float32)
            sent = sent.astype(jnp.bfloat16)
            if part == 0 and at > 0:
                sent, far_scalars = lax.optimization_barrier((sent, far_scalars))
            results.append((rows, permute(sent, lambda i: 1 - i, "kvh")))
    results = [
        (
            jnp.dot(rows, weight_kept, preferred_element_type=jnp.float32)
            + taken.astype(jnp.float32)
        ).astype(jnp.bfloat16)
        for rows, taken in results
    ]
    return jnp.concatenate(results, axis=0)


def solution(mesh):
    placed = (
        P("ctx", "kvh"),
        P("ctx", "kvh"),
        P("ctx", "kvh"),
        P("kvh", None),
        P("kvh", None),
        P("kvh", None),
    )
    return jax.shard_map(
        shards, mesh=mesh, in_specs=placed, out_specs=P("ctx", "kvh"), check_vma=False
    )
```

```python
import functools
import math

import jax
import jax.numpy as jnp
from jax import lax
from jax.experimental import pallas as pl
from jax.experimental.pallas import tpu as pltpu
from jax.sharding import PartitionSpec as P

HD = 128
BLK = 128
NV = 16
CAP = 2
WIN = 512
TOK = 512
GRP = 7
GW = GRP * HD
WINB = WIN // BLK
NEG = -1e30
LOG2 = math.log2(math.e) / math.sqrt(HD)


def coords(i):
    return i // 16, i // 4 % 4, i // 2 % 2, i % 2


def index(x, z, y, c):
    return (x % 4) * 16 + (z % 4) * 4 + (y % 2) * 2 + c % 2


def send_x(by):
    def to(i):
        x, z, y, c = coords(i)
        return index(x + by, z, y, c)

    return to


def send_z(by):
    def to(i):
        x, z, y, c = coords(i)
        return index(x, z + by, y, c)

    return to


def send_y(i):
    x, z, y, c = coords(i)
    return index(x, z, y + 1, c)


def send_core(i):
    return i ^ 1


def permute(value, to, axis="ctx"):
    return lax.ppermute(value, axis, [(i, to(i)) for i in range(lax.axis_size(axis))])


def ring(piece, send):
    return [piece] + [permute(piece, send(by)) for by in (1, -1, 2)]


def to_rows(value):
    return [value[k * BLK : (k + 1) * BLK, :].T[0:1, :] for k in range(2)]


def from_rows(ref, i):
    return jnp.concatenate(
        [jnp.broadcast_to(ref[0, 2 * i + k : 2 * i + k + 1, :], (BLK, BLK)).T for k in range(2)], 0
    )


def dot_t(a, b):
    return lax.dot_general(a, b, (((1,), (1,)), ((), ())), preferred_element_type=jnp.float32)


TILE = 2 * BLK
SPAN = WIN + TILE
NEAR_FLAGS = 2
NEAR_EXTRA = NEAR_FLAGS + 8 * GRP
NEAR_SIZE = NEAR_EXTRA + 4 * GRP
PIECES = 10
FAR_OFF = 1 + GRP
FAR_CODE = FAR_OFF + GRP * (PIECES + 1)
FAR_SIZE = FAR_CODE + GRP * NV


def table_kernel(sc, lists, near, far, marks, codes, heads):
    me = sc[0]
    core, chip = me & 1, me >> 1
    x, z, y = chip >> 3, (chip >> 1) & 3, chip & 1
    start = chip * 8
    near[0] = core
    near[1] = (chip == 0).astype(jnp.int32)
    far[0] = core

    def clear(i, _):
        for k in range(4):
            marks[4 * i + k] = 0
        return 0

    lax.fori_loop(0, 64, clear, 0)

    def clear_near(i, _):
        for k in range(8):
            near[NEAR_FLAGS + 8 * i + k] = 0
        for k in range(4):
            near[NEAR_EXTRA + 4 * i + k] = 99
        return 0

    lax.fori_loop(0, GRP, clear_near, 0)

    def mark(h, _):
        for j in range(NV):
            marks[lists[core * GRP + h, j]] = 1
        return 0

    lax.fori_loop(0, GRP, mark, 0)

    def place(step):
        return jnp.where(step == 0, 0, jnp.where(step == 3, 1, step + 1))

    def one_head(h, _):
        for k in range(PIECES):
            heads[k] = 0

        def classify(j, _):
            b = lists[core * GRP + h, j]
            run = b >> 2
            at = b & 3
            base = b - at
            slot = jnp.where(at > 0, marks[base], 0)
            slot = slot + jnp.where(at > 1, marks[base + 1], 0)
            slot = slot + jnp.where(at > 2, marks[base + 2], 0)
            cx = place(((run >> 4) - x) & 3)
            cz = place(((run >> 2) - z) & 3)
            same = (run & 1) == core
            ring = jnp.where(same, cx, cz)
            low = jnp.where(((run >> 1) & 1) == y, 0, 2) + jnp.minimum(slot, 1)
            within = jnp.where(same, cz, cx) * 4 + low
            upper = (ring == 3) & (within > 7)
            piece = jnp.where(
                ring == 3,
                jnp.where(same, 6, 8) + upper.astype(jnp.int32),
                jnp.where(same, 0, 3) + ring,
            )
            within = within - jnp.where(upper, 8, 0)
            far_block = b <= start - 5
            codes[j] = jnp.where(far_block, piece * 16 + within, -1)
            heads[piece] = heads[piece] + far_block.astype(jnp.int32)
            w = b - (start - WINB)

            @pl.when((w >= 0) & (w < 8))
            def _():
                near[NEAR_FLAGS + h * 8 + w] = 1
                pair = NEAR_EXTRA + h * 4 + (w >> 2) * 2
                second = (near[pair] < 99).astype(jnp.int32)
                near[pair + second] = w

            return 0

        lax.fori_loop(0, NV, classify, 0)
        total = jnp.int32(0)
        for k in range(PIECES):
            far[FAR_OFF + h * (PIECES + 1) + k] = total
            held = heads[k]
            heads[k] = total
            total = total + held
        far[FAR_OFF + h * (PIECES + 1) + PIECES] = total
        far[1 + h] = total

        def store(j, _):
            code = codes[j]

            @pl.when(code >= 0)
            def _():
                k = code >> 4
                far[FAR_CODE + h * NV + heads[k]] = code & 15
                heads[k] = heads[k] + 1

            return 0

        lax.fori_loop(0, NV, store, 0)
        return 0

    lax.fori_loop(0, GRP, one_head, 0)


def tables(me, columns):
    smem = pltpu.MemorySpace.SMEM
    return pl.pallas_call(
        table_kernel,
        in_specs=[pl.BlockSpec(memory_space=smem)] * 2,
        out_specs=[pl.BlockSpec(memory_space=smem)] * 2,
        out_shape=[
            jax.ShapeDtypeStruct((NEAR_SIZE,), jnp.int32),
            jax.ShapeDtypeStruct((FAR_SIZE,), jnp.int32),
        ],
        scratch_shapes=[
            pltpu.SMEM((256,), jnp.int32),
            pltpu.SMEM((NV,), jnp.int32),
            pltpu.SMEM((PIECES,), jnp.int32),
        ],
        name="index_tables",
    )(me, columns)


def near_kernel(
    sc, q_own, q_oth, kv_own, kv_oth, kv_before, offs, o_ref, l_ref, kext, vext, acc_s, m_s
):
    h = pl.program_id(0)
    core = sc[0]

    @pl.when(h == 0)
    def _():
        own_at = pl.ds(pl.multiple_of(TOK + core * TOK, TOK), TOK)
        oth_at = pl.ds(pl.multiple_of(2 * TOK - core * TOK, TOK), TOK)
        for at, part in ((own_at, kv_own), (oth_at, kv_oth)):
            kext[at, :] = part[:, :HD]
            vext[at, :HD] = part[:, HD:]

        kext[:TOK, :] = kv_before[:, :HD]
        vext[:TOK, :HD] = kv_before[:, HD:]
        vext[:, HD:] = jnp.ones((vext.shape[0], HD), jnp.bfloat16)

    line = offs[pl.ds(core * GRP + h, 1), :]
    spread = jnp.broadcast_to(line.astype(jnp.float32), (BLK, BLK)).T
    lane = lax.broadcasted_iota(jnp.int32, (BLK, BLK), 1)
    marks = []
    for k in range(SPAN // BLK):
        hit = spread == (WIN - k * BLK - lane).astype(jnp.float32)
        marks.append(jnp.max(jnp.where(hit, 0.0, NEG), axis=0, keepdims=True))
    pattern = jnp.concatenate(marks, axis=1)
    bias = pltpu.roll(
        jnp.broadcast_to(pattern, (TILE, SPAN)), 0, 1, stride=1, stride_axis=0
    )
    rows = lax.broadcasted_iota(jnp.int32, (TILE, TILE), 0)
    lanes = lax.broadcasted_iota(jnp.int32, (TILE, TILE), 1)
    far_side = lanes <= rows
    tile_lane = lax.broadcasted_iota(jnp.int32, (1, TILE), 1)
    span_lane = lax.broadcasted_iota(jnp.int32, (1, SPAN), 1)

    def tile_of(i):
        return 4 * (core if i < 2 else 1 - core) + 2 * (i % 2)

    def q_of(i):
        return (q_own if i < 2 else q_oth)[(i % 2) * TILE : (i % 2 + 1) * TILE, :]

    for i in range(4):
        t = tile_of(i)
        base = pl.multiple_of(t * BLK, BLK)
        s = dot_t(q_of(i), kext[pl.ds(base, SPAN), :])
        flag = NEAR_FLAGS + h * 8 + t
        la = jnp.where(sc[flag] > 0, 0.0, NEG).astype(jnp.float32)
        lb = jnp.where(sc[flag + 1] > 0, 0.0, NEG).astype(jnp.float32)
        first = jnp.where(far_side, jnp.where(tile_lane < BLK, la, lb), bias[:, :TILE])
        absent = jnp.where(sc[1] > 0, BLK * (WINB - t), 0)
        edge = jnp.where(span_lane < absent, NEG, 0.0).astype(jnp.float32)
        s = s + jnp.concatenate([first, bias[:, TILE:]], axis=1) + edge
        m = jnp.max(s, axis=1, keepdims=True)
        p = jnp.exp2((s - m) * LOG2).astype(jnp.bfloat16)
        acc_s[i] = jnp.dot(p, vext[pl.ds(base, SPAN), :], preferred_element_type=jnp.float32)
        m_s[i] = jnp.broadcast_to(m, (TILE, HD))

    ex = NEAR_EXTRA + 4 * h
    lowest = jnp.minimum(jnp.minimum(sc[ex], sc[ex + 1]), jnp.minimum(sc[ex + 2], sc[ex + 3]))

    @pl.when(lowest < 6)
    def _():
        for i in range(4):
            t = tile_of(i)
            for g in range(2):
                wa, wb = sc[ex + 2 * g], sc[ex + 2 * g + 1]

                @pl.when((wa < t) | (wb < t))
                def _():
                    ra = pl.multiple_of(jnp.minimum(wa, 11) * BLK, BLK)
                    rb = pl.multiple_of(jnp.minimum(wb, 11) * BLK, BLK)
                    ks = jnp.concatenate([kext[pl.ds(ra, BLK), :], kext[pl.ds(rb, BLK), :]], 0)
                    vs = jnp.concatenate([vext[pl.ds(ra, BLK), :], vext[pl.ds(rb, BLK), :]], 0)
                    s = dot_t(q_of(i), ks)
                    ba = jnp.where(wa < t, 0.0, NEG).astype(jnp.float32)
                    bb = jnp.where(wb < t, 0.0, NEG).astype(jnp.float32)
                    s = s + jnp.where(tile_lane < BLK, ba, bb)
                    m_old = m_s[i]
                    m_new = jnp.maximum(m_old, jnp.max(s, axis=1, keepdims=True))
                    scale = jnp.exp2((m_old - m_new) * LOG2)
                    p = jnp.exp2((s - jnp.concatenate([m_new, m_new], 1)) * LOG2)
                    acc_s[i] = acc_s[i] * jnp.concatenate([scale, scale], 1) + jnp.dot(
                        p.astype(jnp.bfloat16), vs, preferred_element_type=jnp.float32
                    )
                    m_s[i] = m_new

    for i in range(4):
        total = acc_s[i, :, HD:]
        o_ref[0, i * TILE : (i + 1) * TILE, :] = acc_s[i, :, :HD] / total
        for k, line in enumerate(to_rows(m_s[i] * LOG2 + jnp.log2(total))):
            l_ref[0, 2 * i + k : 2 * i + k + 1, :] = line


def near_attention(scalars, queries, q_oth, parts, offsets):
    rows = 2 * TOK
    state = jax.ShapeDtypeStruct((GRP, rows, HD), jnp.float32)
    sums = jax.ShapeDtypeStruct((GRP, 8, HD), jnp.float32)
    q_spec = pl.BlockSpec((TOK, HD), lambda h, sc: (0, sc[0] * GRP + h))
    return pl.pallas_call(
        near_kernel,
        grid_spec=pltpu.PrefetchScalarGridSpec(
            num_scalar_prefetch=1,
            grid=(GRP,),
            in_specs=[
                q_spec,
                q_spec,
                *[pl.BlockSpec((TOK, 2 * HD), lambda h, sc: (0, 0))] * 3,
                pl.BlockSpec(offsets.shape, lambda h, sc: (0, 0)),
            ],
            out_specs=[
                pl.BlockSpec((1, rows, HD), lambda h, sc: (h, 0, 0)),
                pl.BlockSpec((1, 8, HD), lambda h, sc: (h, 0, 0)),
            ],
            scratch_shapes=[
                pltpu.VMEM((3 * TOK, HD), jnp.bfloat16),
                pltpu.VMEM((3 * TOK, 2 * HD), jnp.bfloat16),
                pltpu.VMEM((4, TILE, 2 * HD), jnp.float32),
                pltpu.VMEM((4, TILE, HD), jnp.float32),
            ],
        ),
        out_shape=[state, sums],
        compiler_params=pltpu.CompilerParams(vmem_limit_bytes=40 << 20),
        name="near_attention",
    )(scalars, queries, q_oth, *parts, offsets)


def pack_kernel(sc, lists, keys, values, own_slots, kv_own, sent):
    core, me = sc[0], sc[1]
    group = lax.broadcasted_iota(jnp.int32, lists.shape, 0) // GRP
    table = lists[...]

    def head_of(source, head, rows):
        low, high = source[rows, :HD], source[rows, HD:]
        return jnp.where(head == 0, low, high)

    for head, slots in ((core, own_slots), (1 - core, sent)):
        pick = [jnp.int32(0)] * CAP
        seen = jnp.int32(0)
        for b in range(TOK // BLK):
            hit = jnp.max(jnp.where((group == head) & (table == me * (TOK // BLK) + b), 1, 0))
            for k in range(CAP):
                pick[k] = jnp.where((hit > 0) & (seen == k), b, pick[k])
            seen = seen + hit
        for k in range(CAP):
            rows = pl.ds(pl.multiple_of(pick[k] * BLK, BLK), BLK)
            slots[k * BLK : (k + 1) * BLK, :HD] = head_of(keys, head, rows)
            slots[k * BLK : (k + 1) * BLK, HD:] = head_of(values, head, rows)
    whole = slice(0, TOK)
    for head, target, at in ((core, kv_own, 0), (1 - core, sent, CAP * BLK)):
        target[at : at + TOK, :HD] = head_of(keys, head, whole)
        target[at : at + TOK, HD:] = head_of(values, head, whole)


def pack(scalars, columns, keys, values):
    slots = jax.ShapeDtypeStruct((CAP * BLK, 2 * HD), jnp.bfloat16)
    whole = jax.ShapeDtypeStruct((TOK, 2 * HD), jnp.bfloat16)
    sent = jax.ShapeDtypeStruct((CAP * BLK + TOK, 2 * HD), jnp.bfloat16)

    def full(shape):
        return pl.BlockSpec(shape, lambda i, sc: (0, 0))

    return pl.pallas_call(
        pack_kernel,
        grid_spec=pltpu.PrefetchScalarGridSpec(
            num_scalar_prefetch=1,
            grid=(1,),
            in_specs=[full(columns.shape), full(keys.shape), full(values.shape)],
            out_specs=[full(a.shape) for a in (slots, whole, sent)],
        ),
        out_shape=[slots, whole, sent],
        name="pack_blocks",
    )(scalars, columns, keys, values)


def far_kernel(low, high, sizes, last, sc, q_own, q_oth, o_ref, l_ref, *rest):
    pieces, (out_a, out_b, buf, sem) = rest[: high - low], rest[high - low :]
    h = pl.program_id(0)

    def bound(head, k):
        return sc[FAR_OFF + head * (PIECES + 1) + k]

    def fetch(head, slot):
        base = bound(head, low)
        for k in range(low, high):

            def start(i, _, k=k):
                code = sc[FAR_CODE + head * NV + i]
                pltpu.make_async_copy(
                    pieces[k - low].at[pl.ds(pl.multiple_of(code * BLK, BLK), BLK), :],
                    buf.at[
                        slot, pl.ds(pl.multiple_of((i - base) * BLK, BLK), BLK), pl.ds(0, 2 * HD)
                    ],
                    sem.at[slot],
                ).start()
                return 0

            lax.fori_loop(bound(head, k), bound(head, k + 1), start, 0)

    slot = h % 2

    @pl.when(h == 0)
    def _():
        fetch(0, 0)

    @pl.when(h + 1 < GRP)
    def _():
        fetch(h + 1, 1 - slot)

    n = bound(h, high) - bound(h, low)

    def arrived(i, _):
        pltpu.make_async_copy(
            pieces[0].at[pl.ds(0, BLK), :],
            buf.at[slot, pl.ds(0, BLK), pl.ds(0, 2 * HD)],
            sem.at[slot],
        ).wait()
        return 0

    lax.fori_loop(0, n, arrived, 0)
    buf[slot, :, 2 * HD :] = jnp.ones((NV * BLK, HD), jnp.bfloat16)

    def fill(i, _):
        rows = pl.ds(pl.multiple_of(i * BLK, BLK), BLK)
        buf[slot, rows, :HD] = buf[slot, :BLK, :HD]
        buf[slot, rows, HD:] = jnp.zeros((BLK, 2 * HD), jnp.bfloat16)
        return 0

    wanted = jnp.int32(0)
    for size in sizes[::-1]:
        wanted = jnp.where(n <= size, size, wanted)
    lax.fori_loop(jnp.where(n > 0, n, NV), wanted, fill, 0)

    def put(i, o):
        if last:
            out = (out_a, out_b)[i // 2]
            out[(i % 2) * TILE : (i % 2 + 1) * TILE, :] = o.astype(jnp.bfloat16)
        else:
            out_a[0, i * TILE : (i + 1) * TILE, :] = o

    below = 0
    for size in sizes:

        @pl.when((n > below) & (n <= size))
        def _(size=size):
            keys = size * BLK
            for i in range(4):
                q_ref = (q_own, q_oth)[i // 2]
                s = dot_t(q_ref[(i % 2) * TILE : (i % 2 + 1) * TILE, :], buf[slot, :keys, :HD])
                m = jnp.max(s, axis=1, keepdims=True)
                p = jnp.exp2((s - m) * LOG2).astype(jnp.bfloat16)
                acc = jnp.dot(p, buf[slot, :keys, HD:], preferred_element_type=jnp.float32)
                top = jnp.broadcast_to(m * LOG2, (TILE, HD))
                o, l = o_ref[0, i * TILE : (i + 1) * TILE, :], from_rows(l_ref, i)
                both = jnp.maximum(l, top)
                wn = jnp.exp2(l - both)
                wf = jnp.exp2(top - both)
                weight = wn + acc[:, HD:] * wf
                put(i, (o * wn + acc[:, :HD] * wf) / weight)
                if not last:
                    for k, line in enumerate(to_rows(both + jnp.log2(weight))):
                        out_b[0, 2 * i + k : 2 * i + k + 1, :] = line

        below = size

    @pl.when(n == 0)
    def _():
        for i in range(4):
            put(i, o_ref[0, i * TILE : (i + 1) * TILE, :])
        if not last:
            out_b[...] = l_ref[...]


def far_attention(low, high, sizes, last, scalars, queries, q_oth, o, l, pieces):
    q_spec = pl.BlockSpec((TOK, HD), lambda h, sc: (0, sc[0] * GRP + h))
    state = pl.BlockSpec((1, 2 * TOK, HD), lambda h, sc: (h, 0, 0))
    sums = pl.BlockSpec((1, 8, HD), lambda h, sc: (h, 0, 0))
    flat = pl.BlockSpec((TOK, HD), lambda h, sc: (0, h))
    if last:
        out_shape = [jax.ShapeDtypeStruct((TOK, GW), jnp.bfloat16)] * 2
    else:
        out_shape = [
            jax.ShapeDtypeStruct((GRP, 2 * TOK, HD), jnp.float32),
            jax.ShapeDtypeStruct((GRP, 8, HD), jnp.float32),
        ]
    return pl.pallas_call(
        functools.partial(far_kernel, low, high, sizes, last),
        grid_spec=pltpu.PrefetchScalarGridSpec(
            num_scalar_prefetch=1,
            grid=(GRP,),
            in_specs=[
                q_spec,
                q_spec,
                state,
                sums,
                *[pl.BlockSpec(memory_space=pl.ANY)] * (high - low),
            ],
            out_specs=[flat, flat] if last else [state, sums],
            scratch_shapes=[
                pltpu.VMEM((2, NV * BLK, 3 * HD), jnp.bfloat16),
                pltpu.SemaphoreType.DMA((2,)),
            ],
        ),
        out_shape=out_shape,
        compiler_params=pltpu.CompilerParams(vmem_limit_bytes=48 << 20),
        name="far_last" if last else "far_first",
    )(scalars, queries, q_oth, o, l, *pieces)


def shards(queries, keys, values, columns, offsets, out_weight):
    me = lax.axis_index("ctx")
    core = me % 2
    half = lax.axis_index("kvh")
    i32 = jnp.int32

    def cut(value, which, width, axis=1):
        return lax.dynamic_slice_in_dim(value, which * width, width, axis)

    own_slots, kv_own, sent = pack(jnp.stack([core, me]).astype(i32), columns, keys, values)
    got = permute(sent, send_core)
    q_oth = permute(queries, send_core)
    slots = CAP * BLK
    kv_oth = got[slots:]
    both = jnp.concatenate([own_slots, got[:slots]], axis=0)
    both, columns = lax.optimization_barrier((both, columns))
    far_y = permute(both, send_y)
    near_scalars, far_scalars = tables(me[None].astype(i32), columns)
    held = jnp.where(core == 1, kv_own, kv_oth)
    kv_before = lax.ppermute(held, "ctx", [(i, i + 2) for i in range(62)])
    pool_a = jnp.concatenate([both[:slots], far_y[:slots]], axis=0)
    pool_b = jnp.concatenate([both[slots:], far_y[slots:]], axis=0)
    pool_a, pool_b, kv_before, q_oth, near_scalars = lax.optimization_barrier(
        (pool_a, pool_b, kv_before, q_oth, near_scalars)
    )
    pool_a = jnp.concatenate(ring(pool_a, send_z), axis=0)
    pool_b = jnp.concatenate(ring(pool_b, send_x), axis=0)
    low_a, high_a = permute(pool_a, send_x(1)), permute(pool_a, send_x(-1))
    low_b, high_b = permute(pool_b, send_z(1)), permute(pool_b, send_z(-1))
    o, l = near_attention(near_scalars, queries, q_oth, (kv_own, kv_oth, kv_before), offsets)
    low_a, high_a, low_b, high_b, o = lax.optimization_barrier((low_a, high_a, low_b, high_b, o))
    middle = pool_a.shape[0] // 2
    second = [
        permute(low_a[:middle], send_x(1)),
        permute(high_a[middle:], send_x(-1)),
        permute(low_b[:middle], send_z(1)),
        permute(high_b[middle:], send_z(-1)),
    ]
    first = [pool_a, low_a, high_a, pool_b, low_b, high_b]
    o, l = far_attention(0, 6, (12, 16), False, far_scalars, queries, q_oth, o, l, first)
    own, oth = far_attention(6, 10, (4, 6, 8, 16), True, far_scalars, queries, q_oth, o, l, second)

    columns_out = out_weight.shape[1] // 2
    weight_kept = cut(out_weight, half, columns_out)
    weight_sent = cut(out_weight, 1 - half, columns_out)
    results = []
    parts = [slice(0, BLK), slice(BLK, TOK)]
    first, others = [permute(oth[rows], send_core) for rows in parts]
    for at in range(0, TOK, BLK):
        rows = slice(at, at + BLK)
        got = first if at == 0 else others[at - BLK : at]
        attended = jnp.where(
            core == 0,
            jnp.concatenate([own[rows], got], 1),
            jnp.concatenate([got, own[rows]], 1),
        )
        sent = jnp.dot(attended, weight_sent, preferred_element_type=jnp.float32)
        taken = permute(sent.astype(jnp.bfloat16), lambda i: 1 - i, "kvh")
        kept = jnp.dot(attended, weight_kept, preferred_element_type=jnp.float32)
        results.append((kept + taken.astype(jnp.float32)).astype(jnp.bfloat16))
    return jnp.concatenate(results, axis=0)


def solution(mesh):
    placed = (
        P("ctx", "kvh"),
        P("ctx", "kvh"),
        P("ctx", "kvh"),
        P("kvh", None),
        P("kvh", None),
        P("kvh", None),
    )
    return jax.shard_map(
        shards, mesh=mesh, in_specs=placed, out_specs=P("ctx", "kvh"), check_vma=False
    )
```
